32 devices in a mesh: seq: 16 (over z, y, core), tp: 2 (over x).
Axes of the slice: x: 2, y: 2, z: 4, core: 2. Of those that a mesh axis runs over, the one named last changes fastest.
Arguments:
- layer_in: bfloat16 [32768, 768], P(('seq', 'tp')), may hold values from -6 to 6
- skip_values: bfloat16 [32768, 384], P('seq', 'tp'), may hold values from -6 to 6
- block_slot: int32 [16, 8], replicated, may hold values from 0 to 3, as said below
- doc_lengths: int32 [32, 4], replicated, may hold values from 1 to 512, 1024 in all within a row
- gain_attention: float32 [768], replicated, may hold values from 0.5 to 1.5
- shift_attention: float32 [768], replicated, may hold values from -1.5 to 1.5
- query_weight: bfloat16 [768, 768], P(None, 'tp'), may hold values from -0.21875 to 0.21875
- query_bias: float32 [768], P('tp'), may hold values from -1.5 to 1.5
- key_weight: bfloat16 [768, 768], P(None, 'tp'), may hold values from -0.21875 to 0.21875
- value_weight: bfloat16 [768, 384], P(None, 'tp'), may hold values from -0.21875 to 0.21875
- value_bias: float32 [384], P('tp'), may hold values from -1.5 to 1.5
- out_weight: bfloat16 [768, 768], P('tp'), may hold values from -1.75 to 1.75
- out_bias: float32 [768], replicated, may hold values from -1.5 to 1.5
- gain_feed: float32 [768], replicated, may hold values from 0.5 to 1.5
- shift_feed: float32 [768], replicated, may hold values from -1.5 to 1.5
- up_weight: bfloat16 [768, 3072], P(None, 'tp'), may hold values from -0.21875 to 0.21875
- up_bias: float32 [3072], P('tp'), may hold values from -1.5 to 1.5
- down_weight: bfloat16 [3072, 768], P('tp'), may hold values from -0.109375 to 0.109375
- down_bias: float32 [768], replicated, may hold values from -1.5 to 1.5
- out_grad: bfloat16 [32768, 768], P(('seq', 'tp')), may hold values from -6 to 6
Outputs:
- layer_out: bfloat16 [32768, 768], P(('seq', 'tp'))
- input_grad: float32 [32768, 768], P(('seq', 'tp'))
- skip_grad: float32 [32768, 384], P('seq', 'tp')
- grad_gain_attention: float32 [768], replicated
- grad_shift_attention: float32 [768], replicated
- grad_query_weight: float32 [768, 768], P(None, 'tp')
- grad_query_bias: float32 [768], P('tp')
- grad_key_weight: float32 [768, 768], P(None, 'tp')
- grad_value_weight: float32 [768, 384], P(None, 'tp')
- grad_value_bias: float32 [384], P('tp')
- grad_out_weight: float32 [768, 768], P('tp')
- grad_out_bias: float32 [768], replicated
- grad_gain_feed: float32 [768], replicated
- grad_shift_feed: float32 [768], replicated
- grad_up_weight: float32 [768, 3072], P(None, 'tp')
- grad_up_bias: float32 [3072], P('tp')
- grad_down_weight: float32 [3072, 768], P('tp')
- grad_down_bias: float32 [768], replicated
The draws below stay inside these ranges and needn't reach their ends.
Inputs may be any that keep to these rules, and one draw needn't show every extreme that they name: `block_slot`: for each group of 4 consecutive rows (the seq indices that hold one set of sequences) and each column, the entries are a permutation of 0 to 3. `doc_lengths`: each row gives the lengths of the documents of one sequence in order; a row sums to 1024.
All inputs are finite; a program needn't handle non-finite values.
Results may differ from the reference program's by a relative error of at most 0.015.
Values may be sent and summed in bfloat16 or wider, within the bound.
No kernel may reach another device: no remote copies, remote signals or barrier semaphores. Data moves between devices by JAX's collectives and lax.ppermute only.
A program may use at most 320 MiB of HBM per device.

```python
import math
from functools import partial
import jax
import jax.numpy as jnp
import numpy as np
from jax import lax

D = 768
HEADS = 12
HEAD = 64
FF = 3072
FRESH = 6
SEQ_LEN = 1024
BLOCK = 256
DOCS = 4
BATCH = 8
SPAN = 4
GROUPS = 4
NSEQS = 32
TOKENS = 32768
N_TP = 2


def draw_block_slot(key, part):
    keys_all = jax.random.split(key, GROUPS * BATCH)
    orders = jax.vmap(lambda single: jax.random.permutation(single, SPAN))(keys_all)
    orders = orders.reshape(GROUPS, BATCH, SPAN).transpose(0, 2, 1).reshape(GROUPS * SPAN, BATCH)
    return orders.astype(jnp.int32)


def levels(rng, extent, shards, smallest, largest):
    def one(position, blocks):
        steps = jax.random.uniform(jax.random.fold_in(jax.random.fold_in(rng, 6), position), (blocks,), jnp.float32, smallest / len(shards), largest / len(shards))
        return jnp.repeat(jnp.exp(steps), extent[position] // blocks).reshape((-1,) + (1,) * (len(extent) - position - 1))

    level = one(*shards[0])
    for cut in shards[1:]:
        level = level * one(*cut)
    return level


def length_profile(amount, total, reach, slope):
    weights = [(1 << 20) // math.isqrt(standing ** slope) + 1 for standing in range(2, amount + 1)]
    surplus, counts = total - reach - (amount - 1), [1] * (amount - 1)
    while surplus > 0:
        free = [i for i in range(amount - 1) if counts[i] < reach]
        pool, remaining = sum([weights[i] for i in free]), surplus
        for i in free:
            more = min(reach - counts[i], max(1, remaining * weights[i] // pool), surplus)
            counts[i] = counts[i] + more
            surplus = surplus - more
    return np.array([reach] + counts)


def uneven(rng, number_of, total, bound, slope):
    if number_of == 2:
        one = jax.random.randint(rng, (), max(1, total - bound), min(bound, total - 1) + 1)
        return jnp.stack([one, total - one])
    tallies = jnp.asarray(length_profile(number_of, total, bound, slope), jnp.int32)
    couples = (number_of - 1) // 2
    source_of, receiver = tallies[1:1 + 2 * couples:2], tallies[2:2 + 2 * couples:2]
    margin = jnp.minimum(source_of - 1, bound - receiver)
    passed = jax.random.randint(jax.random.fold_in(rng, 1), (couples,), 0, 1 << 20) % (margin + 1)
    tallies = tallies.at[1:1 + 2 * couples:2].set(source_of - passed).at[2:2 + 2 * couples:2].set(receiver + passed)
    return tallies[jax.random.permutation(jax.random.fold_in(rng, 2), number_of)]


def normal_values(stream_key, shape, deviation, bound, shards=(), kind=jnp.bfloat16):
    values = jax.random.normal(stream_key, shape, jnp.float32) * deviation
    if len(shards) > 0:
        values = levels(stream_key, shape, shards, -0.22, 0.18) * values
    return jnp.clip(values, min=-bound, max=bound).astype(kind)


def setup_inputs(seed: int = 0) -> dict:
    key_list = jax.random.split(jax.random.key(seed), 21)
    layer_in = normal_values(key_list[0], (TOKENS, D), 1.0, 6.0, ((0, 32),))
    skip_values = normal_values(key_list[1], (TOKENS, FRESH * HEAD), 1.0, 6.0, ((0, 16), (1, 2)))
    block_slot = draw_block_slot(jax.random.fold_in(key_list[20], 71), 0)
    doc_lengths = jax.vmap(lambda own: uneven(own, DOCS, SEQ_LEN, SEQ_LEN // 2, 2))(jax.random.split(key_list[3], NSEQS)).reshape((NSEQS, DOCS)).astype(jnp.int32)
    gain_attention = jnp.clip(1.0 + 0.1 * jax.random.normal(key_list[4], (D,), jnp.float32), 0.5, 1.5)
    shift_attention = normal_values(key_list[5], (D,), 0.3, 1.5, (), jnp.float32)
    query_weight = normal_values(key_list[6], (D, D), D ** -0.5, 0.21875, ((1, 2),))
    query_bias = normal_values(key_list[7], (D,), 0.3, 1.5, ((0, 2),), jnp.float32)
    key_weight = normal_values(key_list[8], (D, D), D ** -0.5, 0.21875, ((1, 2),))
    value_weight = normal_values(key_list[9], (D, FRESH * HEAD), D ** -0.5, 0.21875, ((1, 2),))
    value_bias = normal_values(key_list[10], (FRESH * HEAD,), 0.3, 1.5, ((0, 2),), jnp.float32)
    out_weight = normal_values(key_list[11], (D, D), HEADS ** -0.5, 1.75, ((0, 2),))
    out_bias = normal_values(key_list[12], (D,), 0.3, 1.5, (), jnp.float32)
    gain_feed = jnp.clip(1.0 + 0.1 * jax.random.normal(key_list[13], (D,), jnp.float32), 0.5, 1.5)
    shift_feed = normal_values(key_list[14], (D,), 0.3, 1.5, (), jnp.float32)
    up_weight = normal_values(key_list[15], (D, FF), D ** -0.5, 0.21875, ((1, 2),))
    up_bias = normal_values(key_list[16], (FF,), 0.3, 1.5, ((0, 2),), jnp.float32)
    down_weight = normal_values(key_list[17], (FF, D), FF ** -0.5, 0.109375, ((0, 2),))
    down_bias = normal_values(key_list[18], (D,), 0.3, 1.5, (), jnp.float32)
    out_grad = normal_values(key_list[19], (TOKENS, D), 1.0, 6.0, ((0, 32),))
    return {"layer_in": layer_in, "skip_values": skip_values, "block_slot": block_slot, "doc_lengths": doc_lengths, "gain_attention": gain_attention, "shift_attention": shift_attention, "query_weight": query_weight, "query_bias": query_bias, "key_weight": key_weight, "value_weight": value_weight, "value_bias": value_bias, "out_weight": out_weight, "out_bias": out_bias, "gain_feed": gain_feed, "shift_feed": shift_feed, "up_weight": up_weight, "up_bias": up_bias, "down_weight": down_weight, "down_bias": down_bias, "out_grad": out_grad}


HIGHEST = lax.Precision.HIGHEST
EPSILON = 1e-05

@jax.custom_vjp
def low(v):
    return lax.optimization_barrier(v.astype(jnp.bfloat16)).astype(jnp.float32)

@jax.custom_vjp
def low_back(v):
    return v

def low_keep(v):
    return (low(v), None)

def low_pass(kept, grad):
    return (grad,)

def back_keep(v):
    return (v, None)

def back_low(kept, grad):
    return (low(grad),)
low.defvjp(low_keep, low_pass)
low_back.defvjp(back_keep, back_low)

def matmul(left, right):
    return jnp.dot(left, right, precision=HIGHEST, preferred_element_type=jnp.float32)

def layer_norm(rows, gain, shift):
    centred = rows - lax.optimization_barrier(jnp.mean(rows, axis=-1, keepdims=True))
    variance = lax.optimization_barrier(jnp.mean(centred * centred, axis=-1, keepdims=True))
    return centred * lax.rsqrt(variance + EPSILON) * gain + shift

def places_and_docs(block_slot, doc_lengths):
    within = jnp.arange(BLOCK, dtype=jnp.int32)
    places = block_slot.astype(jnp.int32)[:, :, None] * BLOCK + within[None, None, :]
    places = places.reshape(GROUPS, SPAN, BATCH, BLOCK).transpose(0, 2, 1, 3).reshape(NSEQS, SEQ_LEN)
    bounds = jnp.cumsum(doc_lengths.astype(jnp.int32), axis=1).astype(jnp.int32)[:, :-1]
    doc_ids = lax.optimization_barrier(jnp.sum((places[:, :, None] >= bounds[:, None, :]).astype(jnp.int32), axis=2)).astype(jnp.int32)
    return (places, doc_ids)

def attend_one(item):
    queries, keys, values, places, doc_ids = item
    scores = low_back(jnp.einsum('qhe,khe->hqk', queries, keys, precision=HIGHEST) * HEAD ** (-0.5))
    visible = (places[None, :] <= places[:, None]) & (doc_ids[None, :] == doc_ids[:, None])
    scores = jnp.where(visible[None], scores, -jnp.inf)
    row_max = lax.optimization_barrier(jnp.max(scores, axis=-1, keepdims=True))
    log_total = row_max + jnp.log(lax.optimization_barrier(jnp.sum(jnp.exp(scores - row_max), axis=-1, keepdims=True)))
    probs = low(jnp.exp(scores - log_total))
    return jnp.einsum('hqk,khe->qhe', probs, values, precision=HIGHEST)

def to_seqs(rows):
    shaped = rows.reshape(GROUPS, SPAN, BATCH, BLOCK, HEADS, HEAD).transpose(0, 2, 1, 3, 4, 5)
    return shaped.reshape(NSEQS, SEQ_LEN, HEADS, HEAD)

def forward(places, doc_ids, layer_in, skip_values, gain_attention, shift_attention, query_weight, query_bias, key_weight, value_weight, value_bias, out_weight, out_bias, gain_feed, shift_feed, up_weight, up_bias, down_weight, down_bias):
    norm_one = low(layer_norm(layer_in, gain_attention, shift_attention))
    queries = low(low_back(matmul(norm_one, query_weight)) + query_bias)
    keys = low(low_back(matmul(norm_one, key_weight)))
    fresh = low(low_back(matmul(norm_one, value_weight)) + value_bias)
    per_group = FRESH // N_TP
    values = jnp.concatenate([fresh.reshape(TOKENS, N_TP, per_group, HEAD), skip_values.reshape(TOKENS, N_TP, per_group, HEAD)], axis=2)
    attended = lax.map(jax.checkpoint(attend_one), (to_seqs(queries), to_seqs(keys), to_seqs(values), places, doc_ids))
    attended = attended.reshape(GROUPS, BATCH, SPAN, BLOCK, HEADS, HEAD).transpose(0, 2, 1, 3, 4, 5).reshape(TOKENS, D)
    attended = low(low_back(attended))
    middle = layer_in + low_back(matmul(attended, out_weight)) + out_bias
    norm_two = low(layer_norm(middle, gain_feed, shift_feed))
    hidden = low_back(matmul(norm_two, up_weight)) + up_bias
    activated = low(jax.nn.gelu(hidden, approximate=True))
    return middle + low_back(matmul(activated, down_weight)) + down_bias

def reference(layer_in, skip_values, block_slot, doc_lengths, gain_attention, shift_attention, query_weight, query_bias, key_weight, value_weight, value_bias, out_weight, out_bias, gain_feed, shift_feed, up_weight, up_bias, down_weight, down_bias, out_grad):
    places, doc_ids = places_and_docs(block_slot, doc_lengths)
    floats = [array.astype(jnp.float32) for array in (layer_in, skip_values, gain_attention, shift_attention, query_weight, query_bias, key_weight, value_weight, value_bias, out_weight, out_bias, gain_feed, shift_feed, up_weight, up_bias, down_weight, down_bias)]
    result, pull = jax.vjp(partial(forward, places, doc_ids), *floats)
    input_grad, skip_grad, grad_gain_attention, grad_shift_attention, grad_query_weight, grad_query_bias, grad_key_weight, grad_value_weight, grad_value_bias, grad_out_weight, grad_out_bias, grad_gain_feed, grad_shift_feed, grad_up_weight, grad_up_bias, grad_down_weight, grad_down_bias = pull(out_grad.astype(jnp.float32))
    layer_out = result.astype(jnp.bfloat16)
    return (layer_out, input_grad, skip_grad, grad_gain_attention, grad_shift_attention, grad_query_weight, grad_query_bias, grad_key_weight, grad_value_weight, grad_value_bias, grad_out_weight, grad_out_bias, grad_gain_feed, grad_shift_feed, grad_up_weight, grad_up_bias, grad_down_weight, grad_down_bias)
```

```python
from functools import partial

import jax
import jax.numpy as jnp
from jax import lax
from jax.experimental import pallas as pl
from jax.experimental.pallas import tpu as pltpu
from jax.sharding import PartitionSpec as P

HEAD = 64
SEQ_LEN = 1024
BLOCK = 256
LONGEST = 512
SPAN = SEQ_LEN // BLOCK
REACH = -(-LONGEST // BLOCK) + 1
PAIR = 2 * HEAD
EPSILON = 1e-05
MASKED = -1e30
GELU_A = 0.7978845608028654
GELU_B = 0.044715
SCALE = HEAD ** (-0.5)
VMEM = 56 * 1024 * 1024

F32 = jnp.float32
BF16 = jnp.bfloat16


def nn(left, right):
    return lax.dot_general(left, right, (((1,), (0,)), ((), ())), preferred_element_type=F32)


def nt(left, right):
    return lax.dot_general(left, right, (((1,), (1,)), ((), ())), preferred_element_type=F32)


def tn(left, right):
    return lax.dot_general(left, right, (((0,), (0,)), ((), ())), preferred_element_type=F32)


def normed(rows):
    centred = rows - jnp.mean(rows, axis=-1, keepdims=True)
    inverse = lax.rsqrt(jnp.mean(centred * centred, axis=-1, keepdims=True) + EPSILON)
    return centred * inverse, inverse


def norm_back(grad_out, scaled, inverse, gain):
    grad_scaled = grad_out * gain
    first_mean = jnp.mean(grad_scaled, axis=-1, keepdims=True)
    second_mean = jnp.mean(grad_scaled * scaled, axis=-1, keepdims=True)
    return inverse * (grad_scaled - first_mean - scaled * second_mean)


def full(shape):
    return pl.BlockSpec(shape, lambda *_: (0,) * len(shape), pipeline_mode=pl.Buffered(1))


def placed(columns):
    return pl.BlockSpec((None, BLOCK, columns), lambda p, src, *_: (src[p], 0, 0))


def in_order(columns):
    return pl.BlockSpec((BLOCK, columns), lambda p, *_: (p, 0))


def by_block(columns):
    return pl.BlockSpec((None, BLOCK, columns), lambda p, *_: (p, 0, 0))


def shape_of(shape, dtype):
    return jax.ShapeDtypeStruct(shape, dtype)


def call(kernel, scalars, grid, ins, outs, out_shapes, scratch=(), flops=0, name=None):
    return pl.pallas_call(
        kernel,
        grid_spec=pltpu.PrefetchScalarGridSpec(
            num_scalar_prefetch=scalars,
            grid=grid,
            in_specs=ins,
            out_specs=outs,
            scratch_shapes=scratch,
        ),
        out_shape=out_shapes,
        compiler_params=pltpu.CompilerParams(
            dimension_semantics=("arbitrary",) * len(grid), vmem_limit_bytes=VMEM
        ),
        cost_estimate=pl.CostEstimate(flops=flops, bytes_accessed=flops // 400, transcendentals=0),
        name=name,
    )


def project_kernel(
    src, x_ref, skip_ref, own_ref, other_ref, bias_ref, gain_ref, shift_ref,
    norm_ref, q_ref, k_ref, v_ref,
):
    half = own_ref.shape[1] * 2 // 5
    fresh = half // 2
    scaled, _ = normed(x_ref[...].astype(F32))
    rows = (scaled * gain_ref[...] + shift_ref[...]).astype(BF16)
    norm_ref[...] = rows
    parts = []
    for side, weight in enumerate((own_ref, other_ref)):
        made = (nn(rows, weight[...]) + bias_ref[side:side + 1, :]).astype(BF16)
        columns = slice(side * half, (side + 1) * half)
        q_ref[:, columns] = made[:, :half]
        k_ref[:, columns] = made[:, half:2 * half]
        parts.append(made[:, 2 * half:])
        parts.append(skip_ref[:, side * fresh:(side + 1) * fresh])
    v_ref[...] = jnp.concatenate(parts, axis=1)


def doc_start(position, bounds, bound_count):
    start = jnp.zeros_like(position)
    for index in range(bound_count):
        start = jnp.where(position >= bounds[index], bounds[index], start)
    return start


def attend_kernel(
    bound_count, src, bounds, x_ref, q_ref, k_ref, v_ref, own_ref, other_ref, bias_ref,
    gain_ref, shift_ref, att_ref, lse_ref, middle_ref, norm_ref, att_s, lse_s,
):
    p = pl.program_id(0)
    width = q_ref.shape[1]
    half = width // 2
    first = doc_start(p * BLOCK, bounds, bound_count)
    needed = p - first // BLOCK + 1
    lane = lax.broadcasted_iota(jnp.int32, (1, PAIR), 1)
    low = lane < HEAD
    picks = [jnp.where(low, SCALE, 0.0).astype(BF16), jnp.where(low, 0.0, SCALE).astype(BF16)]

    def run(count):
        span = count * BLOCK
        base = pl.multiple_of((p - count + 1) * BLOCK, BLOCK)
        row = p * BLOCK + lax.broadcasted_iota(jnp.int32, (BLOCK, 1), 0)
        start = doc_start(row, bounds, bound_count)
        column = base + lax.broadcasted_iota(jnp.int32, (1, span), 1)
        seen = (column <= row) & (column >= start)
        bias = jnp.where(seen, 0.0, MASKED)
        head_lane = lax.broadcasted_iota(jnp.int32, (1, 128), 1)

        @pl.loop(0, width // PAIR)
        def _(pair):
            lanes = pl.ds(pl.multiple_of(pair * PAIR, PAIR), PAIR)
            queries = q_ref[:, lanes]
            keys = k_ref[pl.ds(base, span), lanes]
            values = v_ref[pl.ds(base, span), lanes]
            outs = []
            for side in range(2):
                scores = nt(queries * picks[side], keys) + bias
                top = jnp.max(scores, axis=1, keepdims=True)
                probs = jnp.exp(scores - top)
                total = jnp.sum(probs, axis=1, keepdims=True)
                outs.append(nn(probs.astype(BF16), values) / total)
                lse_s[...] = jnp.where(
                    head_lane == 2 * pair + side, top + jnp.log(total), lse_s[...]
                )
            att_s[:, lanes] = jnp.where(low, outs[0], outs[1]).astype(BF16)

    for count in range(1, REACH + 1):
        pl.when(needed == count)(partial(run, count))

    lse_ref[...] = lse_s[...].T[:lse_ref.shape[0], :]
    attended = att_s[...]
    att_ref[...] = attended
    middle = (
        x_ref[...].astype(F32)
        + (nn(attended[:, :half], own_ref[...]) + nn(attended[:, half:], other_ref[...]))
        + bias_ref[...]
    )
    middle_ref[...] = middle
    scaled, _ = normed(middle)
    norm_ref[...] = (scaled * gain_ref[...] + shift_ref[...]).astype(BF16)


def feed_kernel(
    first_call, core, *refs
):
    if first_call:
        (norm_ref, grad_ref, up_ref, down_ref, bias_ref,
         out_ref, back_ref, ku_ref, su_ref, kd_ref, sd_ref, gb_ref) = refs
    else:
        (norm_ref, grad_ref, ua_ref, ub_ref, da_ref, db_ref, bias_ref, out_in, back_in,
         out_ref, back_ref, ku_ref, su_ref, kd_ref, sd_ref, gb_ref) = refs
    j = pl.program_id(0)
    near = j < pl.num_programs(0) // 2

    @pl.when(j == 0)
    def _():
        if first_call:
            out_ref[...] = jnp.zeros_like(out_ref)
            back_ref[...] = jnp.zeros_like(back_ref)
        else:
            out_ref[...] = out_in[...]
            back_ref[...] = back_in[...]

    if first_call:
        up = up_ref[...]
        down = down_ref[...]
    else:
        up = jnp.where(near, ua_ref[...], ub_ref[...])
        down = jnp.where(near, da_ref[...], db_ref[...])
    rows = norm_ref[...]
    grads = grad_ref[...]
    hidden = nn(rows, up) + bias_ref[...]
    square = hidden * hidden
    curve = jnp.tanh(GELU_A * hidden * (1.0 + GELU_B * square))
    plus = 0.5 * (1.0 + curve)
    active = (hidden * plus).astype(BF16)
    slope = plus + (hidden * plus) * (1.0 - curve) * (GELU_A + 3.0 * GELU_A * GELU_B * square)
    hidden_grad = nt(grads, down) * slope
    gb_ref[...] = jnp.sum(hidden_grad, axis=0, keepdims=True)
    hidden_low = hidden_grad.astype(BF16)
    out_ref[...] += nn(active, down)
    back_ref[...] += nt(hidden_low, up)
    down_grad = tn(active, grads).astype(BF16)
    up_grad = tn(rows, hidden_low).astype(BF16)

    @pl.when(near)
    def _():
        ku_ref[...] = up_grad
        kd_ref[...] = down_grad

    @pl.when(jnp.logical_not(near))
    def _():
        su_ref[...] = up_grad
        sd_ref[...] = down_grad


def feed(first_call, core, rows, grads, weights, bias, carried, chunk):
    tokens, width = rows.shape
    units = bias.shape[1]
    steps = units // chunk
    part = steps // 2
    turn = lambda j, core: lax.rem(j + core[0] * part, steps)
    near = lambda j: jnp.minimum(j, part - 1)
    far = lambda j: jnp.maximum(j - part, 0)
    up_near = pl.BlockSpec((width, chunk), lambda j, core: (0, near(j)))
    up_far = pl.BlockSpec((width, chunk), lambda j, core: (0, far(j)))
    down_near = pl.BlockSpec((chunk, width), lambda j, core: (near(j), 0))
    down_far = pl.BlockSpec((chunk, width), lambda j, core: (far(j), 0))
    if first_call:
        weight_specs = [
            pl.BlockSpec((width, chunk), lambda j, core: (0, turn(j, core))),
            pl.BlockSpec((chunk, width), lambda j, core: (turn(j, core), 0)),
        ]
    else:
        weight_specs = [up_near, up_far, down_near, down_far]
    bias_spec = pl.BlockSpec((1, chunk), lambda j, core: (0, turn(j, core)))
    total = full((tokens, width))
    return call(
        partial(feed_kernel, first_call),
        1,
        (steps,),
        [total, total] + weight_specs + [bias_spec] + [total] * len(carried),
        [total, total, up_near, up_far, down_near, down_far, bias_spec],
        [
            shape_of((tokens, width), F32),
            shape_of((tokens, width), F32),
            shape_of((width, units // 2), BF16),
            shape_of((width, units // 2), BF16),
            shape_of((units // 2, width), BF16),
            shape_of((units // 2, width), BF16),
            shape_of((1, units), F32),
        ],
        flops=12 * tokens * width * units,
        name="feed_own" if first_call else "feed_other",
    )(core, rows, grads, *weights, bias, *carried)


def residual_kernel(
    core, out_ref, back_ref, grad_ref, middle_ref, att_ref, own_ref, other_ref, gain_ref,
    down_bias_ref, layer_ref, mg_ref, ga_ref, keep_ref, send_ref, small_ref, acc_s,
):
    p = pl.program_id(0)
    half = own_ref.shape[0]
    middle = middle_ref[...]
    layer_ref[...] = (middle + out_ref[...] + down_bias_ref[...]).astype(BF16)
    scaled, inverse = normed(middle)
    second = back_ref[...]
    out_grad = grad_ref[...].astype(F32)
    middle_grad = out_grad + norm_back(second, scaled, inverse, gain_ref[...])
    mg_ref[...] = middle_grad
    low = middle_grad.astype(BF16)
    ga_ref[:, :half] = nt(low, own_ref[...]).astype(BF16)
    ga_ref[:, half:] = nt(low, other_ref[...]).astype(BF16)
    weight_grad = tn(att_ref[...], low)
    sums = jnp.concatenate(
        [
            jnp.sum(value, axis=0, keepdims=True)
            for value in (second * scaled, second, middle_grad, out_grad)
        ],
        axis=0,
    )

    @pl.when(p == 0)
    def _():
        acc_s[...] = weight_grad
        small_ref[...] = sums

    @pl.when(p > 0)
    def _():
        acc_s[...] += weight_grad
        small_ref[...] += sums

    @pl.when(p == pl.num_programs(0) - 1)
    def _():
        rows = half // 2
        near = pl.multiple_of(core[0] * rows, 32)
        far = pl.multiple_of(rows - core[0] * rows, 32)
        for side in range(2):
            keep_ref[side] = acc_s[pl.ds(side * half + near, rows), :].astype(BF16)
            send_ref[side] = acc_s[pl.ds(side * half + far, rows), :].astype(BF16)


def attend_back_kernel(
    bound_count, src, bounds, q_ref, k_ref, v_ref, att_ref, ga_ref, lse_ref,
    own_ref, other_ref, skip_ref, dq_s, dk_s, dv_s, delta_s,
):
    p = pl.program_id(0)
    width = q_ref.shape[1]
    half = width // 2
    fresh = half // 2
    place = src[p]
    first = doc_start(p * BLOCK, bounds, bound_count)
    needed = p - first // BLOCK + 1
    low = lax.broadcasted_iota(jnp.int32, (1, PAIR), 1) < HEAD
    picks = [jnp.where(low, SCALE, 0.0).astype(BF16), jnp.where(low, 0.0, SCALE).astype(BF16)]
    ones = [jnp.where(low, 1.0, 0.0).astype(BF16), jnp.where(low, 0.0, 1.0).astype(BF16)]

    @pl.when(p == 0)
    def _():
        dk_s[...] = jnp.zeros_like(dk_s)
        dv_s[...] = jnp.zeros_like(dv_s)

    product = ga_ref[...].astype(F32) * att_ref[...].astype(F32)
    high = product.astype(BF16)
    rest = (product - high.astype(F32)).astype(BF16)
    owner = lax.broadcasted_iota(jnp.int32, (delta_s.shape[0], width), 1) // HEAD
    which = lax.broadcasted_iota(jnp.int32, (delta_s.shape[0], width), 0)
    gather = (owner == which).astype(F32).astype(BF16)
    delta_s[...] = nt(gather, high) + nt(gather, rest)

    def run(count):
        span = count * BLOCK
        base = pl.multiple_of((p - count + 1) * BLOCK, BLOCK)
        row = p * BLOCK + lax.broadcasted_iota(jnp.int32, (1, BLOCK), 1)
        start = doc_start(row, bounds, bound_count)
        column = base + lax.broadcasted_iota(jnp.int32, (span, 1), 0)
        seen = (column <= row) & (column >= start)
        bias = jnp.where(seen, 0.0, MASKED)

        @pl.loop(0, width // PAIR)
        def _(pair):
            lanes = pl.ds(pl.multiple_of(pair * PAIR, PAIR), PAIR)
            queries = q_ref[:, lanes]
            grads = ga_ref[:, lanes]
            keys = k_ref[pl.ds(base, span), lanes]
            values = v_ref[pl.ds(base, span), lanes]
            query_parts = []
            for side in range(2):
                head = 2 * pair + side
                picked = queries * picks[side]
                chosen = grads * ones[side]
                scores = nt(keys, picked) + bias
                probs = jnp.exp(scores - lse_ref[pl.ds(head, 1), :])
                dprobs = nt(values, chosen)
                dscores = (probs * (dprobs - delta_s[pl.ds(head, 1), :])).astype(BF16)
                value_part = nn(probs.astype(BF16), chosen)
                key_part = nn(dscores, picked)
                query_parts.append(tn(dscores, keys))
                if side == 0:
                    value_sum, key_sum = value_part, key_part
                else:
                    value_sum, key_sum = value_sum + value_part, key_sum + key_part
            dv_s[pl.ds(base, span), lanes] += value_sum
            dk_s[pl.ds(base, span), lanes] += key_sum
            dq_s[:, lanes] = (
                jnp.where(low, query_parts[0], query_parts[1]) * SCALE
            ).astype(BF16)

    for count in range(1, REACH + 1):
        pl.when(needed == count)(partial(run, count))

    own_ref[place, :, :half] = dq_s[:, :half]
    other_ref[place, :, :half] = dq_s[:, half:]

    @pl.when(p == pl.num_programs(0) - 1)
    def _():
        for block in range(SPAN):
            rows = slice(block * BLOCK, (block + 1) * BLOCK)
            to = src[block]
            value_grad = dv_s[rows, :]
            own_ref[to, :, half:2 * half] = dk_s[rows, :half].astype(BF16)
            other_ref[to, :, half:2 * half] = dk_s[rows, half:].astype(BF16)
            own_ref[to, :, 2 * half:] = value_grad[:, :fresh].astype(BF16)
            other_ref[to, :, 2 * half:] = value_grad[:, half:half + fresh].astype(BF16)
            skip_ref[to] = jnp.concatenate(
                [value_grad[:, fresh:half], value_grad[:, half + fresh:]], axis=1
            ).astype(BF16)


def weight_kernel(core, norm_ref, own_ref, other_ref, keep_ref, send_ref, sums_ref, made_s):
    rows = norm_ref[...]
    half = made_s.shape[0] // 2
    near = pl.multiple_of(core[0] * half, 128)
    far = pl.multiple_of(half - core[0] * half, 128)
    for side, grads_ref in enumerate((own_ref, other_ref)):
        grads = grads_ref[...]
        made_s[...] = tn(rows, grads)
        keep_ref[side] = made_s[pl.ds(near, half), :].astype(BF16)
        send_ref[side] = made_s[pl.ds(far, half), :].astype(BF16)
        sums_ref[side:side + 1, :] = jnp.sum(grads.astype(F32), axis=0, keepdims=True)


def input_kernel(
    own_ref, other_ref, w_own_ref, w_other_ref, x_ref, mg_ref, gain_ref, grad_ref, small_ref
):
    p = pl.program_id(0)
    first = nt(own_ref[...], w_own_ref[...]) + nt(other_ref[...], w_other_ref[...])
    scaled, inverse = normed(x_ref[...].astype(F32))
    grad_ref[...] = (mg_ref[...] + norm_back(first, scaled, inverse, gain_ref[...])).astype(BF16)
    sums = jnp.concatenate(
        [jnp.sum(value, axis=0, keepdims=True) for value in (first * scaled, first)], axis=0
    )

    @pl.when(p == 0)
    def _():
        small_ref[...] = sums

    @pl.when(p > 0)
    def _():
        small_ref[...] += sums


def per_device(
    sizes,
    layer_in,
    skip_values,
    block_slot,
    doc_lengths,
    gain_attention,
    shift_attention,
    query_weight,
    query_bias,
    key_weight,
    value_weight,
    value_bias,
    out_weight,
    out_bias,
    gain_feed,
    shift_feed,
    up_weight,
    up_bias,
    down_weight,
    down_bias,
    out_grad,
):
    seq_count, tp_count = sizes
    width = layer_in.shape[1]
    half = query_weight.shape[1]
    fresh = value_weight.shape[1]
    units = up_weight.shape[1]
    tokens = layer_in.shape[0]
    batch = skip_values.shape[0] // BLOCK
    seq_index = lax.axis_index("seq")
    tp_index = lax.axis_index("tp")
    member = seq_index % SPAN
    group = seq_index // SPAN
    core = seq_index % 2
    core_scalar = core.reshape(1).astype(jnp.int32)
    members = [[g * SPAN + m for m in range(SPAN)] for g in range(seq_count // SPAN)]
    same_core = [list(range(c, seq_count, 2)) for c in range(2)]
    pieces = seq_count // 2
    local_seq = tp_index * (batch // tp_count) + member

    def swap_core(value):
        return lax.ppermute(value, "seq", [(i, i ^ 1) for i in range(seq_count)])

    def swap_tp(value):
        return lax.ppermute(value, "tp", [(i, i ^ 1) for i in range(tp_count)])

    def to_seqs(value):
        return lax.all_to_all(value, "seq", 0, 0, tiled=True, axis_index_groups=members)

    def in_core_order(mine, theirs, axis):
        return jnp.where(
            core == 0,
            jnp.concatenate([mine, theirs], axis=axis),
            jnp.concatenate([theirs, mine], axis=axis),
        )

    slots = lax.dynamic_slice(block_slot, (group * SPAN, local_seq), (SPAN, 1))[:, 0]
    source = jnp.argsort(slots).astype(jnp.int32)
    lengths = lax.dynamic_index_in_dim(doc_lengths, group * batch + local_seq, 0, keepdims=False)
    bounds = jnp.cumsum(lengths)[:-1].astype(jnp.int32)
    bound_count = bounds.shape[0]

    qkv_own = jnp.concatenate([query_weight, key_weight, value_weight], axis=1)
    qkv_sent = lax.dynamic_slice_in_dim(qkv_own, core * (width // 2), width // 2, 0)
    qkv_near = swap_tp(qkv_sent)
    blocks_in = to_seqs(layer_in.reshape(SPAN, BLOCK, width))
    row_bias = lambda value: value.reshape(1, -1)
    bias_own = jnp.concatenate(
        [query_bias, jnp.zeros((half,), F32), value_bias, up_bias]
    ).reshape(1, -1)
    bias_other = swap_tp(bias_own)
    skip_split = skip_values.reshape(tp_count, batch // tp_count, BLOCK, fresh)
    skip_mine = lax.dynamic_index_in_dim(skip_split, tp_index, 0, keepdims=False)
    skip_theirs = lax.dynamic_index_in_dim(skip_split, 1 - tp_index, 0, keepdims=False)
    skip_theirs = swap_tp(skip_theirs)
    skip_blocks = to_seqs(jnp.concatenate([skip_mine, skip_theirs], axis=2))
    qkv_far = swap_core(qkv_near)
    qkv_other = in_core_order(qkv_near, qkv_far, 0)

    out_near = swap_tp(lax.dynamic_slice_in_dim(out_weight, core * (half // 2), half // 2, 0))
    out_other = in_core_order(out_near, swap_core(out_near), 0)
    up_near = swap_tp(lax.dynamic_slice_in_dim(up_weight, core * (units // 2), units // 2, 1))
    down_near = swap_tp(lax.dynamic_slice_in_dim(down_weight, core * (units // 2), units // 2, 0))
    up_far = swap_core(up_near)
    down_far = swap_core(down_near)
    grad_blocks = to_seqs(out_grad.reshape(SPAN, BLOCK, width))

    gain_one, shift_one = row_bias(gain_attention), row_bias(shift_attention)
    gain_two, shift_two = row_bias(gain_feed), row_bias(shift_feed)
    columns = qkv_own.shape[1]
    qkv_bias = jnp.concatenate([bias_own[:, :columns], bias_other[:, :columns]], axis=0)
    own_shape = (SPAN, BLOCK, width)

    norm_one, queries, keys, values = call(
        project_kernel,
        1,
        (SPAN,),
        [
            placed(width), placed(2 * fresh), full((width, columns)), full((width, columns)),
            full((2, columns)), full((1, width)), full((1, width)),
        ],
        [placed(width), in_order(width), in_order(width), in_order(width)],
        [shape_of(own_shape, BF16)] + [shape_of((tokens, width), BF16)] * 3,
        flops=4 * tokens * width * columns,
        name="project",
    )(source, blocks_in, skip_blocks, qkv_own, qkv_other, qkv_bias, gain_one, shift_one)

    heads = width // HEAD
    head_rows = -(-heads // 8) * 8
    lse_spec = pl.BlockSpec((head_rows, BLOCK), lambda p, *_: (0, p))
    attended, log_total, middle, norm_two = call(
        partial(attend_kernel, bound_count),
        2,
        (SPAN,),
        [
            placed(width), in_order(width), full((tokens, width)), full((tokens, width)),
            full((half, width)), full((half, width)), full((1, width)), full((1, width)),
            full((1, width)),
        ],
        [placed(width), lse_spec, placed(width), placed(width)],
        [
            shape_of(own_shape, BF16), shape_of((head_rows, tokens), F32),
            shape_of(own_shape, F32), shape_of(own_shape, BF16),
        ],
        scratch=[pltpu.VMEM((BLOCK, width), BF16), pltpu.VMEM((BLOCK, 128), F32)],
        flops=8 * tokens * BLOCK * width * 2,
        name="attend",
    )(
        source, bounds, blocks_in, queries, keys, values, out_weight, out_other,
        row_bias(out_bias), gain_two, shift_two,
    )

    rows_two = norm_two.reshape(tokens, width)
    grad_rows = grad_blocks.reshape(tokens, width)
    chunk = 256
    own = feed(
        True, core_scalar, rows_two, grad_rows, (up_weight, down_weight),
        bias_own[:, columns:], (), chunk,
    )
    other = feed(
        False, core_scalar, rows_two, grad_rows, (up_near, up_far, down_near, down_far),
        bias_other[:, columns:], own[:2], chunk,
    )
    feed_out, second_grad = other[:2]

    def reduced(own_keep, own_send, other_keep, other_send):
        mine = own_keep.astype(F32) + swap_core(own_send).astype(F32)
        given = (other_keep.astype(F32) + swap_core(other_send).astype(F32)).astype(BF16)
        return (mine + swap_tp(given).astype(F32)).astype(BF16)

    def across(value):
        rows = value.shape[0]
        split = value.reshape(pieces, rows // pieces, value.shape[1])
        parts = lax.all_to_all(split, "seq", 0, 0, tiled=True, axis_index_groups=same_core)
        piece = jnp.sum(parts.astype(F32), axis=0, keepdims=True).astype(BF16)
        spread = jnp.broadcast_to(piece, split.shape)
        whole = lax.all_to_all(spread, "seq", 0, 0, tiled=True, axis_index_groups=same_core)
        return whole.reshape(value.shape)

    def finished(value, axis):
        return in_core_order(value, swap_core(value), axis).astype(F32)

    grad_up_weight = finished(across(reduced(own[2], own[3], other[2], other[3])), 1)
    grad_down_weight = finished(across(reduced(own[4], own[5], other[4], other[5])), 0)

    layer_blocks, middle_grad, att_grad, out_keep, out_send, small_two = call(
        residual_kernel,
        1,
        (SPAN,),
        [
            in_order(width), in_order(width), in_order(width), by_block(width), by_block(width),
            full((half, width)), full((half, width)), full((1, width)), full((1, width)),
        ],
        [
            by_block(width), by_block(width), by_block(width),
            full((2, half // 2, width)), full((2, half // 2, width)), full((4, width)),
        ],
        [
            shape_of(own_shape, BF16), shape_of(own_shape, F32), shape_of(own_shape, BF16),
            shape_of((2, half // 2, width), BF16), shape_of((2, half // 2, width), BF16),
            shape_of((4, width), F32),
        ],
        scratch=[pltpu.VMEM((width, width), F32)],
        flops=4 * tokens * width * width,
        name="residual",
    )(
        core_scalar, feed_out, second_grad, grad_rows, middle, attended, out_weight, out_other,
        gain_two, row_bias(down_bias),
    )
    layer_out = to_seqs(layer_blocks).reshape(tokens, width)

    grads_own, grads_other, grads_skip = call(
        partial(attend_back_kernel, bound_count),
        2,
        (SPAN,),
        [
            in_order(width), full((tokens, width)), full((tokens, width)), placed(width),
            placed(width), lse_spec,
        ],
        [
            full((SPAN, BLOCK, columns)), full((SPAN, BLOCK, columns)),
            full((SPAN, BLOCK, 2 * fresh)),
        ],
        [
            shape_of((SPAN, BLOCK, columns), BF16), shape_of((SPAN, BLOCK, columns), BF16),
            shape_of((SPAN, BLOCK, 2 * fresh), BF16),
        ],
        scratch=[
            pltpu.VMEM((BLOCK, width), BF16), pltpu.VMEM((tokens, width), F32),
            pltpu.VMEM((tokens, width), F32), pltpu.VMEM((head_rows, BLOCK), F32),
        ],
        flops=20 * tokens * BLOCK * width * 2,
        name="attend_back",
    )(source, bounds, queries, keys, values, attended, att_grad, log_total)

    qkv_keep, qkv_send, qkv_sums = call(
        weight_kernel,
        1,
        (1,),
        [full((tokens, width)), full((tokens, columns)), full((tokens, columns))],
        [
            full((2, width // 2, columns)), full((2, width // 2, columns)), full((2, columns)),
        ],
        [
            shape_of((2, width // 2, columns), BF16), shape_of((2, width // 2, columns), BF16),
            shape_of((2, columns), F32),
        ],
        scratch=[pltpu.VMEM((width, columns), F32)],
        flops=4 * tokens * width * columns,
        name="weights",
    )(
        core_scalar, norm_one.reshape(tokens, width), grads_own.reshape(tokens, columns),
        grads_other.reshape(tokens, columns),
    )

    input_blocks, small_one = call(
        input_kernel,
        0,
        (SPAN,),
        [
            by_block(columns), by_block(columns), full((width, columns)), full((width, columns)),
            by_block(width), by_block(width), full((1, width)),
        ],
        [by_block(width), full((2, width))],
        [shape_of(own_shape, BF16), shape_of((2, width), F32)],
        flops=4 * tokens * width * columns,
        name="input",
    )(grads_own, grads_other, qkv_own, qkv_other, blocks_in, middle_grad, gain_one)
    input_grad = to_seqs(input_blocks).reshape(tokens, width).astype(F32)

    skip_back = to_seqs(grads_skip)
    skip_other = swap_tp(skip_back[:, :, fresh:])
    skip_own = skip_back[:, :, :fresh]
    skip_grad = jnp.where(
        tp_index == 0,
        jnp.concatenate([skip_own, skip_other], axis=0),
        jnp.concatenate([skip_other, skip_own], axis=0),
    ).reshape(batch * BLOCK, fresh).astype(F32)

    def reduced_pair(keep, send):
        both = keep.astype(F32) + swap_core(send).astype(F32)
        return (both[0] + swap_tp(both[1].astype(BF16)).astype(F32)).astype(BF16)

    grad_out_weight = finished(across(reduced_pair(out_keep, out_send)), 0)
    grad_qkv = finished(across(reduced_pair(qkv_keep, qkv_send)), 0)

    shared = jnp.concatenate([small_one.reshape(-1), small_two.reshape(-1)])
    split_own = jnp.concatenate([qkv_sums[0], own[6].reshape(-1)])
    split_other = jnp.concatenate([qkv_sums[1], other[6].reshape(-1)])
    vectors = jnp.concatenate([shared, split_own]) + swap_tp(
        jnp.concatenate([shared, split_other])
    )
    distance = 1
    while distance < seq_count:
        vectors = vectors + lax.ppermute(
            vectors, "seq", [(i, i ^ distance) for i in range(seq_count)]
        )
        distance *= 2
    shared = vectors[:6 * width].reshape(6, width)
    split = vectors[6 * width:]

    return (
        layer_out,
        input_grad,
        skip_grad,
        shared[0],
        shared[1],
        grad_qkv[:, :half],
        split[:half],
        grad_qkv[:, half:2 * half],
        grad_qkv[:, 2 * half:],
        split[2 * half:columns],
        grad_out_weight,
        shared[4],
        shared[2],
        shared[3],
        grad_up_weight,
        split[columns:],
        grad_down_weight,
        shared[5],
    )


def solution(mesh):
    return jax.shard_map(
        partial(per_device, (mesh.shape["seq"], mesh.shape["tp"])),
        mesh=mesh,
        in_specs=(
            P(("seq", "tp"), None),
            P("seq", "tp"),
            P(),
            P(),
            P(),
            P(),
            P(None, "tp"),
            P("tp"),
            P(None, "tp"),
            P(None, "tp"),
            P("tp"),
            P("tp", None),
            P(),
            P(),
            P(),
            P(None, "tp"),
            P("tp"),
            P("tp", None),
            P(),
            P(("seq", "tp"), None),
        ),
        out_specs=(
            P(("seq", "tp"), None),
            P(("seq", "tp"), None),
            P("seq", "tp"),
            P(),
            P(),
            P(None, "tp"),
            P("tp"),
            P(None, "tp"),
            P(None, "tp"),
            P("tp"),
            P("tp", None),
            P(),
            P(),
            P(),
            P(None, "tp"),
            P("tp"),
            P("tp", None),
            P(),
        ),
        check_vma=False,
    )
```

```python
from functools import partial

import jax
import jax.numpy as jnp
from jax import lax
from jax.experimental import pallas as pl
from jax.experimental.pallas import tpu as pltpu
from jax.sharding import PartitionSpec as P

HEAD = 64
SEQ_LEN = 1024
BLOCK = 256
LONGEST = 512
SPAN = SEQ_LEN // BLOCK
REACH = -(-LONGEST // BLOCK) + 1
PAIR = 2 * HEAD
EPSILON = 1e-05
MASKED = -1e30
GELU_A = 0.7978845608028654
GELU_B = 0.044715
SCALE = HEAD ** (-0.5)
DOCS = 4
PARTS = 4
CORE, LINK, OUTER, MEMBER = 0, 1, 2, 3
BOUND = MEMBER + SPAN
PEAK = 1.15e9
VMEM = 56 * 1024 * 1024

F32 = jnp.float32
BF16 = jnp.bfloat16


def nn(left, right):
    return lax.dot_general(left, right, (((1,), (0,)), ((), ())), preferred_element_type=F32)


def nt(left, right):
    return lax.dot_general(left, right, (((1,), (1,)), ((), ())), preferred_element_type=F32)


def tn(left, right):
    return lax.dot_general(left, right, (((0,), (0,)), ((), ())), preferred_element_type=F32)


def vector(ref):
    return ref[...].reshape(1, -1)


def normed(rows):
    centred = rows - jnp.mean(rows, axis=-1, keepdims=True)
    inverse = lax.rsqrt(jnp.mean(centred * centred, axis=-1, keepdims=True) + EPSILON)
    return centred * inverse, inverse


def norm_back(grad_out, scaled, inverse, gain):
    grad_scaled = grad_out * gain
    first_mean = jnp.mean(grad_scaled, axis=-1, keepdims=True)
    second_mean = jnp.mean(grad_scaled * scaled, axis=-1, keepdims=True)
    return inverse * (grad_scaled - first_mean - scaled * second_mean)


def full(shape):
    return pl.BlockSpec(shape, lambda *_: (0,) * len(shape), pipeline_mode=pl.Buffered(1))


def member_at(p, ids):
    return ids[MEMBER + p]


def doc_bounds(ids):
    return [ids[BOUND + index] for index in range(DOCS - 1)]


def placed(columns, rows=BLOCK, column=0):
    return pl.BlockSpec(
        (None, rows, columns), lambda p, ids: (member_at(p, ids), 0, column)
    )


def in_rows(columns):
    return pl.BlockSpec((BLOCK, columns), lambda p, *_: (p, 0))


def by_block(columns):
    return pl.BlockSpec((None, BLOCK, columns), lambda p, *_: (p, 0, 0))


def shape_of(shape, dtype):
    return jax.ShapeDtypeStruct(shape, dtype)


def call(kernel, scalars, grid, ins, outs, out_shapes, scratch=(), micros=1, name=None,
         aliases=None):
    return pl.pallas_call(
        kernel,
        grid_spec=pltpu.PrefetchScalarGridSpec(
            num_scalar_prefetch=scalars,
            grid=grid,
            in_specs=ins,
            out_specs=outs,
            scratch_shapes=scratch,
        ),
        out_shape=out_shapes,
        compiler_params=pltpu.CompilerParams(
            dimension_semantics=("arbitrary",) * len(grid), vmem_limit_bytes=VMEM
        ),
        cost_estimate=pl.CostEstimate(
            flops=int(micros * PEAK), bytes_accessed=int(micros * PEAK) // 1000, transcendentals=0
        ),
        input_output_aliases=aliases or {},
        name=name,
    )


def project_kernel(
    ids, x_ref, own_ref, near_ref, far_ref, bias_ref, gain_ref, shift_ref,
    norm_ref, q_ref, k_ref, fresh_ref, other_ref, out_ref,
):
    half = q_ref.shape[1] // 2
    fresh = half // 2
    split = other_ref.shape[0] // 2

    @pl.when(pl.program_id(0) == 0)
    def _():
        first = ids[CORE] == 0
        near, far = near_ref[...], far_ref[...]
        low, high = jnp.where(first, near, far), jnp.where(first, far, near)
        other_ref[:split, :] = low[:split]
        other_ref[split:, :] = high[:split]
        out_ref[:half // 2, :] = low[split:]
        out_ref[half // 2:, :] = high[split:]

    scaled, _ = normed(x_ref[...].astype(F32))
    rows = (scaled * vector(gain_ref) + vector(shift_ref)).astype(BF16)
    norm_ref[...] = rows
    for side, weight in enumerate((own_ref, other_ref)):
        made = nn(rows, weight[:2 * half, :])
        value = nt(rows, weight[2 * half:, :])
        columns = slice(side * half, (side + 1) * half)
        q_ref[:, columns] = (made[:, :half] + bias_ref[side:side + 1, :half]).astype(BF16)
        k_ref[:, columns] = made[:, half:].astype(BF16)
        fresh_ref[side] = (value + bias_ref[side:side + 1, half:half + fresh]).astype(BF16)


def doc_start(position, bounds):
    start = jnp.zeros_like(position)
    for bound in bounds:
        start = jnp.where(position >= bound, bound, start)
    return start


def attend_kernel(
    ids, x_ref, q_ref, k_ref, fresh_ref, skip_ref, own_ref, other_ref,
    bias_ref, gain_ref, shift_ref, v_ref, att_ref, lse_ref, middle_ref, norm_ref, att_s, lse_s,
):
    p = pl.program_id(0)
    bounds = doc_bounds(ids)
    skipped = skip_ref[...].T
    part = skipped.shape[1] // 2
    v_ref[pl.ds(pl.multiple_of(p * BLOCK, BLOCK), BLOCK), :] = jnp.concatenate(
        [fresh_ref[0], skipped[:, :part], fresh_ref[1], skipped[:, part:]], axis=1
    )
    width = q_ref.shape[1]
    half = width // 2
    first = doc_start(p * BLOCK, bounds)
    needed = p - first // BLOCK + 1
    lane = lax.broadcasted_iota(jnp.int32, (1, PAIR), 1)
    low = lane < HEAD
    picks = [jnp.where(low, SCALE, 0.0).astype(BF16), jnp.where(low, 0.0, SCALE).astype(BF16)]

    def run(count):
        span = count * BLOCK
        base = pl.multiple_of((p - count + 1) * BLOCK, BLOCK)
        row = p * BLOCK + lax.broadcasted_iota(jnp.int32, (BLOCK, 1), 0)
        start = doc_start(row, bounds)
        column = base + lax.broadcasted_iota(jnp.int32, (1, span), 1)
        seen = (column <= row) & (column >= start)
        bias = jnp.where(seen, 0.0, MASKED)
        head_lane = lax.broadcasted_iota(jnp.int32, (1, 128), 1)

        @pl.loop(0, width // PAIR)
        def _(pair):
            lanes = pl.ds(pl.multiple_of(pair * PAIR, PAIR), PAIR)
            queries = q_ref[:, lanes]
            keys = k_ref[pl.ds(base, span), lanes]
            values = v_ref[pl.ds(base, span), lanes]
            outs = []
            for side in range(2):
                scores = nt(queries * picks[side], keys) + bias
                top = jnp.max(scores, axis=1, keepdims=True)
                probs = jnp.exp(scores - top)
                total = jnp.sum(probs, axis=1, keepdims=True)
                outs.append(nn(probs.astype(BF16), values) / total)
                lse_s[...] = jnp.where(
                    head_lane == 2 * pair + side, top + jnp.log(total), lse_s[...]
                )
            att_s[:, lanes] = jnp.where(low, outs[0], outs[1]).astype(BF16)

    for count in range(1, REACH + 1):
        pl.when(needed == count)(partial(run, count))

    lse_ref[...] = lse_s[...].T[:lse_ref.shape[0], :]
    attended = att_s[...]
    att_ref[...] = attended
    middle = (
        x_ref[...].astype(F32)
        + nn(attended[:, :half], own_ref[...])
        + nn(attended[:, half:], other_ref[...])
        + vector(bias_ref)
    )
    middle_ref[...] = middle
    scaled, _ = normed(middle)
    norm_ref[...] = (scaled * vector(gain_ref) + vector(shift_ref)).astype(BF16)


def feed_kernel(fetched, has_sums, has_grads, ids, *refs):
    norm_ref, grad_ref = refs[:2]
    if fetched:
        mine_ref, theirs_ref, down_ref, bias_ref = refs[2:6]
        refs = refs[6:]
        first = ids[OUTER] % 2 == 0
        mine, theirs = mine_ref[...], theirs_ref[...]
        up = jnp.concatenate(
            [jnp.where(first, mine, theirs), jnp.where(first, theirs, mine)], axis=0
        )
        down = down_ref[...]
    else:
        weight_ref, bias_ref = refs[2:4]
        refs = refs[4:]
        up = weight_ref[:weight_ref.shape[0] // 2, :]
        down = weight_ref[weight_ref.shape[0] // 2:, :]
    units = up.shape[0]
    if has_sums:
        out_in, back_in = refs[:2]
        refs = refs[2:]
    if has_grads:
        made_in = refs[0]
        refs = refs[1:]
    out_ref, back_ref, gb_ref = refs[:3]
    made_refs = refs[3:]
    rows = norm_ref[...]
    grads = grad_ref[...]
    hidden = nt(rows, up) + bias_ref[...]
    square = hidden * hidden
    curve = jnp.tanh(hidden * (GELU_A + GELU_A * GELU_B * square))
    plus = 0.5 + 0.5 * curve
    value = hidden * plus
    active = value.astype(BF16)
    slope = plus + value * (1.0 - curve) * (GELU_A + 3.0 * GELU_A * GELU_B * square)
    hidden_grad = nt(grads, down) * slope
    gb_ref[...] = jnp.sum(hidden_grad, axis=0, keepdims=True)
    hidden_low = hidden_grad.astype(BF16)
    out = nn(active, down)
    back = nn(hidden_low, up)
    if has_sums:
        out = out + out_in[...].astype(F32)
        back = back + back_in[...].astype(F32)
    out_ref[...] = out.astype(BF16)
    back_ref[...] = back.astype(BF16)
    for piece, left, right in (
        (slice(0, units), hidden_low, rows), (slice(units, 2 * units), active, grads)
    ):
        made = tn(left, right)
        if has_grads:
            made = made + made_in[piece, :].astype(F32)
        made = made.astype(BF16)
        count = made_refs[0].shape[0]
        for row in range(piece.start, piece.stop, count):
            part = made_refs[row // count]
            if count > units:
                part[piece, :] = made
            else:
                part[...] = made[row - piece.start:row - piece.start + count]


def feed(ids, rows, grads, weights, bias, sums=(), made=(), parts=1):
    tokens, width = rows.shape
    units = bias.shape[1]
    total = full((tokens, width))
    return call(
        partial(feed_kernel, len(weights) > 1, len(sums) > 0, len(made) > 0),
        1,
        (1,),
        [total, total] + [full(weight.shape) for weight in weights] + [full((1, units))]
        + [total] * len(sums) + [full((2 * units, width))] * len(made),
        [total, total, full((1, units))] + [full((2 * units // parts, width))] * parts,
        [
            shape_of((tokens, width), BF16), shape_of((tokens, width), BF16),
            shape_of((1, units), F32),
        ] + [shape_of((2 * units // parts, width), BF16)] * parts,
        micros=14,
        name="feed",
    )(ids, rows, grads, *weights, bias, *sums, *made)


def residual_kernel(
    ids, out_a, out_b, back_a, back_b, grad_ref, middle_ref, att_ref, own_ref, other_ref,
    gain_ref, down_bias_ref, layer_ref, mg_ref, ga_ref, keep_ref, send_ref, small_ref, acc_s,
):
    p = pl.program_id(0)
    half = own_ref.shape[0]
    middle = middle_ref[...]
    summed = lambda refs: sum(ref[...].astype(F32) for ref in refs)
    layer_ref[...] = (middle + summed((out_a, out_b)) + vector(down_bias_ref)).astype(BF16)
    scaled, inverse = normed(middle)
    second = summed((back_a, back_b))
    out_grad = grad_ref[...].astype(F32)
    middle_grad = out_grad + norm_back(second, scaled, inverse, vector(gain_ref))
    mg_ref[...] = middle_grad
    low = middle_grad.astype(BF16)
    ga_ref[:, :half] = nt(low, own_ref[...]).astype(BF16)
    ga_ref[:, half:] = nt(low, other_ref[...]).astype(BF16)
    weight_grad = tn(att_ref[...], low)
    sums = jnp.concatenate(
        [
            jnp.sum(value, axis=0, keepdims=True)
            for value in (second * scaled, second, middle_grad, out_grad)
        ],
        axis=0,
    )

    @pl.when(p == 0)
    def _():
        acc_s[...] = weight_grad
        small_ref[...] = sums

    @pl.when(p > 0)
    def _():
        acc_s[...] += weight_grad
        small_ref[...] += sums

    @pl.when(p == pl.num_programs(0) - 1)
    def _():
        rows = half // 2
        near = pl.multiple_of(ids[CORE] * rows, 32)
        far = pl.multiple_of(rows - ids[CORE] * rows, 32)
        for side in range(2):
            keep_ref[side] = acc_s[pl.ds(side * half + near, rows), :].astype(BF16)
            send_ref[side] = acc_s[pl.ds(side * half + far, rows), :].astype(BF16)


def attend_back_kernel(
    head_base, ids, q_ref, k_ref, v_ref, att_ref, ga_ref, lse_ref,
    made_ref, skip_ref, dq_s, dk_s, dv_s, delta_s,
):
    p = pl.program_id(0)
    width = q_ref.shape[1]
    fresh = width // 2
    bounds = doc_bounds(ids)
    place = member_at(p, ids)
    first = doc_start(p * BLOCK, bounds)
    needed = p - first // BLOCK + 1
    low = lax.broadcasted_iota(jnp.int32, (1, PAIR), 1) < HEAD
    picks = [jnp.where(low, SCALE, 0.0).astype(BF16), jnp.where(low, 0.0, SCALE).astype(BF16)]
    ones = [jnp.where(low, 1.0, 0.0).astype(BF16), jnp.where(low, 0.0, 1.0).astype(BF16)]

    @pl.when(p == 0)
    def _():
        dk_s[...] = jnp.zeros_like(dk_s)
        dv_s[...] = jnp.zeros_like(dv_s)

    product = ga_ref[...].astype(F32) * att_ref[...].astype(F32)
    high = product.astype(BF16)
    rest = (product - high.astype(F32)).astype(BF16)
    owner = lax.broadcasted_iota(jnp.int32, (delta_s.shape[0], width), 1) // HEAD
    which = lax.broadcasted_iota(jnp.int32, (delta_s.shape[0], width), 0)
    gather = (owner == which).astype(F32).astype(BF16)
    delta_s[...] = nt(gather, high) + nt(gather, rest)

    def run(count):
        span = count * BLOCK
        base = pl.multiple_of((p - count + 1) * BLOCK, BLOCK)
        row = p * BLOCK + lax.broadcasted_iota(jnp.int32, (1, BLOCK), 1)
        start = doc_start(row, bounds)
        column = base + lax.broadcasted_iota(jnp.int32, (span, 1), 0)
        seen = (column <= row) & (column >= start)
        bias = jnp.where(seen, 0.0, MASKED)

        @pl.loop(0, width // PAIR)
        def _(pair):
            lanes = pl.ds(pl.multiple_of(pair * PAIR, PAIR), PAIR)
            queries = q_ref[:, lanes]
            grads = ga_ref[:, lanes]
            keys = k_ref[pl.ds(base, span), lanes]
            values = v_ref[pl.ds(base, span), lanes]
            query_parts = []
            for side in range(2):
                head = 2 * pair + side
                picked = queries * picks[side]
                chosen = grads * ones[side]
                scores = nt(keys, picked) + bias
                probs = jnp.exp(scores - lse_ref[pl.ds(head_base + head, 1), :])
                dprobs = nt(values, chosen)
                dscores = (probs * (dprobs - delta_s[pl.ds(head, 1), :])).astype(BF16)
                value_part = nn(probs.astype(BF16), chosen)
                key_part = nn(dscores, picked)
                query_parts.append(tn(dscores, keys))
                if side == 0:
                    value_sum, key_sum = value_part, key_part
                else:
                    value_sum, key_sum = value_sum + value_part, key_sum + key_part
            dv_s[pl.ds(base, span), lanes] += value_sum
            dk_s[pl.ds(base, span), lanes] += key_sum
            dq_s[:, lanes] = (
                jnp.where(low, query_parts[0], query_parts[1]) * SCALE
            ).astype(BF16)

    for count in range(1, REACH + 1):
        pl.when(needed == count)(partial(run, count))

    made_ref[place, :, :width] = dq_s[...]

    @pl.when(p == pl.num_programs(0) - 1)
    def _():
        for block in range(SPAN):
            rows = slice(block * BLOCK, (block + 1) * BLOCK)
            to = member_at(block, ids)
            made_ref[to, :, width:2 * width] = dk_s[rows, :].astype(BF16)
            value_grad = dv_s[rows, :]
            made_ref[to, :, 2 * width:] = value_grad[:, :fresh].astype(BF16)
            skip_ref[to] = value_grad.T[fresh:, :].astype(BF16)


def weight_kernel(ids, norm_ref, made_ref, keep_ref, send_ref, sums_ref, made_s):
    rows = norm_ref[...]
    grads = made_ref[...]
    width = rows.shape[1]
    made_s[:width, :] = tn(rows, grads[:, :width])
    made_s[width:, :] = tn(grads[:, width:], rows)
    half = made_s.shape[0] // 2
    near = pl.multiple_of(ids[CORE] * half, 32)
    far = pl.multiple_of(half - ids[CORE] * half, 32)
    for target, start in ((keep_ref, near), (send_ref, far)):
        target[:half, :] = made_s[pl.ds(start, half), :].astype(BF16)
        target[half:, :] = jnp.zeros((target.shape[0] - half, width), BF16)
    sums_ref[...] = jnp.sum(grads.astype(F32), axis=0, keepdims=True)


def input_kernel(
    own_ref, other_ref, w_own_ref, w_other_ref, x_ref, mg_ref, gain_ref, grad_ref, small_ref
):
    p = pl.program_id(0)
    first = None
    for made_ref, weight in ((own_ref, w_own_ref), (other_ref, w_other_ref)):
        width = weight.shape[1]
        part = nt(made_ref[:, :width], weight[:width, :]) + nn(made_ref[:, width:], weight[width:, :])
        first = part if first is None else first + part
    scaled, inverse = normed(x_ref[...].astype(F32))
    grad_ref[...] = (mg_ref[...] + norm_back(first, scaled, inverse, vector(gain_ref))).astype(BF16)
    sums = jnp.concatenate(
        [jnp.sum(value, axis=0, keepdims=True) for value in (first * scaled, first)], axis=0
    )

    @pl.when(p == 0)
    def _():
        small_ref[...] = sums

    @pl.when(p > 0)
    def _():
        small_ref[...] += sums


def fold_kernel(groups, starts, ids, *refs):
    sources = sum(len(group) for group in groups)
    outs = refs[sources:-1]
    total_s = refs[-1]
    row = 0
    place = 0
    for group in groups:
        total = None
        for index in group:
            ref = refs[place]
            place += 1
            value = (ref[...] if index is None else ref[index]).astype(F32)
            total = value if total is None else total + value
        total_s[row:row + total.shape[0], :] = total
        row += total.shape[0]
    for out, start in zip(outs, starts):
        at = start(ids)
        if not isinstance(at, int):
            at = pl.multiple_of(at, 8)
        out[...] = total_s[pl.ds(at, out.shape[0]), :].astype(BF16)


def fold(ids, groups, starts, count):
    arrays = [entry[0] for group in groups for entry in group]
    indices = tuple(tuple(entry[1] for entry in group) for group in groups)
    width = arrays[0].shape[-1]
    rows = sum(group[0][0].shape[-2] for group in groups)
    return call(
        partial(fold_kernel, indices, starts),
        1,
        (1,),
        [full(array.shape) for array in arrays],
        [full((count, width)) for _ in starts],
        [shape_of((count, width), BF16) for _ in starts],
        scratch=[pltpu.VMEM((rows, width), F32)],
        micros=3.5,
        name="fold",
    )(ids, *arrays)


def join_kernel(ends, ids, *refs):
    for ref, end in zip(refs[:-1], ends):
        rows = ref.shape[0]
        refs[-1][pl.ds(pl.multiple_of(end(ids) * rows, 8), rows), :] = ref[...]


def join(ids, pieces, ends):
    rows, width = pieces[0].shape
    spec = full((rows, width))
    return call(
        partial(join_kernel, ends),
        1,
        (1,),
        [spec] * len(pieces),
        [full((rows * len(pieces), width))],
        [shape_of((rows * len(pieces), width), BF16)],
        micros=2.5,
        name="join",
    )(ids, *pieces)[0]


def both_halves(ids, bit, mine, theirs):
    first = ids[bit] == 0
    return jnp.where(first, mine, theirs), jnp.where(first, theirs, mine)


def place_feed_kernel(ids, mine_ref, theirs_ref, up_ref, down_ref, out_ref):
    units = down_ref.shape[0]
    here = pl.program_id(0) == ids[CORE]
    whole = jnp.where(here, mine_ref[...], theirs_ref[...]).astype(F32)
    up_ref[...] = whole[:units].T
    down_ref[...] = whole[units:2 * units]
    out_ref[...] = whole[2 * units:]


def place_feed(ids, mine, theirs, units):
    rows, width = mine.shape
    size = units // 2
    out_rows = rows - 2 * size
    return call(
        place_feed_kernel,
        1,
        (2,),
        [full((rows, width))] * 2,
        [
            pl.BlockSpec((width, size), lambda h, ids: (0, h)),
            pl.BlockSpec((size, width), lambda h, ids: (h, 0)),
            pl.BlockSpec((out_rows, width), lambda h, ids: (h, 0)),
        ],
        [
            shape_of((width, units), F32), shape_of((units, width), F32),
            shape_of((2 * out_rows, width), F32),
        ],
        micros=8,
        name="place_feed",
    )(ids, mine, theirs)


def place_qkv_kernel(ids, mine, mine_far, theirs, theirs_far, q_ref, k_ref, v_ref):
    half = q_ref.shape[1]
    split = (q_ref.shape[0] + v_ref.shape[0]) // 2
    near = jnp.concatenate(both_halves(ids, LINK, mine[...], mine_far[...]), axis=0)
    far = jnp.concatenate(both_halves(ids, LINK, theirs[...], theirs_far[...]), axis=0)
    low, high = [value[:split].astype(F32) for value in both_halves(ids, CORE, near, far)]
    rest = q_ref.shape[0] - split
    for ref, columns in ((q_ref, slice(0, half)), (k_ref, slice(half, 2 * half))):
        ref[:split, :] = low[:, columns]
        ref[split:, :] = high[:rest, columns]
    v_ref[...] = high[rest:]


def place_qkv(ids, pieces, half, fresh):
    rows, width = pieces[0].shape
    return call(
        place_qkv_kernel,
        1,
        (1,),
        [full((rows, width))] * 4,
        [full((width, half)), full((width, half)), full((fresh, width))],
        [shape_of((width, half), F32), shape_of((width, half), F32), shape_of((fresh, width), F32)],
        micros=4,
        name="place_qkv",
    )(ids, *pieces)


def tie(value, *others):
    return lax.optimization_barrier((value,) + others)[0]


def per_device(
    sizes,
    layer_in,
    skip_values,
    block_slot,
    doc_lengths,
    gain_attention,
    shift_attention,
    query_weight,
    query_bias,
    key_weight,
    value_weight,
    value_bias,
    out_weight,
    out_bias,
    gain_feed,
    shift_feed,
    up_weight,
    up_bias,
    down_weight,
    down_bias,
    out_grad,
):
    seq_count, tp_count = sizes
    width = layer_in.shape[1]
    half = query_weight.shape[1]
    fresh = value_weight.shape[1]
    units = up_weight.shape[1]
    tokens = layer_in.shape[0]
    batch = skip_values.shape[0] // BLOCK
    heads = width // HEAD
    head_rows = -(-heads // 8) * 8
    packed = 2 * half + fresh
    side = units // 2
    seq_index = lax.axis_index("seq")
    tp_index = lax.axis_index("tp")
    member = seq_index % SPAN
    group = seq_index // SPAN
    core = seq_index % 2
    pair_bit = seq_index // 2 % 2
    members = [[g * SPAN + m for m in range(SPAN)] for g in range(seq_count // SPAN)]
    alike = [list(range(m, seq_count, SPAN)) for m in range(SPAN)]
    same_core = [list(range(c, seq_count, 2)) for c in range(2)]
    pieces = seq_count // SPAN
    local_seq = tp_index * (batch // tp_count) + member

    def swap_seq(value, distance):
        return lax.ppermute(value, "seq", [(i, i ^ distance) for i in range(seq_count)])

    def swap_core(value):
        return swap_seq(value, 1)

    def swap_tp(value):
        return lax.ppermute(value, "tp", [(i, i ^ 1) for i in range(tp_count)])

    def to_seqs(value):
        return lax.all_to_all(value, "seq", 0, 0, tiled=True, axis_index_groups=members)

    def either(bit, first, second):
        return jnp.where(bit == 0, first, second)

    def in_order(bit, mine, theirs):
        return either(
            bit, jnp.concatenate([mine, theirs], 0), jnp.concatenate([theirs, mine], 0)
        )

    def rows_of(value, start, count):
        return lax.dynamic_slice_in_dim(value, start, count, 0)

    def row(value):
        return value.reshape(1, -1)

    local_seq = tp_index * (batch // tp_count) + member
    slots = lax.dynamic_slice(block_slot, (group * SPAN, local_seq), (SPAN, 1))
    holders = jnp.sum(
        jnp.where(
            slots == lax.broadcasted_iota(jnp.int32, (SPAN, SPAN), 1),
            lax.broadcasted_iota(jnp.int32, (SPAN, SPAN), 0), 0,
        ),
        axis=0,
    )
    lengths = lax.dynamic_slice(doc_lengths, (group * batch + local_seq, 0), (1, DOCS))
    ends = jnp.sum(
        jnp.where(
            lax.broadcasted_iota(jnp.int32, (DOCS, DOCS), 0)
            <= lax.broadcasted_iota(jnp.int32, (DOCS, DOCS), 1),
            lengths.reshape(DOCS, 1), 0,
        ),
        axis=0,
    )
    ids = jnp.concatenate(
        [jnp.stack([core, pair_bit, group]).astype(jnp.int32), holders, ends[:DOCS - 1]]
    ).astype(jnp.int32)

    qkv_own = jnp.concatenate(
        [jnp.concatenate([query_weight, key_weight], axis=1), value_weight.T], axis=0
    )
    early_sent = jnp.concatenate(
        [
            rows_of(qkv_own, core * (packed // 2), packed // 2),
            rows_of(out_weight, core * (half // 2), half // 2),
        ],
        0,
    )
    early_near = swap_tp(early_sent)
    layer_in, skip_values = lax.optimization_barrier((layer_in, skip_values, early_sent))[:2]
    blocks_in = to_seqs(layer_in.reshape(SPAN, BLOCK, width))
    skip_split = skip_values.T.reshape(fresh, batch, BLOCK).transpose(1, 0, 2)
    skip_split = skip_split.reshape(tp_count, batch // tp_count, fresh, BLOCK)
    skip_mine = lax.dynamic_index_in_dim(skip_split, tp_index, 0, keepdims=False)
    skip_theirs = swap_tp(lax.dynamic_index_in_dim(skip_split, 1 - tp_index, 0, keepdims=False))
    up_bias_half = rows_of(up_bias, core * side, side)
    bias_own = jnp.concatenate([query_bias, value_bias, up_bias_half])
    bias_other = swap_tp(bias_own)
    feed_own = jnp.concatenate(
        [lax.dynamic_slice_in_dim(up_weight, core * side, side, 1).T,
         rows_of(down_weight, core * side, side)], 0,
    )
    feed_own, ids = lax.optimization_barrier((feed_own, ids))
    early_near, skip_theirs, bias_other = lax.optimization_barrier(
        (early_near, skip_theirs, bias_other, feed_own)
    )[:3]
    early_far = swap_core(early_near)
    up_part = rows_of(feed_own, group % 2 * (side // 2), side // 2)
    up_near = swap_tp(tie(up_part, early_near))
    down_sent = tie(feed_own[side:], early_near)

    qkv_bias = jnp.stack([bias_own[:half + fresh], bias_other[:half + fresh]])
    own_shape = (SPAN, BLOCK, width)
    flat = (tokens, width)

    norm_one, queries, keys, fresh_values, qkv_other, out_other = call(
        project_kernel,
        1,
        (SPAN,),
        [
            placed(width), full((packed, width)), full((packed // 2 + half // 2, width)),
            full((packed // 2 + half // 2, width)), full((2, half + fresh)), full((width,)), full((width,)),
        ],
        [
            placed(width), in_rows(width), in_rows(width),
            pl.BlockSpec((2, BLOCK, fresh), lambda p, *_: (0, p, 0)), full((packed, width)),
            full((half, width)),
        ],
        [
            shape_of(own_shape, BF16), shape_of(flat, BF16), shape_of(flat, BF16),
            shape_of((2, tokens, fresh), BF16), shape_of((packed, width), BF16),
            shape_of((half, width), BF16),
        ],
        micros=9,
        name="project",
    )(ids, blocks_in, qkv_own, early_near, early_far, qkv_bias, gain_attention, shift_attention)

    skip_blocks = to_seqs(
        tie(jnp.concatenate([skip_mine, skip_theirs], axis=1), blocks_in)
    )
    grad_blocks = to_seqs(tie(out_grad.reshape(SPAN, BLOCK, width), skip_blocks))
    up_near = tie(up_near, queries)
    up_far = swap_seq(up_near, SPAN)
    down_other = swap_tp(down_sent)
    lse_spec = pl.BlockSpec((head_rows, BLOCK), lambda p, *_: (0, p))
    values, attended, log_total, middle, norm_two = call(
        attend_kernel,
        1,
        (SPAN,),
        [
            placed(width), in_rows(width), full(flat),
            pl.BlockSpec((2, BLOCK, fresh), lambda p, *_: (0, p, 0)), placed(BLOCK, 2 * fresh),
            full((half, width)), full((half, width)), full((width,)), full((width,)),
            full((width,)),
        ],
        [full(flat), placed(width), lse_spec, placed(width), placed(width)],
        [
            shape_of(flat, BF16), shape_of(own_shape, BF16), shape_of((head_rows, tokens), F32),
            shape_of(own_shape, F32), shape_of(own_shape, BF16),
        ],
        scratch=[pltpu.VMEM((BLOCK, width), BF16), pltpu.VMEM((BLOCK, 128), F32)],
        micros=27,
        name="attend",
    )(
        ids, blocks_in, queries, keys, fresh_values, skip_blocks, out_weight, out_other,
        out_bias, gain_feed, shift_feed,
    )
    rows_mine = norm_two.reshape(flat)
    grads_mine = grad_blocks.reshape(flat)

    rows_theirs = swap_core(rows_mine)
    grads_theirs = swap_core(grads_mine)
    feed_other = (up_near, up_far, down_other)
    bias_here = row(up_bias_half)
    bias_there = row(bias_other[half + fresh:])
    out_mine, back_mine, bias_one, made_other = feed(
        ids, rows_mine, grads_mine, feed_other, bias_there
    )
    rows_theirs = tie(rows_theirs, out_mine)
    out_theirs, back_theirs, bias_two, *made_other = feed(
        ids, rows_theirs, grads_theirs, feed_other, bias_there, (), (made_other,), PARTS
    )
    cross_feed = [swap_tp(made_other[0])]
    out_theirs, back_theirs, bias_three, made_own = feed(
        ids, rows_theirs, grads_theirs, (feed_own,), tie(bias_here, made_other[0]),
        (out_theirs, back_theirs),
    )
    out_given = swap_core(out_theirs)
    back_given = swap_core(back_theirs)
    cross_feed.append(swap_tp(tie(made_other[1], cross_feed[0], out_theirs)))
    out_mine, back_mine, bias_four, *made_own = feed(
        ids, rows_mine, grads_mine, (feed_own,), tie(bias_here, cross_feed[0]),
        (out_mine, back_mine), (made_own,), PARTS,
    )
    cross_feed.append(swap_tp(tie(made_other[2], cross_feed[1], out_mine)))

    def begin(groups, rows):
        kept, sent = fold(
            ids, groups,
            [lambda ids: ids[LINK] * (rows // 2), lambda ids: (1 - ids[LINK]) * (rows // 2)],
            rows // 2,
        )
        return kept, swap_seq(sent, 2)

    def inner(kept, given):
        rows = kept.shape[0] // pieces
        groups = [[(kept, None), (given, None)]]
        if pieces > 4:
            whole, = fold(ids, groups, [lambda ids: 0], kept.shape[0])
            whole = whole.reshape(pieces, rows, width)
            return [lax.all_to_all(whole, "seq", 0, 0, tiled=True, axis_index_groups=alike)]
        cut = fold(
            ids, groups,
            [lambda ids, k=k: (ids[OUTER] ^ k) * rows for k in range(pieces)], rows,
        )
        return [cut[0]] + [swap_seq(cut[k], SPAN * k) for k in range(1, pieces)]

    def outer(parts):
        if pieces > 4:
            piece = jnp.sum(parts[0].astype(F32), axis=0, keepdims=True).astype(BF16)
            spread = jnp.broadcast_to(piece, parts[0].shape)
            return [lax.all_to_all(spread, "seq", 0, 0, tiled=True, axis_index_groups=alike)]
        piece, = fold(
            ids, [[(part, None) for part in parts]], [lambda ids: 0], parts[0].shape[0]
        )
        return [piece] + [swap_seq(piece, SPAN * k) for k in range(1, pieces)]

    def joined(spread):
        if pieces > 4:
            return spread[0].reshape(-1, width)
        return join(ids, spread, [lambda ids, k=k: ids[OUTER] ^ k for k in range(pieces)])

    layer_blocks, middle_grad, att_grad, out_keep, out_send, small_two = call(
        residual_kernel,
        1,
        (SPAN,),
        [in_rows(width)] * 5
        + [
            by_block(width), by_block(width), full((half, width)), full((half, width)),
            full((width,)), full((width,)),
        ],
        [
            by_block(width), by_block(width), by_block(width),
            full((2, half // 2, width)), full((2, half // 2, width)), full((4, width)),
        ],
        [
            shape_of(own_shape, BF16), shape_of(own_shape, F32), shape_of(own_shape, BF16),
            shape_of((2, half // 2, width), BF16), shape_of((2, half // 2, width), BF16),
            shape_of((4, width), F32),
        ],
        scratch=[pltpu.VMEM((width, width), F32)],
        micros=12.5,
        name="residual",
    )(
        ids, tie(out_mine, cross_feed[1]), out_given, back_mine, back_given, grads_mine, middle, attended, out_weight,
        out_other, gain_feed, down_bias,
    )
    sent_given = swap_core(out_send)
    out_total = (out_keep.astype(F32) + sent_given.astype(F32)).astype(BF16)
    out_total = tie(out_total, cross_feed[2])
    cross_feed.append(swap_tp(tie(made_other[3], cross_feed[2])))
    cross_out = swap_tp(out_total[1])

    def attend_back(which, query_rows):
        return call(
            partial(attend_back_kernel, which * (heads // 2)),
            1,
            (SPAN,),
            [
                pl.BlockSpec((BLOCK, half), lambda p, *_: (p, which)),
                pl.BlockSpec((tokens, half), lambda p, *_: (0, which)),
                pl.BlockSpec((tokens, half), lambda p, *_: (0, which)),
                placed(half, column=which), placed(half, column=which), lse_spec,
            ],
            [full((SPAN, BLOCK, packed)), full((SPAN, fresh, BLOCK))],
            [shape_of((SPAN, BLOCK, packed), BF16), shape_of((SPAN, fresh, BLOCK), BF16)],
            scratch=[
                pltpu.VMEM((BLOCK, half), BF16), pltpu.VMEM((tokens, half), F32),
                pltpu.VMEM((tokens, half), F32), pltpu.VMEM((8, BLOCK), F32),
            ],
            micros=17.5,
            name="attend_back",
        )(
            ids, query_rows, keys, values, attended, att_grad,
            log_total,
        )

    qkv_rows = -(-packed // 128) * 64

    def weights(made):
        return call(
            weight_kernel,
            1,
            (1,),
            [full(flat), full((tokens, packed))],
            [full((qkv_rows, width)), full((qkv_rows, width)), full((1, packed))],
            [
                shape_of((qkv_rows, width), BF16), shape_of((qkv_rows, width), BF16),
                shape_of((1, packed), F32),
            ],
            scratch=[pltpu.VMEM((packed, width), F32)],
            micros=6,
            name="weights",
        )(ids, norm_one.reshape(flat), made.reshape(tokens, packed))

    layer_out = to_seqs(tie(layer_blocks, out_total)).reshape(flat)
    grads_other, skip_other = attend_back(1, tie(queries, out_total))
    cross_feed[3], cross_out = lax.optimization_barrier(
        (cross_feed[3], cross_out, grads_other)
    )[:2]
    ready_feed, = fold(
        ids,
        [[(mine, None), (theirs, None)] for mine, theirs in zip(made_own, cross_feed)]
        + [[(out_total, 0), (cross_out, None)]],
        [lambda ids: 0],
        2 * side + half // 2,
    )
    total_feed = lax.psum(ready_feed, "seq", axis_index_groups=same_core)
    keep_other, send_other, sums_other = weights(tie(grads_other, ready_feed, layer_out))
    given_other = swap_core(send_other)
    skip_theirs = swap_tp(skip_other)
    total_other, = fold(
        ids, [[(keep_other, None), (given_other, None)]], [lambda ids: 0], qkv_rows
    )
    cross_other = swap_tp(total_other)
    grads_own, skip_own = attend_back(0, tie(queries, total_other))
    keep_own, send_own, sums_own = weights(tie(grads_own, cross_other))
    given_own = swap_core(send_own)

    input_blocks, small_one = call(
        input_kernel,
        0,
        (SPAN,),
        [
            by_block(packed), by_block(packed), full((packed, width)), full((packed, width)),
            by_block(width), by_block(width), full((width,)),
        ],
        [by_block(width), full((2, width))],
        [shape_of(own_shape, BF16), shape_of((2, width), F32)],
        micros=9,
        name="input",
    )(
        tie(grads_own, keep_own), grads_other, qkv_own, qkv_other, blocks_in, middle_grad,
        gain_attention,
    )
    given_own, skip_theirs = lax.optimization_barrier((given_own, skip_theirs, input_blocks))[:2]
    kept_qkv, given_y_qkv = begin(
        [[(keep_own, None), (given_own, None), (cross_other, None)]], qkv_rows
    )
    input_blocks = tie(input_blocks, kept_qkv)
    input_back = to_seqs(input_blocks)
    shared = jnp.concatenate([small_one.reshape(-1), small_two.reshape(-1)])
    widened = lambda value: jnp.where(
        lax.broadcasted_iota(jnp.int32, (2, 1), 0) == core, value, 0.0
    ).reshape(-1)
    split_own = jnp.concatenate([sums_own.reshape(-1), widened(bias_three + bias_four)])
    split_other = jnp.concatenate([sums_other.reshape(-1), widened(bias_one + bias_two)])
    vector_own = jnp.concatenate([shared, split_own])
    vector_other = jnp.concatenate([shared, split_other])

    distances = [1 << bit for bit in range(seq_count.bit_length() - 1)]
    crossed = swap_tp(tie(vector_other, kept_qkv))

    def step(values, vectors, given):
        values = list(values)
        held = lax.optimization_barrier(tuple(values) + (vectors, given))
        return list(held[:-2]), held[-2] + held[-1]

    (given_y_qkv,), vectors = step([given_y_qkv], vector_own, crossed)
    parts_qkv = inner(kept_qkv, given_y_qkv)
    given = swap_seq(vectors, distances[0])
    parts_qkv, vectors = step(parts_qkv, vectors, given)
    spread_qkv = outer(parts_qkv)
    given = swap_seq(vectors, distances[1])
    spread_qkv, vectors = step(spread_qkv, vectors, given)
    whole_qkv = joined(spread_qkv)
    far_qkv = swap_seq(whole_qkv, 2)
    near_theirs = swap_core(whole_qkv)
    given = swap_seq(vectors, distances[2])
    (far_qkv,), vectors = step([far_qkv], vectors, given)
    far_theirs = swap_core(far_qkv)
    for distance in distances[3:]:
        vectors = vectors + swap_seq(vectors, distance)
    pieces_qkv = (whole_qkv, far_qkv, near_theirs, far_theirs)
    grad_query, grad_key, grad_value = place_qkv(ids, pieces_qkv, half, fresh)
    shared = vectors[:6 * width].reshape(6, width)
    split = vectors[6 * width:]

    input_back, skip_theirs = lax.optimization_barrier((input_back, skip_theirs))
    input_grad = input_back.reshape(flat).astype(F32)
    skip_back = to_seqs(jnp.concatenate([skip_own, skip_theirs], axis=1))
    skip_halves = skip_back.reshape(SPAN, 2, fresh, BLOCK).transpose(1, 0, 2, 3)
    skip_halves = either(tp_index, skip_halves, skip_halves[::-1])
    skip_grad = skip_halves.reshape(batch, fresh, BLOCK).transpose(1, 0, 2)
    skip_grad = skip_grad.reshape(fresh, batch * BLOCK).astype(F32).T

    total_feed = tie(total_feed, *pieces_qkv, skip_back)
    grad_up_weight, grad_down_weight, grad_out_weight = place_feed(
        ids, total_feed, swap_core(total_feed), units
    )

    return (
        layer_out,
        input_grad,
        skip_grad,
        shared[0],
        shared[1],
        grad_query,
        split[:half],
        grad_key,
        grad_value.T,
        split[2 * half:packed],
        grad_out_weight,
        shared[4],
        shared[2],
        shared[3],
        grad_up_weight,
        split[packed:],
        grad_down_weight,
        shared[5],
    )


def solution(mesh):
    return jax.shard_map(
        partial(per_device, (mesh.shape["seq"], mesh.shape["tp"])),
        mesh=mesh,
        in_specs=(
            P(("seq", "tp"), None),
            P("seq", "tp"),
            P(),
            P(),
            P(),
            P(),
            P(None, "tp"),
            P("tp"),
            P(None, "tp"),
            P(None, "tp"),
            P("tp"),
            P("tp", None),
            P(),
            P(),
            P(),
            P(None, "tp"),
            P("tp"),
            P("tp", None),
            P(),
            P(("seq", "tp"), None),
        ),
        out_specs=(
            P(("seq", "tp"), None),
            P(("seq", "tp"), None),
            P("seq", "tp"),
            P(),
            P(),
            P(None, "tp"),
            P("tp"),
            P(None, "tp"),
            P(None, "tp"),
            P("tp"),
            P("tp", None),
            P(),
            P(),
            P(),
            P(None, "tp"),
            P("tp"),
            P("tp", None),
            P(),
        ),
        check_vma=False,
    )
```

```python
from functools import partial

import jax
import jax.numpy as jnp
from jax import lax
from jax.experimental import pallas as pl
from jax.experimental.pallas import tpu as pltpu
from jax.sharding import PartitionSpec as P

HEAD = 64
SEQ_LEN = 1024
BLOCK = 256
LONGEST = 512
SPAN = SEQ_LEN // BLOCK
REACH = -(-LONGEST // BLOCK) + 1
PAIR = 2 * HEAD
EPSILON = 1e-05
MASKED = -1e30
GELU_A = 0.7978845608028654
GELU_B = 0.044715
SCALE = HEAD ** (-0.5)
DOCS = 4
PARTS = 4
CORE, MINE, OUTER, TP, MEMBER = 0, 1, 2, 3, 4
BOUND = MEMBER + SPAN
PEAK = 1.15e9
VMEM = 56 * 1024 * 1024

F32 = jnp.float32
BF16 = jnp.bfloat16


def nn(left, right):
    return lax.dot_general(left, right, (((1,), (0,)), ((), ())), preferred_element_type=F32)


def nt(left, right):
    return lax.dot_general(left, right, (((1,), (1,)), ((), ())), preferred_element_type=F32)


def tn(left, right):
    return lax.dot_general(left, right, (((0,), (0,)), ((), ())), preferred_element_type=F32)


def vector(ref):
    return ref[...].reshape(1, -1)


def normed(rows):
    centred = rows - jnp.mean(rows, axis=-1, keepdims=True)
    inverse = lax.rsqrt(jnp.mean(centred * centred, axis=-1, keepdims=True) + EPSILON)
    return centred * inverse, inverse


def norm_back(grad_out, scaled, inverse, gain):
    grad_scaled = grad_out * gain
    first_mean = jnp.mean(grad_scaled, axis=-1, keepdims=True)
    second_mean = jnp.mean(grad_scaled * scaled, axis=-1, keepdims=True)
    return inverse * (grad_scaled - first_mean - scaled * second_mean)


def full(shape):
    return pl.BlockSpec(shape, lambda *_: (0,) * len(shape), pipeline_mode=pl.Buffered(1))


def member_at(p, ids):
    return ids[MEMBER + p]


def doc_bounds(ids):
    return [ids[BOUND + index] for index in range(DOCS - 1)]


def placed(columns, rows=BLOCK, column=0):
    return pl.BlockSpec(
        (None, rows, columns), lambda p, ids: (member_at(p, ids), 0, column)
    )


def in_rows(columns):
    return pl.BlockSpec((BLOCK, columns), lambda p, *_: (p, 0))


def by_block(columns):
    return pl.BlockSpec((None, BLOCK, columns), lambda p, *_: (p, 0, 0))


def shape_of(shape, dtype):
    return jax.ShapeDtypeStruct(shape, dtype)


def call(kernel, scalars, grid, ins, outs, out_shapes, scratch=(), micros=1, name=None,
         aliases=None):
    return pl.pallas_call(
        kernel,
        grid_spec=pltpu.PrefetchScalarGridSpec(
            num_scalar_prefetch=scalars,
            grid=grid,
            in_specs=ins,
            out_specs=outs,
            scratch_shapes=scratch,
        ),
        out_shape=out_shapes,
        compiler_params=pltpu.CompilerParams(
            dimension_semantics=("arbitrary",) * len(grid), vmem_limit_bytes=VMEM
        ),
        cost_estimate=pl.CostEstimate(
            flops=int(micros * PEAK), bytes_accessed=int(micros * PEAK) // 1000, transcendentals=0
        ),
        input_output_aliases=aliases or {},
        name=name,
    )


def project_kernel(
    ids, x_ref, own_ref, near_ref, far_ref, bias_ref, gain_ref, shift_ref,
    norm_ref, q_ref, k_ref, fresh_ref, other_ref, out_ref,
):
    half = q_ref.shape[1] // 2
    fresh = half // 2
    split = other_ref.shape[0] // 2

    @pl.when(pl.program_id(0) == 0)
    def _():
        first = ids[CORE] == 0
        near, far = near_ref[...], far_ref[...]
        low, high = jnp.where(first, near, far), jnp.where(first, far, near)
        other_ref[:split, :] = low[:split]
        other_ref[split:, :] = high[:split]
        out_ref[:half // 2, :] = low[split:]
        out_ref[half // 2:, :] = high[split:]

    scaled, _ = normed(x_ref[...].astype(F32))
    rows = (scaled * vector(gain_ref) + vector(shift_ref)).astype(BF16)
    norm_ref[...] = rows
    for side, weight in enumerate((own_ref, other_ref)):
        made = nn(rows, weight[:2 * half, :])
        value = nt(rows, weight[2 * half:, :])
        columns = slice(side * half, (side + 1) * half)
        q_ref[:, columns] = (made[:, :half] + bias_ref[side:side + 1, :half]).astype(BF16)
        k_ref[:, columns] = made[:, half:].astype(BF16)
        fresh_ref[side] = (value + bias_ref[side:side + 1, half:half + fresh]).astype(BF16)


def unpacked(value):
    return jnp.concatenate(
        [value[:, start:start + BLOCK] for start in range(0, value.shape[1], BLOCK)], axis=0
    ).T


def packed_rows(value):
    return jnp.concatenate(
        [value[start:start + HEAD] for start in range(0, value.shape[0], HEAD)], axis=1
    )


def doc_start(position, bounds):
    start = jnp.zeros_like(position)
    for bound in bounds:
        start = jnp.where(position >= bound, bound, start)
    return start


def attend_kernel(
    ids, x_ref, q_ref, k_ref, fresh_ref, skip_own_ref, skip_other_ref, own_ref, other_ref,
    bias_ref, gain_ref, shift_ref, v_ref, att_ref, lse_ref, middle_ref, norm_ref, att_s, lse_s,
):
    p = pl.program_id(0)
    bounds = doc_bounds(ids)
    skip_own, skip_other = unpacked(skip_own_ref[...]), unpacked(skip_other_ref[...])
    v_ref[pl.ds(pl.multiple_of(p * BLOCK, BLOCK), BLOCK), :] = jnp.concatenate(
        [fresh_ref[0], skip_own, fresh_ref[1], skip_other], axis=1
    )
    width = q_ref.shape[1]
    half = width // 2
    first = doc_start(p * BLOCK, bounds)
    needed = p - first // BLOCK + 1
    lane = lax.broadcasted_iota(jnp.int32, (1, PAIR), 1)
    low = lane < HEAD
    picks = [jnp.where(low, SCALE, 0.0).astype(BF16), jnp.where(low, 0.0, SCALE).astype(BF16)]

    def run(count):
        span = count * BLOCK
        base = pl.multiple_of((p - count + 1) * BLOCK, BLOCK)
        row = p * BLOCK + lax.broadcasted_iota(jnp.int32, (BLOCK, 1), 0)
        start = doc_start(row, bounds)
        column = base + lax.broadcasted_iota(jnp.int32, (1, span), 1)
        seen = (column <= row) & (column >= start)
        bias = jnp.where(seen, 0.0, MASKED)
        head_lane = lax.broadcasted_iota(jnp.int32, (1, 128), 1)

        @pl.loop(0, width // PAIR, unroll=3)
        def _(pair):
            lanes = pl.ds(pl.multiple_of(pair * PAIR, PAIR), PAIR)
            queries = q_ref[:, lanes]
            keys = k_ref[pl.ds(base, span), lanes]
            values = v_ref[pl.ds(base, span), lanes]
            outs = []
            for side in range(2):
                scores = nt(queries * picks[side], keys) + bias
                top = jnp.max(scores, axis=1, keepdims=True)
                probs = jnp.exp(scores - top)
                total = jnp.sum(probs, axis=1, keepdims=True)
                outs.append(nn(probs.astype(BF16), values) / total)
                lse_s[...] = jnp.where(
                    head_lane == 2 * pair + side, top + jnp.log(total), lse_s[...]
                )
            att_s[:, lanes] = jnp.where(low, outs[0], outs[1]).astype(BF16)

    for count in range(1, REACH + 1):
        pl.when(needed == count)(partial(run, count))

    lse_ref[...] = lse_s[...].T[:lse_ref.shape[0], :]
    attended = att_s[...]
    att_ref[...] = attended
    middle = (
        x_ref[...].astype(F32)
        + nn(attended[:, :half], own_ref[...])
        + nn(attended[:, half:], other_ref[...])
        + vector(bias_ref)
    )
    middle_ref[...] = middle
    scaled, _ = normed(middle)
    norm_ref[...] = (scaled * vector(gain_ref) + vector(shift_ref)).astype(BF16)


def feed_kernel(fetched, has_sums, has_grads, swapped, ids, *refs):
    norm_ref, grad_ref = refs[:2]
    if fetched:
        mine_ref, theirs_ref, down_ref, bias_ref = refs[2:6]
        refs = refs[6:]
        first = ids[OUTER] % 2 == 0
        mine, theirs = mine_ref[...], theirs_ref[...]
        up = jnp.concatenate(
            [jnp.where(first, mine, theirs), jnp.where(first, theirs, mine)], axis=0
        )
        down = down_ref[...]
    else:
        weight_ref, bias_ref = refs[2:4]
        refs = refs[4:]
        up = weight_ref[:weight_ref.shape[0] // 2, :]
        down = weight_ref[weight_ref.shape[0] // 2:, :]
    units = up.shape[0]
    if has_sums:
        out_in, back_in = refs[:2]
        refs = refs[2:]
    if has_grads:
        made_in = refs[0]
        refs = refs[1:]
    out_ref, back_ref, gb_ref = refs[:3]
    made_refs = refs[3:]
    rows = norm_ref[...]
    grads = grad_ref[...]
    hidden = nt(rows, up) + bias_ref[...]
    square = hidden * hidden
    curve = jnp.tanh(hidden * (GELU_A + GELU_A * GELU_B * square))
    plus = 0.5 + 0.5 * curve
    value = hidden * plus
    active = value.astype(BF16)
    slope = plus + value * (1.0 - curve) * (GELU_A + 3.0 * GELU_A * GELU_B * square)
    hidden_grad = nt(grads, down) * slope
    gb_ref[...] = jnp.sum(hidden_grad, axis=0, keepdims=True)
    hidden_low = hidden_grad.astype(BF16)
    out = nn(active, down)
    back = nn(hidden_low, up)
    if has_sums:
        out = out + out_in[...].astype(F32)
        back = back + back_in[...].astype(F32)
    out_ref[...] = out.astype(BF16)
    back_ref[...] = back.astype(BF16)
    for piece, left, right in (
        (slice(0, units), hidden_low, rows), (slice(units, 2 * units), active, grads)
    ):
        made = tn(left, right)
        if has_grads:
            made = made + made_in[piece, :].astype(F32)
        made = made.astype(BF16)
        count = made_refs[0].shape[0]
        for row in range(piece.start, piece.stop, count):
            part = made_refs[row // count]
            if count > units:
                part[piece, :] = made
            elif swapped and piece.start > 0:
                near = made[row - piece.start:row - piece.start + count]
                far = made[units - count - row + piece.start:units - row + piece.start]
                part[...] = jnp.where(ids[OUTER] % 2 == 0, near, far)
            else:
                part[...] = made[row - piece.start:row - piece.start + count]


def feed(ids, rows, grads, weights, bias, sums=(), made=(), parts=1,
         swapped=False):
    tokens, width = rows.shape
    units = bias.shape[1]
    total = full((tokens, width))
    return call(
        partial(feed_kernel, len(weights) > 1, len(sums) > 0, len(made) > 0, swapped),
        1,
        (1,),
        [total, total] + [full(weight.shape) for weight in weights] + [full((1, units))]
        + [total] * len(sums) + [full((2 * units, width))] * len(made),
        [total, total, full((1, units))] + [full((2 * units // parts, width))] * parts,
        [
            shape_of((tokens, width), BF16), shape_of((tokens, width), BF16),
            shape_of((1, units), F32),
        ] + [shape_of((2 * units // parts, width), BF16)] * parts,
        micros=14,
        name="feed",
    )(ids, rows, grads, *weights, bias, *sums, *made)


def residual_kernel(
    ids, out_a, out_b, back_a, back_b, grad_ref, middle_ref, att_ref, own_ref, other_ref,
    gain_ref, down_bias_ref, layer_ref, mg_ref, ga_ref, keep_ref, send_ref, small_ref, acc_s,
):
    p = pl.program_id(0)
    half = own_ref.shape[0]
    middle = middle_ref[...]
    summed = lambda refs: sum(ref[...].astype(F32) for ref in refs)
    layer_ref[...] = (middle + summed((out_a, out_b)) + vector(down_bias_ref)).astype(BF16)
    scaled, inverse = normed(middle)
    second = summed((back_a, back_b))
    out_grad = grad_ref[...].astype(F32)
    middle_grad = out_grad + norm_back(second, scaled, inverse, vector(gain_ref))
    mg_ref[...] = middle_grad
    low = middle_grad.astype(BF16)
    ga_ref[:, :half] = nt(low, own_ref[...]).astype(BF16)
    ga_ref[:, half:] = nt(low, other_ref[...]).astype(BF16)
    weight_grad = tn(att_ref[...], low)
    sums = jnp.concatenate(
        [
            jnp.sum(value, axis=0, keepdims=True)
            for value in (second * scaled, second, middle_grad, out_grad)
        ],
        axis=0,
    )

    @pl.when(p == 0)
    def _():
        acc_s[...] = weight_grad
        small_ref[...] = sums

    @pl.when(p > 0)
    def _():
        acc_s[...] += weight_grad
        small_ref[...] += sums

    @pl.when(p == pl.num_programs(0) - 1)
    def _():
        rows = half // 2
        near = pl.multiple_of(ids[CORE] * rows, 32)
        far = pl.multiple_of(rows - ids[CORE] * rows, 32)
        for side in range(2):
            keep_ref[side] = acc_s[pl.ds(side * half + near, rows), :].astype(BF16)
            send_ref[side] = acc_s[pl.ds(side * half + far, rows), :].astype(BF16)


def attend_back_kernel(
    head_base, ids, q_ref, k_ref, v_ref, att_ref, ga_ref, lse_ref,
    made_ref, skip_ref, dq_s, dk_s, dv_s, delta_s,
):
    p = pl.program_id(0)
    width = q_ref.shape[1]
    fresh = width // 2
    bounds = doc_bounds(ids)
    place = member_at(p, ids)
    first = doc_start(p * BLOCK, bounds)
    needed = p - first // BLOCK + 1
    low = lax.broadcasted_iota(jnp.int32, (1, PAIR), 1) < HEAD
    picks = [jnp.where(low, SCALE, 0.0).astype(BF16), jnp.where(low, 0.0, SCALE).astype(BF16)]
    ones = [jnp.where(low, 1.0, 0.0).astype(BF16), jnp.where(low, 0.0, 1.0).astype(BF16)]

    @pl.when(p == 0)
    def _():
        dk_s[...] = jnp.zeros_like(dk_s)
        dv_s[...] = jnp.zeros_like(dv_s)

    product = ga_ref[...].astype(F32) * att_ref[...].astype(F32)
    high = product.astype(BF16)
    rest = (product - high.astype(F32)).astype(BF16)
    owner = lax.broadcasted_iota(jnp.int32, (delta_s.shape[0], width), 1) // HEAD
    which = lax.broadcasted_iota(jnp.int32, (delta_s.shape[0], width), 0)
    gather = (owner == which).astype(F32).astype(BF16)
    delta_s[...] = nt(gather, high) + nt(gather, rest)

    def run(count):
        span = count * BLOCK
        base = pl.multiple_of((p - count + 1) * BLOCK, BLOCK)
        row = p * BLOCK + lax.broadcasted_iota(jnp.int32, (1, BLOCK), 1)
        start = doc_start(row, bounds)
        column = base + lax.broadcasted_iota(jnp.int32, (span, 1), 0)
        seen = (column <= row) & (column >= start)
        bias = jnp.where(seen, 0.0, MASKED)

        @pl.loop(0, width // PAIR, unroll=3)
        def _(pair):
            lanes = pl.ds(pl.multiple_of(pair * PAIR, PAIR), PAIR)
            queries = q_ref[:, lanes]
            grads = ga_ref[:, lanes]
            keys = k_ref[pl.ds(base, span), lanes]
            values = v_ref[pl.ds(base, span), lanes]
            query_parts = []
            for side in range(2):
                head = 2 * pair + side
                picked = queries * picks[side]
                chosen = grads * ones[side]
                scores = nt(keys, picked) + bias
                probs = jnp.exp(scores - lse_ref[pl.ds(head_base + head, 1), :])
                dprobs = nt(values, chosen)
                dscores = (probs * (dprobs - delta_s[pl.ds(head, 1), :])).astype(BF16)
                value_part = nn(probs.astype(BF16), chosen)
                key_part = nn(dscores, picked)
                query_parts.append(tn(dscores, keys))
                if side == 0:
                    value_sum, key_sum = value_part, key_part
                else:
                    value_sum, key_sum = value_sum + value_part, key_sum + key_part
            dv_s[pl.ds(base, span), lanes] += value_sum
            dk_s[pl.ds(base, span), lanes] += key_sum
            dq_s[:, lanes] = (
                jnp.where(low, query_parts[0], query_parts[1]) * SCALE
            ).astype(BF16)

    for count in range(1, REACH + 1):
        pl.when(needed == count)(partial(run, count))

    made_ref[place, :, :width] = dq_s[...]

    @pl.when(p == pl.num_programs(0) - 1)
    def _():
        for block in range(SPAN):
            rows = slice(block * BLOCK, (block + 1) * BLOCK)
            to = member_at(block, ids)
            made_ref[to, :, width:2 * width] = dk_s[rows, :].astype(BF16)
            value_grad = dv_s[rows, :]
            made_ref[to, :, 2 * width:] = value_grad[:, :fresh].astype(BF16)
            skip_ref[to] = packed_rows(value_grad.T[fresh:, :].astype(BF16))


def weight_kernel(ids, norm_ref, made_ref, keep_ref, send_ref, sums_ref, made_s):
    rows = norm_ref[...]
    grads = made_ref[...]
    width = rows.shape[1]
    made_s[:width, :] = tn(rows, grads[:, :width])
    made_s[width:, :] = tn(grads[:, width:], rows)
    half = made_s.shape[0] // 2
    near = pl.multiple_of(ids[CORE] * half, 32)
    far = pl.multiple_of(half - ids[CORE] * half, 32)
    for target, start in ((keep_ref, near), (send_ref, far)):
        target[...] = made_s[pl.ds(start, half), :].astype(BF16)
    sums_ref[...] = jnp.sum(grads.astype(F32), axis=0, keepdims=True)


def input_kernel(
    ids, own_ref, other_ref, w_own_ref, w_other_ref, x_ref, mg_ref, skip_own_ref, skip_other_ref,
    gain_ref, *refs
):
    grad_refs, small_ref = refs[:-1], refs[-1]
    p = pl.program_id(0)
    first = None
    for made_ref, weight in ((own_ref, w_own_ref), (other_ref, w_other_ref)):
        width = weight.shape[1]
        part = nt(made_ref[:, :width], weight[:width, :]) + nn(made_ref[:, width:], weight[width:, :])
        first = part if first is None else first + part
    scaled, inverse = normed(x_ref[...].astype(F32))
    tokens, each = x_ref.shape[0], skip_own_ref.shape[0]
    made = (mg_ref[...] + norm_back(first, scaled, inverse, vector(gain_ref))).astype(BF16)
    for distance, grad_ref in enumerate(grad_refs):

        @pl.when(p == distance)
        def _():
            grad_ref[:tokens, :] = made
            grad_ref[tokens:tokens + each, :] = skip_own_ref[...]
            grad_ref[tokens + each:, :] = skip_other_ref[...]
    sums = jnp.concatenate(
        [jnp.sum(value, axis=0, keepdims=True) for value in (first * scaled, first)], axis=0
    )

    @pl.when(p == 0)
    def _():
        small_ref[...] = sums

    @pl.when(p > 0)
    def _():
        small_ref[...] += sums


def fold_kernel(groups, starts, ids, *refs):
    sources = sum(len(group) for group in groups)
    outs = refs[sources:-1]
    total_s = refs[-1]
    row = 0
    place = 0
    for group in groups:
        total = None
        for index in group:
            ref = refs[place]
            place += 1
            if isinstance(index, str):
                value = ref[...].astype(F32)
                value = jnp.where(ids[OUTER] % 2 == int(index), value, jnp.zeros_like(value))
            else:
                value = (ref[...] if index is None else ref[index]).astype(F32)
            total = value if total is None else total + value
        total_s[row:row + total.shape[0], :] = total
        row += total.shape[0]
    if row < total_s.shape[0]:
        total_s[row:, :] = jnp.zeros((total_s.shape[0] - row, total_s.shape[1]), F32)
    for out, start in zip(outs, starts):
        at = start(ids)
        if not isinstance(at, int):
            at = pl.multiple_of(at, 8)
        out[...] = total_s[pl.ds(at, out.shape[0]), :].astype(BF16)


def fold(ids, groups, starts, count, rows=0):
    arrays = [entry[0] for group in groups for entry in group]
    indices = tuple(tuple(entry[1] for entry in group) for group in groups)
    width = arrays[0].shape[-1]
    rows = max(rows, sum(group[0][0].shape[-2] for group in groups))
    return call(
        partial(fold_kernel, indices, starts),
        1,
        (1,),
        [full(array.shape) for array in arrays],
        [full((count, width)) for _ in starts],
        [shape_of((count, width), BF16) for _ in starts],
        scratch=[pltpu.VMEM((rows, width), F32)],
        micros=3.5,
        name="fold",
    )(ids, *arrays)


def spread_sum_kernel(ids, parts_ref, spread_ref):
    total = jnp.sum(parts_ref[...].astype(F32), axis=0).astype(BF16)
    for index in range(parts_ref.shape[0]):
        spread_ref[index] = total


def spread_sum(ids, parts):
    return call(
        spread_sum_kernel,
        1,
        (1,),
        [full(parts.shape)],
        [full(parts.shape)],
        [shape_of(parts.shape, BF16)],
        micros=2.5,
        name="spread_sum",
    )(ids, parts)[0]


def collect_kernel(ids, *refs):
    grad_ref, skip_ref = refs[-2:]
    for distance, ref in enumerate(refs[:-2]):
        place = ids[MINE] ^ distance
        grad_ref[place] = ref[:BLOCK, :].astype(F32)
        for side in range(2):
            rows = ref[BLOCK + side * HEAD:BLOCK + (side + 1) * HEAD, :].astype(F32)
            column = ((ids[TP] ^ side) * SPAN + place) * BLOCK
            columns = pl.ds(pl.multiple_of(column, BLOCK), BLOCK)
            for index in range(rows.shape[1] // BLOCK):
                skip_ref[index * HEAD:(index + 1) * HEAD, columns] = rows[
                    :, index * BLOCK:(index + 1) * BLOCK
                ]


def collect(ids, pieces):
    rows, width = pieces[0].shape
    features = width // BLOCK * HEAD
    return call(
        collect_kernel,
        1,
        (1,),
        [full((rows, width))] * len(pieces),
        [full((SPAN, BLOCK, width)), full((features, 2 * SPAN * BLOCK))],
        [shape_of((SPAN, BLOCK, width), F32), shape_of((features, 2 * SPAN * BLOCK), F32)],
        micros=5,
        name="collect",
    )(ids, *pieces)


def place_feed_kernel(ids, mine_ref, theirs_ref, up_ref, down_ref):
    units = down_ref.shape[0]
    here = pl.program_id(0) == ids[CORE]
    whole = jnp.where(here, mine_ref[...], theirs_ref[...]).astype(F32)
    up_ref[...] = whole[:units].T
    down_ref[...] = whole[units:]


def place_feed(ids, mine, theirs):
    rows, width = mine.shape
    return call(
        place_feed_kernel,
        1,
        (2,),
        [full((rows, width))] * 2,
        [
            pl.BlockSpec((width, rows // 2), lambda h, ids: (0, h)),
            pl.BlockSpec((rows // 2, width), lambda h, ids: (h, 0)),
        ],
        [shape_of((width, rows), F32), shape_of((rows, width), F32)],
        micros=8,
        name="place_feed",
    )(ids, mine, theirs)


def place_qkv_kernel(ids, mine_ref, theirs_ref, q_ref, k_ref, v_ref, out_ref):
    half = q_ref.shape[1]
    split = (q_ref.shape[0] + v_ref.shape[0]) // 2
    half_out = out_ref.shape[0] // 2
    first = ids[CORE] == 0
    mine, theirs = mine_ref[...], theirs_ref[...]
    low = jnp.where(first, mine, theirs).astype(F32)
    high = jnp.where(first, theirs, mine).astype(F32)
    out_ref[:half_out, :] = low[split:split + half_out]
    out_ref[half_out:, :] = high[split:split + half_out]
    rest = q_ref.shape[0] - split
    for ref, columns in ((q_ref, slice(0, half)), (k_ref, slice(half, 2 * half))):
        ref[:split, :] = low[:split, columns]
        ref[split:, :] = high[:rest, columns]
    v_ref[...] = high[rest:split]


def place_qkv(ids, mine, theirs, half, fresh):
    rows, width = mine.shape
    return call(
        place_qkv_kernel,
        1,
        (1,),
        [full((rows, width))] * 2,
        [full((width, half)), full((width, half)), full((fresh, width)), full((half, width))],
        [
            shape_of((width, half), F32), shape_of((width, half), F32),
            shape_of((fresh, width), F32), shape_of((half, width), F32),
        ],
        micros=4,
        name="place_qkv",
    )(ids, mine, theirs)


def tie(value, *others):
    return lax.optimization_barrier((value,) + others)[0]


def per_device(
    sizes,
    layer_in,
    skip_values,
    block_slot,
    doc_lengths,
    gain_attention,
    shift_attention,
    query_weight,
    query_bias,
    key_weight,
    value_weight,
    value_bias,
    out_weight,
    out_bias,
    gain_feed,
    shift_feed,
    up_weight,
    up_bias,
    down_weight,
    down_bias,
    out_grad,
):
    seq_count, tp_count = sizes
    width = layer_in.shape[1]
    half = query_weight.shape[1]
    fresh = value_weight.shape[1]
    units = up_weight.shape[1]
    tokens = layer_in.shape[0]
    batch = skip_values.shape[0] // BLOCK
    heads = width // HEAD
    head_rows = -(-heads // 8) * 8
    packed = 2 * half + fresh
    side = units // 2
    seq_index = lax.axis_index("seq")
    tp_index = lax.axis_index("tp")
    member = seq_index % SPAN
    group = seq_index // SPAN
    core = seq_index % 2
    members = [[g * SPAN + m for m in range(SPAN)] for g in range(seq_count // SPAN)]
    same_core = [list(range(c, seq_count, 2)) for c in range(2)]
    others = seq_count // 2
    local_seq = tp_index * (batch // tp_count) + member

    def swap_seq(value, distance):
        return lax.ppermute(value, "seq", [(i, i ^ distance) for i in range(seq_count)])

    def swap_core(value):
        return swap_seq(value, 1)

    def swap_tp(value):
        return lax.ppermute(value, "tp", [(i, i ^ 1) for i in range(tp_count)])

    def to_seqs(value):
        return lax.all_to_all(value, "seq", 0, 0, tiled=True, axis_index_groups=members)

    def either(bit, first, second):
        return jnp.where(bit == 0, first, second)

    def in_order(bit, mine, theirs):
        return either(
            bit, jnp.concatenate([mine, theirs], 0), jnp.concatenate([theirs, mine], 0)
        )

    def rows_of(value, start, count):
        return lax.dynamic_slice_in_dim(value, start, count, 0)

    def row(value):
        return value.reshape(1, -1)

    local_seq = tp_index * (batch // tp_count) + member
    slots = lax.dynamic_slice(block_slot, (group * SPAN, local_seq), (SPAN, 1))
    holders = jnp.sum(
        jnp.where(
            slots == lax.broadcasted_iota(jnp.int32, (SPAN, SPAN), 1),
            lax.broadcasted_iota(jnp.int32, (SPAN, SPAN), 0), 0,
        ),
        axis=0,
    )
    lengths = lax.dynamic_slice(doc_lengths, (group * batch + local_seq, 0), (1, DOCS))
    ends = jnp.sum(
        jnp.where(
            lax.broadcasted_iota(jnp.int32, (DOCS, DOCS), 0)
            <= lax.broadcasted_iota(jnp.int32, (DOCS, DOCS), 1),
            lengths.reshape(DOCS, 1), 0,
        ),
        axis=0,
    )
    ids = jnp.concatenate(
        [
            jnp.stack([core, member, group, tp_index]).astype(jnp.int32), holders,
            ends[:DOCS - 1],
        ]
    ).astype(jnp.int32)

    qkv_own = jnp.concatenate(
        [jnp.concatenate([query_weight, key_weight], axis=1), value_weight.T], axis=0
    )
    early_sent = jnp.concatenate(
        [
            rows_of(qkv_own, core * (packed // 2), packed // 2),
            rows_of(out_weight, core * (half // 2), half // 2),
        ],
        0,
    )
    early_near = swap_tp(early_sent)
    layer_in, skip_values = lax.optimization_barrier((layer_in, skip_values, early_sent))[:2]
    thirds = fresh // HEAD
    skip_sent = skip_values.T.reshape(thirds, HEAD, tp_count, SPAN, BLOCK)
    skip_sent = skip_sent.transpose(3, 2, 1, 0, 4).reshape(SPAN, tp_count * HEAD, thirds * BLOCK)
    blocks_in = to_seqs(
        jnp.concatenate([layer_in.reshape(SPAN, BLOCK, width), skip_sent], axis=1)
    )
    skip_other = swap_tp(
        lax.dynamic_slice(
            blocks_in, (0, BLOCK + (1 - tp_index) * HEAD, 0), (SPAN, HEAD, width)
        )
    )
    up_bias_half = rows_of(up_bias, core * side, side)
    bias_own = jnp.concatenate([query_bias, value_bias, up_bias_half])
    bias_other = swap_tp(bias_own)
    feed_own = jnp.concatenate(
        [lax.dynamic_slice_in_dim(up_weight, core * side, side, 1).T,
         rows_of(down_weight, core * side, side)], 0,
    )
    feed_own, ids = lax.optimization_barrier((feed_own, ids))
    early_near, bias_other = lax.optimization_barrier((early_near, bias_other, feed_own))[:2]
    early_far = swap_core(early_near)
    up_part = rows_of(feed_own, group % 2 * (side // 2), side // 2)
    up_near = swap_tp(tie(up_part, early_near))

    qkv_bias = jnp.stack([bias_own[:half + fresh], bias_other[:half + fresh]])
    own_shape = (SPAN, BLOCK, width)
    flat = (tokens, width)

    norm_one, queries, keys, fresh_values, qkv_other, out_other = call(
        project_kernel,
        1,
        (SPAN,),
        [
            placed(width), full((packed, width)), full((packed // 2 + half // 2, width)),
            full((packed // 2 + half // 2, width)), full((2, half + fresh)), full((width,)), full((width,)),
        ],
        [
            placed(width), in_rows(width), in_rows(width),
            pl.BlockSpec((2, BLOCK, fresh), lambda p, *_: (0, p, 0)), full((packed, width)),
            full((half, width)),
        ],
        [
            shape_of(own_shape, BF16), shape_of(flat, BF16), shape_of(flat, BF16),
            shape_of((2, tokens, fresh), BF16), shape_of((packed, width), BF16),
            shape_of((half, width), BF16),
        ],
        micros=9,
        name="project",
    )(ids, blocks_in, qkv_own, early_near, early_far, qkv_bias, gain_attention, shift_attention)

    grad_blocks = to_seqs(tie(out_grad.reshape(SPAN, BLOCK, width), queries))
    up_near = tie(up_near, queries)
    up_far = swap_seq(up_near, SPAN)
    down_other = swap_tp(tie(feed_own[side:], queries))
    lse_spec = pl.BlockSpec((head_rows, BLOCK), lambda p, *_: (0, p))
    values, attended, log_total, middle, norm_two = call(
        attend_kernel,
        1,
        (SPAN,),
        [
            placed(width), in_rows(width), full(flat),
            pl.BlockSpec((2, BLOCK, fresh), lambda p, *_: (0, p, 0)),
            pl.BlockSpec(
                (None, HEAD, width),
                lambda p, ids: (member_at(p, ids), BLOCK // HEAD + ids[TP], 0),
            ),
            placed(width, HEAD),
            full((half, width)), full((half, width)), full((width,)), full((width,)),
            full((width,)),
        ],
        [full(flat), placed(width), lse_spec, placed(width), placed(width)],
        [
            shape_of(flat, BF16), shape_of(own_shape, BF16), shape_of((head_rows, tokens), F32),
            shape_of(own_shape, F32), shape_of(own_shape, BF16),
        ],
        scratch=[pltpu.VMEM((BLOCK, width), BF16), pltpu.VMEM((BLOCK, 128), F32)],
        micros=27,
        name="attend",
    )(
        ids, blocks_in, queries, keys, fresh_values, blocks_in, skip_other, out_weight,
        out_other,        out_bias, gain_feed, shift_feed,
    )
    rows_mine = norm_two.reshape(flat)
    grads_mine = grad_blocks.reshape(flat)

    rows_theirs = swap_core(rows_mine)
    grads_theirs = swap_core(grads_mine)
    feed_other = (up_near, up_far, down_other)
    bias_here = row(up_bias_half)
    bias_there = row(bias_other[half + fresh:])
    out_mine, back_mine, bias_one, made_other = feed(
        ids, rows_mine, grads_mine, feed_other, bias_there
    )
    rows_theirs = tie(rows_theirs, out_mine)
    out_theirs, back_theirs, bias_two, *made_other = feed(
        ids, rows_theirs, grads_theirs, feed_other, bias_there, (), (made_other,), PARTS, True
    )
    cross_one = swap_tp(made_other[0])
    given = swap_seq(made_other[3], SPAN)
    out_theirs, back_theirs, bias_three, made_own = feed(
        ids, rows_theirs, grads_theirs, (feed_own,), tie(bias_here, made_other[0]),
        (out_theirs, back_theirs),
    )
    out_given = swap_core(out_theirs)
    back_given = swap_core(back_theirs)
    cross_two = swap_tp(tie(made_other[1], cross_one, out_theirs))
    given, kept = lax.optimization_barrier((given, made_other[2], out_theirs))[:2]
    pair_sum, = fold(ids, [[(kept, None), (given, None)]], [lambda ids: 0], kept.shape[0])
    out_mine, back_mine, bias_four, *made_own = feed(
        ids, rows_mine, grads_mine, (feed_own,), tie(bias_here, cross_one, pair_sum),
        (out_mine, back_mine), (made_own,), PARTS,
    )
    cross_three = swap_tp(tie(pair_sum, cross_two, out_mine))

    def scatter(value):
        parts = value.reshape(others, value.shape[0] // others, width)
        return lax.all_to_all(parts, "seq", 0, 0, tiled=True, axis_index_groups=same_core)

    def gather(parts):
        spread = spread_sum(ids, parts)
        whole = lax.all_to_all(spread, "seq", 0, 0, tiled=True, axis_index_groups=same_core)
        return whole.reshape(-1, width)

    layer_blocks, middle_grad, att_grad, out_keep, out_send, small_two = call(
        residual_kernel,
        1,
        (SPAN,),
        [in_rows(width)] * 5
        + [
            by_block(width), by_block(width), full((half, width)), full((half, width)),
            full((width,)), full((width,)),
        ],
        [
            by_block(width), by_block(width), by_block(width),
            full((2, half // 2, width)), full((2, half // 2, width)), full((4, width)),
        ],
        [
            shape_of(own_shape, BF16), shape_of(own_shape, F32), shape_of(own_shape, BF16),
            shape_of((2, half // 2, width), BF16), shape_of((2, half // 2, width), BF16),
            shape_of((4, width), F32),
        ],
        scratch=[pltpu.VMEM((width, width), F32)],
        micros=12.5,
        name="residual",
    )(
        ids, tie(out_mine, cross_two), out_given, back_mine, back_given, grads_mine, middle, attended, out_weight,
        out_other, gain_feed, down_bias,
    )
    sent_given = swap_core(out_send)
    out_total = (out_keep.astype(F32) + sent_given.astype(F32)).astype(BF16)
    cross_three = tie(cross_three, att_grad)
    ready_feed, = fold(
        ids,
        [
            [(made_own[0], None), (cross_one, None)],
            [(made_own[1], None), (cross_two, None)],
            [(made_own[2], None), (cross_three, "0")],
            [(made_own[3], None), (cross_three, "1")],
        ],
        [lambda ids: 0],
        2 * side,
    )
    total_feed = lax.psum(ready_feed, "seq", axis_index_groups=same_core)
    def rest():
        cross_out = swap_tp(out_total[1])

        def attend_back(which, query_rows):
            return call(
                partial(attend_back_kernel, which * (heads // 2)),
                1,
                (SPAN,),
                [
                    pl.BlockSpec((BLOCK, half), lambda p, *_: (p, which)),
                    pl.BlockSpec((tokens, half), lambda p, *_: (0, which)),
                    pl.BlockSpec((tokens, half), lambda p, *_: (0, which)),
                    placed(half, column=which), placed(half, column=which), lse_spec,
                ],
                [full((SPAN, BLOCK, packed)), full((SPAN, HEAD, width))],
                [shape_of((SPAN, BLOCK, packed), BF16), shape_of((SPAN, HEAD, width), BF16)],
                scratch=[
                    pltpu.VMEM((BLOCK, half), BF16), pltpu.VMEM((tokens, half), F32),
                    pltpu.VMEM((tokens, half), F32), pltpu.VMEM((8, BLOCK), F32),
                ],
                micros=17.5,
                name="attend_back",
            )(
                ids, query_rows, keys, values, attended, att_grad,
                log_total,
            )

        qkv_rows = packed // 2
        last_rows = -(-(qkv_rows + half // 2) // 64) * 64

        def weights(made):
            return call(
                weight_kernel,
                1,
                (1,),
                [full(flat), full((tokens, packed))],
                [full((qkv_rows, width)), full((qkv_rows, width)), full((1, packed))],
                [
                    shape_of((qkv_rows, width), BF16), shape_of((qkv_rows, width), BF16),
                    shape_of((1, packed), F32),
                ],
                scratch=[pltpu.VMEM((packed, width), F32)],
                micros=6,
                name="weights",
            )(ids, norm_one.reshape(flat), made.reshape(tokens, packed))

        layer_out = to_seqs(layer_blocks).reshape(flat)
        grads_other, skip_made = attend_back(1, queries)
        keep_other, send_other, sums_other = weights(tie(grads_other, cross_out))
        given_other = swap_core(send_other)
        total_other, = fold(
            ids, [[(keep_other, None), (given_other, None)]], [lambda ids: 0], qkv_rows
        )
        cross_other = swap_tp(total_other)
        grads_own, skip_own = attend_back(0, tie(queries, total_other, layer_out))
        skip_theirs = swap_tp(tie(skip_made, grads_own))
        keep_own, send_own, sums_own = weights(tie(grads_own, cross_other))
        given_own = swap_core(send_own)

        ready_qkv, = fold(
            ids,
            [
                [(keep_own, None), (given_own, None), (cross_other, None)],
                [(out_total, 0), (cross_out, None)],
            ],
            [lambda ids: 0],
            last_rows,
            last_rows,
        )
        parts_qkv = scatter(ready_qkv)
        def by_distance(columns, rows=BLOCK):
            return pl.BlockSpec((None, rows, columns), lambda p, ids: (ids[MINE] ^ p, 0, 0))

        *input_blocks, small_one = call(
            input_kernel,
            1,
            (SPAN,),
            [
                by_distance(packed), by_distance(packed), full((packed, width)),
                full((packed, width)), by_distance(width), by_distance(width),
                by_distance(width, HEAD), by_distance(width, HEAD), full((width,)),
            ],
            [full((BLOCK + 2 * HEAD, width))] * SPAN + [full((2, width))],
            [shape_of((BLOCK + 2 * HEAD, width), BF16)] * SPAN + [shape_of((2, width), F32)],
            micros=9,
            name="input",
        )(
            ids, tie(grads_own, ready_qkv), grads_other, qkv_own, qkv_other, blocks_in, middle_grad,
            skip_own, skip_theirs, gain_attention,
        )
        back = [input_blocks[0]] + [
            swap_seq(input_blocks[distance], distance) for distance in range(1, SPAN)
        ]
        shared = jnp.concatenate([small_one.reshape(-1), small_two.reshape(-1)])
        widened = lambda value: jnp.where(
            lax.broadcasted_iota(jnp.int32, (2, 1), 0) == core, value, 0.0
        ).reshape(-1)
        split_own = jnp.concatenate([sums_own.reshape(-1), widened(bias_three + bias_four)])
        split_other = jnp.concatenate([sums_other.reshape(-1), widened(bias_one + bias_two)])
        vector_own = jnp.concatenate([shared, split_own])
        vector_other = jnp.concatenate([shared, split_other])

        vectors = vector_own + swap_tp(vector_other)
        for distance in [1] + [SPAN << bit for bit in range((seq_count // SPAN).bit_length() - 1)]:
            vectors = vectors + swap_seq(vectors, distance)
        parts_qkv, *back = lax.optimization_barrier((parts_qkv, vectors, *back))
        vectors = back.pop(0)
        return (layer_out, parts_qkv, vectors, *back)

    shapes = jax.eval_shape(rest)
    results = lax.cond(
        jnp.min(lengths) > 0, rest, lambda: tuple(jnp.zeros(s.shape, s.dtype) for s in shapes)
    )
    layer_out, parts_qkv, vectors, *back = results
    late = ids + (vectors[0] * 0.0).astype(jnp.int32)
    whole_qkv = gather(parts_qkv)
    total_feed = tie(total_feed, late)
    far_feed = swap_core(total_feed)
    input_grad, skip_grad = collect(ids, back)
    input_grad, skip_grad = input_grad.reshape(flat), skip_grad.T
    vectors = vectors + swap_seq(vectors, 2)
    grad_up_weight, grad_down_weight = place_feed(late, total_feed, far_feed)
    whole_qkv, vectors = lax.optimization_barrier(
        (whole_qkv, vectors, grad_up_weight, input_grad, skip_grad)
    )[:2]
    grad_query, grad_key, grad_value, grad_out_weight = place_qkv(
        ids, whole_qkv, swap_core(whole_qkv), half, fresh
    )
    shared = vectors[:6 * width].reshape(6, width)
    split = vectors[6 * width:]

    return (
        layer_out,
        input_grad,
        skip_grad,
        shared[0],
        shared[1],
        grad_query,
        split[:half],
        grad_key,
        grad_value.T,
        split[2 * half:packed],
        grad_out_weight,
        shared[4],
        shared[2],
        shared[3],
        grad_up_weight,
        split[packed:],
        grad_down_weight,
        shared[5],
    )


def solution(mesh):
    return jax.shard_map(
        partial(per_device, (mesh.shape["seq"], mesh.shape["tp"])),
        mesh=mesh,
        in_specs=(
            P(("seq", "tp"), None),
            P("seq", "tp"),
            P(),
            P(),
            P(),
            P(),
            P(None, "tp"),
            P("tp"),
            P(None, "tp"),
            P(None, "tp"),
            P("tp"),
            P("tp", None),
            P(),
            P(),
            P(),
            P(None, "tp"),
            P("tp"),
            P("tp", None),
            P(),
            P(("seq", "tp"), None),
        ),
        out_specs=(
            P(("seq", "tp"), None),
            P(("seq", "tp"), None),
            P("seq", "tp"),
            P(),
            P(),
            P(None, "tp"),
            P("tp"),
            P(None, "tp"),
            P(None, "tp"),
            P("tp"),
            P("tp", None),
            P(),
            P(),
            P(),
            P(None, "tp"),
            P("tp"),
            P("tp", None),
            P(),
        ),
        check_vma=False,
    )
```

```python
from functools import partial

import jax
import jax.numpy as jnp
from jax import lax
from jax.experimental import pallas as pl
from jax.experimental.pallas import tpu as pltpu
from jax.sharding import PartitionSpec as P

HEAD = 64
SEQ_LEN = 1024
BLOCK = 256
LONGEST = 512
SPAN = SEQ_LEN // BLOCK
REACH = -(-LONGEST // BLOCK) + 1
PAIR = 2 * HEAD
EPSILON = 1e-05
MASKED = -1e30
GELU_A = 0.7978845608028654
GELU_B = 0.044715
SCALE = HEAD ** (-0.5)
DOCS = 4
PARTS = 4
CORE, MINE, OUTER, TP, MEMBER = 0, 1, 2, 3, 4
BOUND = MEMBER + SPAN
PEAK = 1.15e9
VMEM = 56 * 1024 * 1024

F32 = jnp.float32
BF16 = jnp.bfloat16


def nn(left, right):
    return lax.dot_general(left, right, (((1,), (0,)), ((), ())), preferred_element_type=F32)


def nt(left, right):
    return lax.dot_general(left, right, (((1,), (1,)), ((), ())), preferred_element_type=F32)


def tn(left, right):
    return lax.dot_general(left, right, (((0,), (0,)), ((), ())), preferred_element_type=F32)


def vector(ref):
    return ref[...].reshape(1, -1)


def normed(rows):
    centred = rows - jnp.mean(rows, axis=-1, keepdims=True)
    inverse = lax.rsqrt(jnp.mean(centred * centred, axis=-1, keepdims=True) + EPSILON)
    return centred * inverse, inverse


def norm_back(grad_out, scaled, inverse, gain):
    grad_scaled = grad_out * gain
    first_mean = jnp.mean(grad_scaled, axis=-1, keepdims=True)
    second_mean = jnp.mean(grad_scaled * scaled, axis=-1, keepdims=True)
    return inverse * (grad_scaled - first_mean - scaled * second_mean)


def full(shape):
    return pl.BlockSpec(shape, lambda *_: (0,) * len(shape), pipeline_mode=pl.Buffered(1))


def member_at(p, ids):
    return ids[MEMBER + p]


def doc_bounds(ids):
    return [ids[BOUND + index] for index in range(DOCS - 1)]


def placed(columns, rows=BLOCK, column=0):
    return pl.BlockSpec(
        (None, rows, columns), lambda p, ids: (member_at(p, ids), 0, column)
    )


def in_rows(columns):
    return pl.BlockSpec((BLOCK, columns), lambda p, *_: (p, 0))


def by_block(columns):
    return pl.BlockSpec((None, BLOCK, columns), lambda p, *_: (p, 0, 0))


def shape_of(shape, dtype):
    return jax.ShapeDtypeStruct(shape, dtype)


def call(kernel, scalars, grid, ins, outs, out_shapes, scratch=(), micros=1, name=None,
         aliases=None):
    return pl.pallas_call(
        kernel,
        grid_spec=pltpu.PrefetchScalarGridSpec(
            num_scalar_prefetch=scalars,
            grid=grid,
            in_specs=ins,
            out_specs=outs,
            scratch_shapes=scratch,
        ),
        out_shape=out_shapes,
        compiler_params=pltpu.CompilerParams(
            dimension_semantics=("arbitrary",) * len(grid), vmem_limit_bytes=VMEM
        ),
        cost_estimate=pl.CostEstimate(
            flops=int(micros * PEAK), bytes_accessed=int(micros * PEAK) // 1000, transcendentals=0
        ),
        input_output_aliases=aliases or {},
        name=name,
    )


def project_kernel(
    ids, x_ref, own_ref, near_ref, far_ref, bias_ref, gain_ref, shift_ref,
    norm_ref, q_ref, k_ref, fresh_ref, other_ref, out_ref,
):
    half = q_ref.shape[1] // 2
    fresh = half // 2
    split = other_ref.shape[0] // 2

    @pl.when(pl.program_id(0) == 0)
    def _():
        first = ids[CORE] == 0
        near, far = near_ref[...], far_ref[...]
        low, high = jnp.where(first, near, far), jnp.where(first, far, near)
        other_ref[:split, :] = low[:split]
        other_ref[split:, :] = high[:split]
        out_ref[:half // 2, :] = low[split:]
        out_ref[half // 2:, :] = high[split:]

    scaled, _ = normed(x_ref[...].astype(F32))
    rows = (scaled * vector(gain_ref) + vector(shift_ref)).astype(BF16)
    norm_ref[...] = rows
    for side, weight in enumerate((own_ref, other_ref)):
        made = nn(rows, weight[:2 * half, :])
        value = nt(rows, weight[2 * half:, :])
        columns = slice(side * half, (side + 1) * half)
        q_ref[:, columns] = (made[:, :half] + bias_ref[side:side + 1, :half]).astype(BF16)
        k_ref[:, columns] = made[:, half:].astype(BF16)
        fresh_ref[side] = (value + bias_ref[side:side + 1, half:half + fresh]).astype(BF16)


def unpacked(value):
    return jnp.concatenate(
        [value[:, start:start + BLOCK] for start in range(0, value.shape[1], BLOCK)], axis=0
    ).T


def packed_rows(value):
    return jnp.concatenate(
        [value[start:start + HEAD] for start in range(0, value.shape[0], HEAD)], axis=1
    )


def doc_start(position, bounds):
    start = jnp.zeros_like(position)
    for bound in bounds:
        start = jnp.where(position >= bound, bound, start)
    return start


def attend_kernel(
    ids, x_ref, q_ref, k_ref, fresh_ref, skip_own_ref, skip_other_ref, own_ref, other_ref,
    bias_ref, gain_ref, shift_ref, v_ref, att_ref, lse_ref, middle_ref, norm_ref, att_s, lse_s,
):
    p = pl.program_id(0)
    bounds = doc_bounds(ids)
    skip_own, skip_other = unpacked(skip_own_ref[...]), unpacked(skip_other_ref[...])
    v_ref[pl.ds(pl.multiple_of(p * BLOCK, BLOCK), BLOCK), :] = jnp.concatenate(
        [fresh_ref[0], skip_own, fresh_ref[1], skip_other], axis=1
    )
    width = q_ref.shape[1]
    half = width // 2
    first = doc_start(p * BLOCK, bounds)
    needed = p - first // BLOCK + 1
    lane = lax.broadcasted_iota(jnp.int32, (1, PAIR), 1)
    low = lane < HEAD
    picks = [jnp.where(low, SCALE, 0.0).astype(BF16), jnp.where(low, 0.0, SCALE).astype(BF16)]

    def run(count):
        span = count * BLOCK
        base = pl.multiple_of((p - count + 1) * BLOCK, BLOCK)
        row = p * BLOCK + lax.broadcasted_iota(jnp.int32, (BLOCK, 1), 0)
        start = doc_start(row, bounds)
        column = base + lax.broadcasted_iota(jnp.int32, (1, span), 1)
        seen = (column <= row) & (column >= start)
        bias = jnp.where(seen, 0.0, MASKED)
        head_lane = lax.broadcasted_iota(jnp.int32, (1, 128), 1)

        @pl.loop(0, width // PAIR, unroll=3)
        def _(pair):
            lanes = pl.ds(pl.multiple_of(pair * PAIR, PAIR), PAIR)
            queries = q_ref[:, lanes]
            keys = k_ref[pl.ds(base, span), lanes]
            values = v_ref[pl.ds(base, span), lanes]
            outs = []
            for side in range(2):
                scores = nt(queries * picks[side], keys) + bias
                top = jnp.max(scores, axis=1, keepdims=True)
                probs = jnp.exp(scores - top)
                total = jnp.sum(probs, axis=1, keepdims=True)
                outs.append(nn(probs.astype(BF16), values) / total)
                lse_s[...] = jnp.where(
                    head_lane == 2 * pair + side, top + jnp.log(total), lse_s[...]
                )
            att_s[:, lanes] = jnp.where(low, outs[0], outs[1]).astype(BF16)

    for count in range(1, REACH + 1):
        pl.when(needed == count)(partial(run, count))

    lse_ref[...] = lse_s[...].T[:lse_ref.shape[0], :]
    attended = att_s[...]
    att_ref[...] = attended
    middle = (
        x_ref[...].astype(F32)
        + nn(attended[:, :half], own_ref[...])
        + nn(attended[:, half:], other_ref[...])
        + vector(bias_ref)
    )
    middle_ref[...] = middle.astype(BF16)
    scaled, _ = normed(middle)
    norm_ref[...] = (scaled * vector(gain_ref) + vector(shift_ref)).astype(BF16)


def feed_kernel(fetched, has_sums, has_grads, swapped, ids, *refs):
    norm_ref, grad_ref = refs[:2]
    if fetched:
        mine_ref, theirs_ref, down_ref, bias_ref = refs[2:6]
        refs = refs[6:]
        first = ids[OUTER] % 2 == 0
        mine, theirs = mine_ref[...], theirs_ref[...]
        up = jnp.concatenate(
            [jnp.where(first, mine, theirs), jnp.where(first, theirs, mine)], axis=0
        )
        down = down_ref[...]
    else:
        weight_ref, bias_ref = refs[2:4]
        refs = refs[4:]
        up = weight_ref[:weight_ref.shape[0] // 2, :]
        down = weight_ref[weight_ref.shape[0] // 2:, :]
    units = up.shape[0]
    if has_sums:
        out_in, back_in = refs[:2]
        refs = refs[2:]
    if has_grads:
        made_in = refs[0]
        refs = refs[1:]
    out_ref, back_ref, gb_ref = refs[:3]
    made_refs = refs[3:]
    rows = norm_ref[...]
    grads = grad_ref[...]
    hidden = nt(rows, up) + bias_ref[...]
    square = hidden * hidden
    curve = jnp.tanh(hidden * (GELU_A + GELU_A * GELU_B * square))
    plus = 0.5 + 0.5 * curve
    value = hidden * plus
    active = value.astype(BF16)
    slope = plus + value * (1.0 - curve) * (GELU_A + 3.0 * GELU_A * GELU_B * square)
    hidden_grad = nt(grads, down) * slope
    gb_ref[...] = jnp.sum(hidden_grad, axis=0, keepdims=True)
    hidden_low = hidden_grad.astype(BF16)
    out = nn(active, down)
    back = nn(hidden_low, up)
    if has_sums:
        out = out + out_in[...].astype(F32)
        back = back + back_in[...].astype(F32)
    out_ref[...] = out.astype(BF16)
    back_ref[...] = back.astype(BF16)
    for piece, left, right in (
        (slice(0, units), hidden_low, rows), (slice(units, 2 * units), active, grads)
    ):
        made = tn(left, right)
        if has_grads:
            made = made + made_in[piece, :].astype(F32)
        made = made.astype(BF16)
        count = made_refs[0].shape[0]
        for row in range(piece.start, piece.stop, count):
            part = made_refs[row // count]
            if count > units:
                part[piece, :] = made
            elif swapped and piece.start > 0:
                near = made[row - piece.start:row - piece.start + count]
                far = made[units - count - row + piece.start:units - row + piece.start]
                part[...] = jnp.where(ids[OUTER] % 2 == 0, near, far)
            else:
                part[...] = made[row - piece.start:row - piece.start + count]


def feed(ids, rows, grads, weights, bias, sums=(), made=(), parts=1,
         swapped=False):
    tokens, width = rows.shape
    units = bias.shape[1]
    total = full((tokens, width))
    return call(
        partial(feed_kernel, len(weights) > 1, len(sums) > 0, len(made) > 0, swapped),
        1,
        (1,),
        [total, total] + [full(weight.shape) for weight in weights] + [full((1, units))]
        + [total] * len(sums) + [full((2 * units, width))] * len(made),
        [total, total, full((1, units))] + [full((2 * units // parts, width))] * parts,
        [
            shape_of((tokens, width), BF16), shape_of((tokens, width), BF16),
            shape_of((1, units), F32),
        ] + [shape_of((2 * units // parts, width), BF16)] * parts,
        micros=14,
        name="feed",
    )(ids, rows, grads, *weights, bias, *sums, *made)


def residual_kernel(
    ids, out_a, out_b, back_a, back_b, grad_ref, middle_ref, att_ref, own_ref, other_ref,
    gain_ref, down_bias_ref, layer_ref, mg_ref, ga_ref, keep_ref, send_ref, small_ref, acc_s,
):
    p = pl.program_id(0)
    half = own_ref.shape[0]
    middle = middle_ref[...].astype(F32)
    summed = lambda refs: sum(ref[...].astype(F32) for ref in refs)
    layer_ref[...] = (middle + summed((out_a, out_b)) + vector(down_bias_ref)).astype(BF16)
    scaled, inverse = normed(middle)
    second = summed((back_a, back_b))
    out_grad = grad_ref[...].astype(F32)
    middle_grad = out_grad + norm_back(second, scaled, inverse, vector(gain_ref))
    low = middle_grad.astype(BF16)
    mg_ref[...] = low
    ga_ref[:, :half] = nt(low, own_ref[...]).astype(BF16)
    ga_ref[:, half:] = nt(low, other_ref[...]).astype(BF16)
    weight_grad = tn(att_ref[...], low)
    sums = jnp.concatenate(
        [
            jnp.sum(value, axis=0, keepdims=True)
            for value in (second * scaled, second, middle_grad, out_grad)
        ],
        axis=0,
    )

    @pl.when(p == 0)
    def _():
        acc_s[...] = weight_grad
        small_ref[...] = sums

    @pl.when(p > 0)
    def _():
        acc_s[...] += weight_grad
        small_ref[...] += sums

    @pl.when(p == pl.num_programs(0) - 1)
    def _():
        rows = half // 2
        near = pl.multiple_of(ids[CORE] * rows, 32)
        far = pl.multiple_of(rows - ids[CORE] * rows, 32)
        for side in range(2):
            keep_ref[side] = acc_s[pl.ds(side * half + near, rows), :].astype(BF16)
            send_ref[side] = acc_s[pl.ds(side * half + far, rows), :].astype(BF16)


def attend_back_kernel(
    head_base, ids, q_ref, k_ref, v_ref, att_ref, ga_ref, lse_ref,
    made_ref, skip_ref, dq_s, dk_s, dv_s, delta_s,
):
    p = pl.program_id(0)
    width = q_ref.shape[1]
    fresh = width // 2
    bounds = doc_bounds(ids)
    place = member_at(p, ids)
    first = doc_start(p * BLOCK, bounds)
    needed = p - first // BLOCK + 1
    low = lax.broadcasted_iota(jnp.int32, (1, PAIR), 1) < HEAD
    picks = [jnp.where(low, SCALE, 0.0).astype(BF16), jnp.where(low, 0.0, SCALE).astype(BF16)]
    ones = [jnp.where(low, 1.0, 0.0).astype(BF16), jnp.where(low, 0.0, 1.0).astype(BF16)]

    @pl.when(p == 0)
    def _():
        dk_s[...] = jnp.zeros_like(dk_s)
        dv_s[...] = jnp.zeros_like(dv_s)

    product = ga_ref[...].astype(F32) * att_ref[...].astype(F32)
    high = product.astype(BF16)
    rest = (product - high.astype(F32)).astype(BF16)
    owner = lax.broadcasted_iota(jnp.int32, (delta_s.shape[0], width), 1) // HEAD
    which = lax.broadcasted_iota(jnp.int32, (delta_s.shape[0], width), 0)
    gather = (owner == which).astype(F32).astype(BF16)
    delta_s[...] = nt(gather, high) + nt(gather, rest)

    def run(count):
        span = count * BLOCK
        base = pl.multiple_of((p - count + 1) * BLOCK, BLOCK)
        row = p * BLOCK + lax.broadcasted_iota(jnp.int32, (1, BLOCK), 1)
        start = doc_start(row, bounds)
        column = base + lax.broadcasted_iota(jnp.int32, (span, 1), 0)
        seen = (column <= row) & (column >= start)
        bias = jnp.where(seen, 0.0, MASKED)

        @pl.loop(0, width // PAIR, unroll=3)
        def _(pair):
            lanes = pl.ds(pl.multiple_of(pair * PAIR, PAIR), PAIR)
            queries = q_ref[:, lanes]
            grads = ga_ref[:, lanes]
            keys = k_ref[pl.ds(base, span), lanes]
            values = v_ref[pl.ds(base, span), lanes]
            query_parts = []
            for side in range(2):
                head = 2 * pair + side
                picked = queries * picks[side]
                chosen = grads * ones[side]
                scores = nt(keys, picked) + bias
                probs = jnp.exp(scores - lse_ref[pl.ds(head_base + head, 1), :])
                dprobs = nt(values, chosen)
                dscores = (probs * (dprobs - delta_s[pl.ds(head, 1), :])).astype(BF16)
                value_part = nn(probs.astype(BF16), chosen)
                key_part = nn(dscores, picked)
                query_parts.append(tn(dscores, keys))
                if side == 0:
                    value_sum, key_sum = value_part, key_part
                else:
                    value_sum, key_sum = value_sum + value_part, key_sum + key_part
            dv_s[pl.ds(base, span), lanes] += value_sum
            dk_s[pl.ds(base, span), lanes] += key_sum
            dq_s[:, lanes] = (
                jnp.where(low, query_parts[0], query_parts[1]) * SCALE
            ).astype(BF16)

    for count in range(1, REACH + 1):
        pl.when(needed == count)(partial(run, count))

    made_ref[place, :, :width] = dq_s[...]

    @pl.when(p == pl.num_programs(0) - 1)
    def _():
        for block in range(SPAN):
            rows = slice(block * BLOCK, (block + 1) * BLOCK)
            to = member_at(block, ids)
            made_ref[to, :, width:2 * width] = dk_s[rows, :].astype(BF16)
            value_grad = dv_s[rows, :]
            made_ref[to, :, 2 * width:] = value_grad[:, :fresh].astype(BF16)
            skip_ref[to] = packed_rows(value_grad.T[fresh:, :].astype(BF16))


def weight_kernel(ids, norm_ref, made_ref, keep_ref, send_ref, sums_ref, made_s):
    rows = norm_ref[...]
    grads = made_ref[...]
    width = rows.shape[1]
    made_s[:width, :] = tn(rows, grads[:, :width])
    made_s[width:, :] = tn(grads[:, width:], rows)
    half = made_s.shape[0] // 2
    near = pl.multiple_of(ids[CORE] * half, 32)
    far = pl.multiple_of(half - ids[CORE] * half, 32)
    for target, start in ((keep_ref, near), (send_ref, far)):
        target[...] = made_s[pl.ds(start, half), :].astype(BF16)
    sums_ref[...] = jnp.sum(grads.astype(F32), axis=0, keepdims=True)


def input_kernel(
    ids, own_ref, other_ref, w_own_ref, w_other_ref, x_ref, mg_ref, skip_own_ref, skip_other_ref,
    gain_ref, *refs
):
    grad_refs, small_ref = refs[:-1], refs[-1]
    p = pl.program_id(0)
    first = None
    for made_ref, weight in ((own_ref, w_own_ref), (other_ref, w_other_ref)):
        width = weight.shape[1]
        part = nt(made_ref[:, :width], weight[:width, :]) + nn(made_ref[:, width:], weight[width:, :])
        first = part if first is None else first + part
    scaled, inverse = normed(x_ref[...].astype(F32))
    tokens, each = x_ref.shape[0], skip_own_ref.shape[0]
    made = (mg_ref[...].astype(F32) + norm_back(first, scaled, inverse, vector(gain_ref))).astype(BF16)
    for distance, grad_ref in enumerate(grad_refs):

        @pl.when(p == distance)
        def _():
            grad_ref[:tokens, :] = made
            grad_ref[tokens:tokens + each, :] = skip_own_ref[...]
            grad_ref[tokens + each:, :] = skip_other_ref[...]
    sums = jnp.concatenate(
        [jnp.sum(value, axis=0, keepdims=True) for value in (first * scaled, first)], axis=0
    )

    @pl.when(p == 0)
    def _():
        small_ref[...] = sums

    @pl.when(p > 0)
    def _():
        small_ref[...] += sums


def fold_kernel(groups, starts, ids, *refs):
    sources = sum(len(group) for group in groups)
    outs = refs[sources:-1]
    total_s = refs[-1]
    row = 0
    place = 0
    for group in groups:
        total = None
        for index in group:
            ref = refs[place]
            place += 1
            if isinstance(index, str):
                value = ref[...].astype(F32)
                value = jnp.where(ids[OUTER] % 2 == int(index), value, jnp.zeros_like(value))
            else:
                value = (ref[...] if index is None else ref[index]).astype(F32)
            total = value if total is None else total + value
        total_s[row:row + total.shape[0], :] = total
        row += total.shape[0]
    if row < total_s.shape[0]:
        total_s[row:, :] = jnp.zeros((total_s.shape[0] - row, total_s.shape[1]), F32)
    for out, start in zip(outs, starts):
        at = start(ids)
        if not isinstance(at, int):
            at = pl.multiple_of(at, 8)
        out[...] = total_s[pl.ds(at, out.shape[0]), :].astype(BF16)


def fold(ids, groups, starts, count, rows=0):
    arrays = [entry[0] for group in groups for entry in group]
    indices = tuple(tuple(entry[1] for entry in group) for group in groups)
    width = arrays[0].shape[-1]
    rows = max(rows, sum(group[0][0].shape[-2] for group in groups))
    return call(
        partial(fold_kernel, indices, starts),
        1,
        (1,),
        [full(array.shape) for array in arrays],
        [full((count, width)) for _ in starts],
        [shape_of((count, width), BF16) for _ in starts],
        scratch=[pltpu.VMEM((rows, width), F32)],
        micros=3.5,
        name="fold",
    )(ids, *arrays)


def spread_sum_kernel(ids, parts_ref, spread_ref):
    total = jnp.sum(parts_ref[...].astype(F32), axis=0).astype(BF16)
    for index in range(parts_ref.shape[0]):
        spread_ref[index] = total


def spread_sum(ids, parts):
    return call(
        spread_sum_kernel,
        1,
        (1,),
        [full(parts.shape)],
        [full(parts.shape)],
        [shape_of(parts.shape, BF16)],
        micros=2.5,
        name="spread_sum",
    )(ids, parts)[0]


def collect_kernel(ids, *refs):
    grad_ref, skip_ref = refs[-2:]
    for distance, ref in enumerate(refs[:-2]):
        place = ids[MINE] ^ distance
        grad_ref[place] = ref[:BLOCK, :].astype(F32)
        for side in range(2):
            rows = ref[BLOCK + side * HEAD:BLOCK + (side + 1) * HEAD, :].astype(F32)
            column = ((ids[TP] ^ side) * SPAN + place) * BLOCK
            columns = pl.ds(pl.multiple_of(column, BLOCK), BLOCK)
            for index in range(rows.shape[1] // BLOCK):
                skip_ref[index * HEAD:(index + 1) * HEAD, columns] = rows[
                    :, index * BLOCK:(index + 1) * BLOCK
                ]


def collect(ids, pieces):
    rows, width = pieces[0].shape
    features = width // BLOCK * HEAD
    return call(
        collect_kernel,
        1,
        (1,),
        [full((rows, width))] * len(pieces),
        [full((SPAN, BLOCK, width)), full((features, 2 * SPAN * BLOCK))],
        [shape_of((SPAN, BLOCK, width), F32), shape_of((features, 2 * SPAN * BLOCK), F32)],
        micros=5,
        name="collect",
    )(ids, *pieces)


def place_feed_kernel(ids, mine_ref, theirs_ref, up_ref, down_ref):
    units = down_ref.shape[0]
    here = pl.program_id(0) == ids[CORE]
    whole = jnp.where(here, mine_ref[...], theirs_ref[...]).astype(F32)
    up_ref[...] = whole[:units].T
    down_ref[...] = whole[units:]


def place_feed(ids, mine, theirs):
    rows, width = mine.shape
    return call(
        place_feed_kernel,
        1,
        (2,),
        [full((rows, width))] * 2,
        [
            pl.BlockSpec((width, rows // 2), lambda h, ids: (0, h)),
            pl.BlockSpec((rows // 2, width), lambda h, ids: (h, 0)),
        ],
        [shape_of((width, rows), F32), shape_of((rows, width), F32)],
        micros=8,
        name="place_feed",
    )(ids, mine, theirs)


def place_qkv_kernel(ids, mine_ref, theirs_ref, q_ref, k_ref, v_ref, out_ref):
    half = q_ref.shape[1]
    split = (q_ref.shape[0] + v_ref.shape[0]) // 2
    half_out = out_ref.shape[0] // 2
    first = ids[CORE] == 0
    mine, theirs = mine_ref[...], theirs_ref[...]
    low = jnp.where(first, mine, theirs).astype(F32)
    high = jnp.where(first, theirs, mine).astype(F32)
    out_ref[:half_out, :] = low[split:split + half_out]
    out_ref[half_out:, :] = high[split:split + half_out]
    rest = q_ref.shape[0] - split
    for ref, columns in ((q_ref, slice(0, half)), (k_ref, slice(half, 2 * half))):
        ref[:split, :] = low[:split, columns]
        ref[split:, :] = high[:rest, columns]
    v_ref[...] = high[rest:split]


def place_qkv(ids, mine, theirs, half, fresh):
    rows, width = mine.shape
    return call(
        place_qkv_kernel,
        1,
        (1,),
        [full((rows, width))] * 2,
        [full((width, half)), full((width, half)), full((fresh, width)), full((half, width))],
        [
            shape_of((width, half), F32), shape_of((width, half), F32),
            shape_of((fresh, width), F32), shape_of((half, width), F32),
        ],
        micros=4,
        name="place_qkv",
    )(ids, mine, theirs)


def tie(value, *others):
    return lax.optimization_barrier((value,) + others)[0]


def per_device(
    sizes,
    layer_in,
    skip_values,
    block_slot,
    doc_lengths,
    gain_attention,
    shift_attention,
    query_weight,
    query_bias,
    key_weight,
    value_weight,
    value_bias,
    out_weight,
    out_bias,
    gain_feed,
    shift_feed,
    up_weight,
    up_bias,
    down_weight,
    down_bias,
    out_grad,
):
    seq_count, tp_count = sizes
    width = layer_in.shape[1]
    half = query_weight.shape[1]
    fresh = value_weight.shape[1]
    units = up_weight.shape[1]
    tokens = layer_in.shape[0]
    batch = skip_values.shape[0] // BLOCK
    heads = width // HEAD
    head_rows = -(-heads // 8) * 8
    packed = 2 * half + fresh
    side = units // 2
    seq_index = lax.axis_index("seq")
    tp_index = lax.axis_index("tp")
    member = seq_index % SPAN
    group = seq_index // SPAN
    core = seq_index % 2
    members = [[g * SPAN + m for m in range(SPAN)] for g in range(seq_count // SPAN)]
    same_core = [list(range(c, seq_count, 2)) for c in range(2)]
    others = seq_count // 2
    local_seq = tp_index * (batch // tp_count) + member

    def swap_seq(value, distance):
        return lax.ppermute(value, "seq", [(i, i ^ distance) for i in range(seq_count)])

    def swap_core(value):
        return swap_seq(value, 1)

    def swap_tp(value):
        return lax.ppermute(value, "tp", [(i, i ^ 1) for i in range(tp_count)])

    def to_seqs(value):
        return lax.all_to_all(value, "seq", 0, 0, tiled=True, axis_index_groups=members)

    def either(bit, first, second):
        return jnp.where(bit == 0, first, second)

    def in_order(bit, mine, theirs):
        return either(
            bit, jnp.concatenate([mine, theirs], 0), jnp.concatenate([theirs, mine], 0)
        )

    def rows_of(value, start, count):
        return lax.dynamic_slice_in_dim(value, start, count, 0)

    def row(value):
        return value.reshape(1, -1)

    local_seq = tp_index * (batch // tp_count) + member
    slots = lax.dynamic_slice(block_slot, (group * SPAN, local_seq), (SPAN, 1))
    holders = jnp.sum(
        jnp.where(
            slots == lax.broadcasted_iota(jnp.int32, (SPAN, SPAN), 1),
            lax.broadcasted_iota(jnp.int32, (SPAN, SPAN), 0), 0,
        ),
        axis=0,
    )
    lengths = lax.dynamic_slice(doc_lengths, (group * batch + local_seq, 0), (1, DOCS))
    ends = jnp.sum(
        jnp.where(
            lax.broadcasted_iota(jnp.int32, (DOCS, DOCS), 0)
            <= lax.broadcasted_iota(jnp.int32, (DOCS, DOCS), 1),
            lengths.reshape(DOCS, 1), 0,
        ),
        axis=0,
    )
    ids = jnp.concatenate(
        [
            jnp.stack([core, member, group, tp_index]).astype(jnp.int32), holders,
            ends[:DOCS - 1],
        ]
    ).astype(jnp.int32)

    qkv_own = jnp.concatenate(
        [jnp.concatenate([query_weight, key_weight], axis=1), value_weight.T], axis=0
    )
    early_sent = jnp.concatenate(
        [
            rows_of(qkv_own, core * (packed // 2), packed // 2),
            rows_of(out_weight, core * (half // 2), half // 2),
        ],
        0,
    )
    early_near = swap_tp(early_sent)
    layer_in, skip_values = lax.optimization_barrier((layer_in, skip_values, early_sent))[:2]
    thirds = fresh // HEAD
    skip_sent = skip_values.T.reshape(thirds, HEAD, tp_count, SPAN, BLOCK)
    skip_sent = skip_sent.transpose(3, 2, 1, 0, 4).reshape(SPAN, tp_count * HEAD, thirds * BLOCK)
    blocks_in = to_seqs(layer_in.reshape(SPAN, BLOCK, width))
    up_bias_half = rows_of(up_bias, core * side, side)
    bias_own = jnp.concatenate([query_bias, value_bias, up_bias_half])
    bias_other = swap_tp(bias_own)
    feed_own = jnp.concatenate(
        [lax.dynamic_slice_in_dim(up_weight, core * side, side, 1).T,
         rows_of(down_weight, core * side, side)], 0,
    )
    feed_own, ids = lax.optimization_barrier((feed_own, ids))
    early_near, bias_other, skip_sent = lax.optimization_barrier(
        (early_near, bias_other, skip_sent, feed_own)
    )[:3]
    skip_in = to_seqs(tie(skip_sent, blocks_in))
    early_far = swap_core(early_near)
    up_part = rows_of(feed_own, group % 2 * (side // 2), side // 2)
    up_near = swap_tp(tie(up_part, early_near))

    qkv_bias = jnp.stack([bias_own[:half + fresh], bias_other[:half + fresh]])
    own_shape = (SPAN, BLOCK, width)
    flat = (tokens, width)

    norm_one, queries, keys, fresh_values, qkv_other, out_other = call(
        project_kernel,
        1,
        (SPAN,),
        [
            placed(width), full((packed, width)), full((packed // 2 + half // 2, width)),
            full((packed // 2 + half // 2, width)), full((2, half + fresh)), full((width,)), full((width,)),
        ],
        [
            placed(width), in_rows(width), in_rows(width),
            pl.BlockSpec((2, BLOCK, fresh), lambda p, *_: (0, p, 0)), full((packed, width)),
            full((half, width)),
        ],
        [
            shape_of(own_shape, BF16), shape_of(flat, BF16), shape_of(flat, BF16),
            shape_of((2, tokens, fresh), BF16), shape_of((packed, width), BF16),
            shape_of((half, width), BF16),
        ],
        micros=9,
        name="project",
    )(ids, blocks_in, qkv_own, early_near, early_far, qkv_bias, gain_attention, shift_attention)

    grad_blocks = to_seqs(tie(out_grad.reshape(SPAN, BLOCK, width), queries, skip_in))
    up_near = tie(up_near, queries)
    up_far = swap_seq(up_near, SPAN)
    skip_in = tie(skip_in, queries)
    skip_other = swap_tp(
        lax.dynamic_slice(
            skip_in, (0, (1 - tp_index) * HEAD, 0), (SPAN, HEAD, width)
        )
    )
    down_other = swap_tp(tie(feed_own[side:], skip_in))
    lse_spec = pl.BlockSpec((head_rows, BLOCK), lambda p, *_: (0, p))
    values, attended, log_total, middle, norm_two = call(
        attend_kernel,
        1,
        (SPAN,),
        [
            placed(width), in_rows(width), full(flat),
            pl.BlockSpec((2, BLOCK, fresh), lambda p, *_: (0, p, 0)),
            pl.BlockSpec(
                (None, HEAD, width),
                lambda p, ids: (member_at(p, ids), ids[TP], 0),
            ),
            placed(width, HEAD),
            full((half, width)), full((half, width)), full((width,)), full((width,)),
            full((width,)),
        ],
        [full(flat), placed(width), lse_spec, placed(width), placed(width)],
        [
            shape_of(flat, BF16), shape_of(own_shape, BF16), shape_of((head_rows, tokens), F32),
            shape_of(own_shape, BF16), shape_of(own_shape, BF16),
        ],
        scratch=[pltpu.VMEM((BLOCK, width), BF16), pltpu.VMEM((BLOCK, 128), F32)],
        micros=27,
        name="attend",
    )(
        ids, blocks_in, queries, keys, fresh_values, skip_in, skip_other, out_weight,
        out_other,        out_bias, gain_feed, shift_feed,
    )
    rows_mine = norm_two.reshape(flat)
    grads_mine = grad_blocks.reshape(flat)

    rows_theirs = swap_core(rows_mine)
    grads_theirs = swap_core(grads_mine)
    feed_other = (up_near, up_far, down_other)
    bias_here = row(up_bias_half)
    bias_there = row(bias_other[half + fresh:])
    out_mine, back_mine, bias_one, made_other = feed(
        ids, rows_mine, grads_mine, feed_other, bias_there
    )
    rows_theirs = tie(rows_theirs, out_mine)
    out_theirs, back_theirs, bias_two, *made_other = feed(
        ids, rows_theirs, grads_theirs, feed_other, bias_there, (), (made_other,), PARTS, True
    )
    cross_one = swap_tp(made_other[0])
    given = swap_seq(made_other[3], SPAN)
    out_theirs, back_theirs, bias_three, made_own = feed(
        ids, rows_theirs, grads_theirs, (feed_own,), tie(bias_here, made_other[0]),
        (out_theirs, back_theirs),
    )
    out_given = swap_core(out_theirs)
    back_given = swap_core(back_theirs)
    cross_two = swap_tp(tie(made_other[1], cross_one, out_theirs))
    given, kept = lax.optimization_barrier((given, made_other[2], out_theirs))[:2]
    pair_sum, = fold(ids, [[(kept, None), (given, None)]], [lambda ids: 0], kept.shape[0])
    out_mine, back_mine, bias_four, *made_own = feed(
        ids, rows_mine, grads_mine, (feed_own,), tie(bias_here, cross_one, pair_sum),
        (out_mine, back_mine), (made_own,), PARTS,
    )
    cross_three = swap_tp(tie(pair_sum, cross_two, out_mine))

    def scatter(value):
        parts = value.reshape(others, value.shape[0] // others, width)
        return lax.all_to_all(parts, "seq", 0, 0, tiled=True, axis_index_groups=same_core)

    def gather(parts):
        spread = spread_sum(ids, parts)
        whole = lax.all_to_all(spread, "seq", 0, 0, tiled=True, axis_index_groups=same_core)
        return whole.reshape(-1, width)

    layer_blocks, middle_grad, att_grad, out_keep, out_send, small_two = call(
        residual_kernel,
        1,
        (SPAN,),
        [in_rows(width)] * 5
        + [
            by_block(width), by_block(width), full((half, width)), full((half, width)),
            full((width,)), full((width,)),
        ],
        [
            by_block(width), by_block(width), by_block(width),
            full((2, half // 2, width)), full((2, half // 2, width)), full((4, width)),
        ],
        [
            shape_of(own_shape, BF16), shape_of(own_shape, BF16), shape_of(own_shape, BF16),
            shape_of((2, half // 2, width), BF16), shape_of((2, half // 2, width), BF16),
            shape_of((4, width), F32),
        ],
        scratch=[pltpu.VMEM((width, width), F32)],
        micros=12.5,
        name="residual",
    )(
        ids, tie(out_mine, cross_two), out_given, back_mine, back_given, grads_mine, middle, attended, out_weight,
        out_other, gain_feed, down_bias,
    )
    sent_given = swap_core(out_send)
    out_total = (out_keep.astype(F32) + sent_given.astype(F32)).astype(BF16)
    cross_three = tie(cross_three, att_grad)
    ready_feed, = fold(
        ids,
        [
            [(made_own[0], None), (cross_one, None)],
            [(made_own[1], None), (cross_two, None)],
            [(made_own[2], None), (cross_three, "0")],
            [(made_own[3], None), (cross_three, "1")],
        ],
        [lambda ids: 0],
        2 * side,
    )
    total_feed = lax.psum(ready_feed, "seq", axis_index_groups=same_core)
    def rest():
        cross_out = swap_tp(out_total[1])

        def attend_back(which, query_rows):
            return call(
                partial(attend_back_kernel, which * (heads // 2)),
                1,
                (SPAN,),
                [
                    pl.BlockSpec((BLOCK, half), lambda p, *_: (p, which)),
                    pl.BlockSpec((tokens, half), lambda p, *_: (0, which)),
                    pl.BlockSpec((tokens, half), lambda p, *_: (0, which)),
                    placed(half, column=which), placed(half, column=which), lse_spec,
                ],
                [full((SPAN, BLOCK, packed)), full((SPAN, HEAD, width))],
                [shape_of((SPAN, BLOCK, packed), BF16), shape_of((SPAN, HEAD, width), BF16)],
                scratch=[
                    pltpu.VMEM((BLOCK, half), BF16), pltpu.VMEM((tokens, half), F32),
                    pltpu.VMEM((tokens, half), F32), pltpu.VMEM((8, BLOCK), F32),
                ],
                micros=17.5,
                name="attend_back",
            )(
                ids, query_rows, keys, values, attended, att_grad,
                log_total,
            )

        qkv_rows = packed // 2
        last_rows = -(-(qkv_rows + half // 2) // 64) * 64

        def weights(made):
            return call(
                weight_kernel,
                1,
                (1,),
                [full(flat), full((tokens, packed))],
                [full((qkv_rows, width)), full((qkv_rows, width)), full((1, packed))],
                [
                    shape_of((qkv_rows, width), BF16), shape_of((qkv_rows, width), BF16),
                    shape_of((1, packed), F32),
                ],
                scratch=[pltpu.VMEM((packed, width), F32)],
                micros=6,
                name="weights",
            )(ids, norm_one.reshape(flat), made.reshape(tokens, packed))

        layer_out = to_seqs(layer_blocks).reshape(flat)
        grads_other, skip_made = attend_back(1, queries)
        keep_other, send_other, sums_other = weights(tie(grads_other, cross_out))
        given_other = swap_core(send_other)
        total_other, = fold(
            ids, [[(keep_other, None), (given_other, None)]], [lambda ids: 0], qkv_rows
        )
        cross_other = swap_tp(total_other)
        grads_own, skip_own = attend_back(0, tie(queries, total_other, layer_out))
        skip_theirs = swap_tp(tie(skip_made, grads_own))
        keep_own, send_own, sums_own = weights(tie(grads_own, cross_other))
        given_own = swap_core(send_own)

        ready_qkv, = fold(
            ids,
            [
                [(keep_own, None), (given_own, None), (cross_other, None)],
                [(out_total, 0), (cross_out, None)],
            ],
            [lambda ids: 0],
            last_rows,
            last_rows,
        )
        parts_qkv = scatter(ready_qkv)
        def by_distance(columns, rows=BLOCK):
            return pl.BlockSpec((None, rows, columns), lambda p, ids: (ids[MINE] ^ p, 0, 0))

        *input_blocks, small_one = call(
            input_kernel,
            1,
            (SPAN,),
            [
                by_distance(packed), by_distance(packed), full((packed, width)),
                full((packed, width)), by_distance(width), by_distance(width),
                by_distance(width, HEAD), by_distance(width, HEAD), full((width,)),
            ],
            [full((BLOCK + 2 * HEAD, width))] * SPAN + [full((2, width))],
            [shape_of((BLOCK + 2 * HEAD, width), BF16)] * SPAN + [shape_of((2, width), F32)],
            micros=9,
            name="input",
        )(
            ids, tie(grads_own, ready_qkv), grads_other, qkv_own, qkv_other, blocks_in, middle_grad,
            skip_own, skip_theirs, gain_attention,
        )
        back = [input_blocks[0]] + [
            swap_seq(input_blocks[distance], distance) for distance in range(1, SPAN)
        ]
        shared = jnp.concatenate([small_one.reshape(-1), small_two.reshape(-1)])
        widened = lambda value: jnp.where(
            lax.broadcasted_iota(jnp.int32, (2, 1), 0) == core, value, 0.0
        ).reshape(-1)
        split_own = jnp.concatenate([sums_own.reshape(-1), widened(bias_three + bias_four)])
        split_other = jnp.concatenate([sums_other.reshape(-1), widened(bias_one + bias_two)])
        vector_own = jnp.concatenate([shared, split_own])
        vector_other = jnp.concatenate([shared, split_other])

        vectors = vector_own + swap_tp(vector_other)
        for distance in [1] + [SPAN << bit for bit in range((seq_count // SPAN).bit_length() - 1)]:
            vectors = vectors + swap_seq(vectors, distance)
        parts_qkv, *back = lax.optimization_barrier((parts_qkv, vectors, *back))
        vectors = back.pop(0)
        return (layer_out, parts_qkv, vectors, *back)

    shapes = jax.eval_shape(rest)
    results = lax.cond(
        jnp.min(lengths) > 0, rest, lambda: tuple(jnp.zeros(s.shape, s.dtype) for s in shapes)
    )
    layer_out, parts_qkv, vectors, *back = results
    late = ids + (vectors[0] * 0.0).astype(jnp.int32)
    whole_qkv = gather(parts_qkv)
    total_feed = tie(total_feed, late)
    far_feed = swap_core(total_feed)
    input_grad, skip_grad = collect(ids, back)
    input_grad, skip_grad = input_grad.reshape(flat), skip_grad.T
    vectors = vectors + swap_seq(vectors, 2)
    grad_up_weight, grad_down_weight = place_feed(late, total_feed, far_feed)
    whole_qkv, vectors = lax.optimization_barrier(
        (whole_qkv, vectors, grad_up_weight, input_grad, skip_grad)
    )[:2]
    grad_query, grad_key, grad_value, grad_out_weight = place_qkv(
        ids, whole_qkv, swap_core(whole_qkv), half, fresh
    )
    shared = vectors[:6 * width].reshape(6, width)
    split = vectors[6 * width:]

    return (
        layer_out,
        input_grad,
        skip_grad,
        shared[0],
        shared[1],
        grad_query,
        split[:half],
        grad_key,
        grad_value.T,
        split[2 * half:packed],
        grad_out_weight,
        shared[4],
        shared[2],
        shared[3],
        grad_up_weight,
        split[packed:],
        grad_down_weight,
        shared[5],
    )


def solution(mesh):
    return jax.shard_map(
        partial(per_device, (mesh.shape["seq"], mesh.shape["tp"])),
        mesh=mesh,
        in_specs=(
            P(("seq", "tp"), None),
            P("seq", "tp"),
            P(),
            P(),
            P(),
            P(),
            P(None, "tp"),
            P("tp"),
            P(None, "tp"),
            P(None, "tp"),
            P("tp"),
            P("tp", None),
            P(),
            P(),
            P(),
            P(None, "tp"),
            P("tp"),
            P("tp", None),
            P(),
            P(("seq", "tp"), None),
        ),
        out_specs=(
            P(("seq", "tp"), None),
            P(("seq", "tp"), None),
            P("seq", "tp"),
            P(),
            P(),
            P(None, "tp"),
            P("tp"),
            P(None, "tp"),
            P(None, "tp"),
            P("tp"),
            P("tp", None),
            P(),
            P(),
            P(),
            P(None, "tp"),
            P("tp"),
            P("tp", None),
            P(),
        ),
        check_vma=False,
    )
```

```python
from functools import partial

import jax
import jax.numpy as jnp
from jax import lax
from jax.experimental import pallas as pl
from jax.experimental.pallas import tpu as pltpu
from jax.sharding import PartitionSpec as P

HEAD = 64
SEQ_LEN = 1024
BLOCK = 256
LONGEST = 512
SPAN = SEQ_LEN // BLOCK
REACH = -(-LONGEST // BLOCK) + 1
PAIR = 2 * HEAD
EPSILON = 1e-05
MASKED = -1e30
GELU_A = 0.7978845608028654
GELU_B = 0.044715
SCALE = HEAD ** (-0.5)
DOCS = 4
PARTS = 4
CORE, MINE, OUTER, TP, MEMBER = 0, 1, 2, 3, 4
BOUND = MEMBER + SPAN
PEAK = 1.15e9
VMEM = 56 * 1024 * 1024

F32 = jnp.float32
BF16 = jnp.bfloat16


def nn(left, right):
    return lax.dot_general(left, right, (((1,), (0,)), ((), ())), preferred_element_type=F32)


def nt(left, right):
    return lax.dot_general(left, right, (((1,), (1,)), ((), ())), preferred_element_type=F32)


def tn(left, right):
    return lax.dot_general(left, right, (((0,), (0,)), ((), ())), preferred_element_type=F32)


def vector(ref):
    return ref[...].reshape(1, -1)


def normed(rows):
    centred = rows - jnp.mean(rows, axis=-1, keepdims=True)
    inverse = lax.rsqrt(jnp.mean(centred * centred, axis=-1, keepdims=True) + EPSILON)
    return centred * inverse, inverse


def norm_back(grad_out, scaled, inverse, gain):
    grad_scaled = grad_out * gain
    first_mean = jnp.mean(grad_scaled, axis=-1, keepdims=True)
    second_mean = jnp.mean(grad_scaled * scaled, axis=-1, keepdims=True)
    return inverse * (grad_scaled - first_mean - scaled * second_mean)


def full(shape):
    return pl.BlockSpec(shape, lambda *_: (0,) * len(shape), pipeline_mode=pl.Buffered(1))


def member_at(p, ids):
    return ids[MEMBER + p]


def doc_bounds(ids):
    return [ids[BOUND + index] for index in range(DOCS - 1)]


def placed(columns, rows=BLOCK, column=0):
    return pl.BlockSpec(
        (None, rows, columns), lambda p, ids: (member_at(p, ids), 0, column)
    )


def in_rows(columns):
    return pl.BlockSpec((BLOCK, columns), lambda p, *_: (p, 0))


def by_block(columns):
    return pl.BlockSpec((None, BLOCK, columns), lambda p, *_: (p, 0, 0))


def shape_of(shape, dtype):
    return jax.ShapeDtypeStruct(shape, dtype)


def call(kernel, scalars, grid, ins, outs, out_shapes, scratch=(), micros=1, name=None,
         aliases=None):
    return pl.pallas_call(
        kernel,
        grid_spec=pltpu.PrefetchScalarGridSpec(
            num_scalar_prefetch=scalars,
            grid=grid,
            in_specs=ins,
            out_specs=outs,
            scratch_shapes=scratch,
        ),
        out_shape=out_shapes,
        compiler_params=pltpu.CompilerParams(
            dimension_semantics=("arbitrary",) * len(grid), vmem_limit_bytes=VMEM
        ),
        cost_estimate=pl.CostEstimate(
            flops=int(micros * PEAK), bytes_accessed=int(micros * PEAK) // 1000, transcendentals=0
        ),
        input_output_aliases=aliases or {},
        name=name,
    )


def project_kernel(
    ids, x_ref, own_ref, near_ref, far_ref, bias_ref, gain_ref, shift_ref,
    norm_ref, q_ref, k_ref, fresh_ref, other_ref, out_ref,
):
    half = q_ref.shape[1] // 2
    fresh = half // 2
    split = other_ref.shape[0] // 2

    @pl.when(pl.program_id(0) == 0)
    def _():
        first = ids[CORE] == 0
        near, far = near_ref[...], far_ref[...]
        low, high = jnp.where(first, near, far), jnp.where(first, far, near)
        other_ref[:split, :] = low[:split]
        other_ref[split:, :] = high[:split]
        out_ref[:half // 2, :] = low[split:]
        out_ref[half // 2:, :] = high[split:]

    scaled, _ = normed(x_ref[...].astype(F32))
    rows = (scaled * vector(gain_ref) + vector(shift_ref)).astype(BF16)
    norm_ref[...] = rows
    for side, weight in enumerate((own_ref, other_ref)):
        made = nn(rows, weight[:2 * half, :])
        value = nt(rows, weight[2 * half:, :])
        columns = slice(side * half, (side + 1) * half)
        q_ref[:, columns] = (made[:, :half] + bias_ref[side:side + 1, :half]).astype(BF16)
        k_ref[:, columns] = made[:, half:].astype(BF16)
        fresh_ref[side] = (value + bias_ref[side:side + 1, half:half + fresh]).astype(BF16)


def unpacked(value):
    return jnp.concatenate(
        [value[:, start:start + BLOCK] for start in range(0, value.shape[1], BLOCK)], axis=0
    ).T


def packed_rows(value):
    return jnp.concatenate(
        [value[start:start + HEAD] for start in range(0, value.shape[0], HEAD)], axis=1
    )


def doc_start(position, bounds):
    start = jnp.zeros_like(position)
    for bound in bounds:
        start = jnp.where(position >= bound, bound, start)
    return start


def attend_kernel(
    ids, x_ref, q_ref, k_ref, fresh_ref, skip_own_ref, skip_other_ref, own_ref, other_ref,
    bias_ref, gain_ref, shift_ref, v_ref, att_ref, lse_ref, middle_ref, norm_ref, att_s, lse_s,
):
    p = pl.program_id(0)
    bounds = doc_bounds(ids)
    skip_own, skip_other = unpacked(skip_own_ref[...]), unpacked(skip_other_ref[...])
    v_ref[pl.ds(pl.multiple_of(p * BLOCK, BLOCK), BLOCK), :] = jnp.concatenate(
        [fresh_ref[0], skip_own, fresh_ref[1], skip_other], axis=1
    )
    width = q_ref.shape[1]
    half = width // 2
    first = doc_start(p * BLOCK, bounds)
    needed = p - first // BLOCK + 1
    lane = lax.broadcasted_iota(jnp.int32, (1, PAIR), 1)
    low = lane < HEAD
    picks = [jnp.where(low, SCALE, 0.0).astype(BF16), jnp.where(low, 0.0, SCALE).astype(BF16)]

    def run(count):
        span = count * BLOCK
        base = pl.multiple_of((p - count + 1) * BLOCK, BLOCK)
        row = p * BLOCK + lax.broadcasted_iota(jnp.int32, (BLOCK, 1), 0)
        start = doc_start(row, bounds)
        column = base + lax.broadcasted_iota(jnp.int32, (1, span), 1)
        seen = (column <= row) & (column >= start)
        bias = jnp.where(seen, 0.0, MASKED)
        head_lane = lax.broadcasted_iota(jnp.int32, (1, 128), 1)

        @pl.loop(0, width // PAIR, unroll=6)
        def _(pair):
            lanes = pl.ds(pl.multiple_of(pair * PAIR, PAIR), PAIR)
            queries = q_ref[:, lanes]
            keys = k_ref[pl.ds(base, span), lanes]
            values = v_ref[pl.ds(base, span), lanes]
            outs = []
            for side in range(2):
                scores = nt(queries * picks[side], keys) + bias
                top = jnp.max(scores, axis=1, keepdims=True)
                probs = jnp.exp(scores - top)
                total = jnp.sum(probs, axis=1, keepdims=True)
                outs.append(nn(probs.astype(BF16), values) / total)
                lse_s[...] = jnp.where(
                    head_lane == 2 * pair + side, top + jnp.log(total), lse_s[...]
                )
            att_s[:, lanes] = jnp.where(low, outs[0], outs[1]).astype(BF16)

    for count in range(1, REACH + 1):
        pl.when(needed == count)(partial(run, count))

    lse_ref[...] = lse_s[...].T[:lse_ref.shape[0], :]
    attended = att_s[...]
    att_ref[...] = attended
    middle = (
        x_ref[...].astype(F32)
        + nn(attended[:, :half], own_ref[...])
        + nn(attended[:, half:], other_ref[...])
        + vector(bias_ref)
    )
    middle_ref[...] = middle.astype(BF16)
    scaled, _ = normed(middle)
    norm_ref[...] = (scaled * vector(gain_ref) + vector(shift_ref)).astype(BF16)


def feed_kernel(fetched, has_sums, has_grads, swapped, ids, *refs):
    norm_ref, grad_ref = refs[:2]
    if fetched:
        mine_ref, theirs_ref, down_ref, bias_ref = refs[2:6]
        refs = refs[6:]
        first = ids[OUTER] % 2 == 0
        mine, theirs = mine_ref[...], theirs_ref[...]
        up = jnp.concatenate(
            [jnp.where(first, mine, theirs), jnp.where(first, theirs, mine)], axis=0
        )
        down = down_ref[...]
    else:
        weight_ref, bias_ref = refs[2:4]
        refs = refs[4:]
        up = weight_ref[:weight_ref.shape[0] // 2, :]
        down = weight_ref[weight_ref.shape[0] // 2:, :]
    units = up.shape[0]
    if has_sums:
        out_in, back_in = refs[:2]
        refs = refs[2:]
    if has_grads:
        made_in = refs[0]
        refs = refs[1:]
    out_ref, back_ref, gb_ref = refs[:3]
    made_refs = refs[3:]
    rows = norm_ref[...]
    grads = grad_ref[...]
    hidden = nt(rows, up) + bias_ref[...]
    square = hidden * hidden
    curve = jnp.tanh(hidden * (GELU_A + GELU_A * GELU_B * square))
    plus = 0.5 + 0.5 * curve
    value = hidden * plus
    active = value.astype(BF16)
    slope = plus + value * (1.0 - curve) * (GELU_A + 3.0 * GELU_A * GELU_B * square)
    hidden_grad = nt(grads, down) * slope
    gb_ref[...] = jnp.sum(hidden_grad, axis=0, keepdims=True)
    hidden_low = hidden_grad.astype(BF16)
    out = nn(active, down)
    back = nn(hidden_low, up)
    if has_sums:
        out = out + out_in[...].astype(F32)
        back = back + back_in[...].astype(F32)
    out_ref[...] = out.astype(BF16)
    back_ref[...] = back.astype(BF16)
    for piece, left, right in (
        (slice(0, units), hidden_low, rows), (slice(units, 2 * units), active, grads)
    ):
        made = tn(left, right)
        if has_grads:
            made = made + made_in[piece, :].astype(F32)
        made = made.astype(BF16)
        count = made_refs[0].shape[0]
        for row in range(piece.start, piece.stop, count):
            part = made_refs[row // count]
            if count > units:
                part[piece, :] = made
            elif swapped and piece.start > 0:
                near = made[row - piece.start:row - piece.start + count]
                far = made[units - count - row + piece.start:units - row + piece.start]
                part[...] = jnp.where(ids[OUTER] % 2 == 0, near, far)
            else:
                part[...] = made[row - piece.start:row - piece.start + count]


def feed(ids, rows, grads, weights, bias, sums=(), made=(), parts=1,
         swapped=False):
    tokens, width = rows.shape
    units = bias.shape[1]
    total = full((tokens, width))
    return call(
        partial(feed_kernel, len(weights) > 1, len(sums) > 0, len(made) > 0, swapped),
        1,
        (1,),
        [total, total] + [full(weight.shape) for weight in weights] + [full((1, units))]
        + [total] * len(sums) + [full((2 * units, width))] * len(made),
        [total, total, full((1, units))] + [full((2 * units // parts, width))] * parts,
        [
            shape_of((tokens, width), BF16), shape_of((tokens, width), BF16),
            shape_of((1, units), F32),
        ] + [shape_of((2 * units // parts, width), BF16)] * parts,
        micros=14,
        name="feed",
    )(ids, rows, grads, *weights, bias, *sums, *made)


def residual_kernel(
    ids, out_a, out_b, back_a, back_b, grad_ref, middle_ref, att_ref, own_ref, other_ref,
    gain_ref, down_bias_ref, layer_ref, mg_ref, ga_ref, keep_ref, send_ref, small_ref, acc_s,
):
    p = pl.program_id(0)
    half = own_ref.shape[0]
    middle = middle_ref[...].astype(F32)
    summed = lambda refs: sum(ref[...].astype(F32) for ref in refs)
    layer_ref[...] = (middle + summed((out_a, out_b)) + vector(down_bias_ref)).astype(BF16)
    scaled, inverse = normed(middle)
    second = summed((back_a, back_b))
    out_grad = grad_ref[...].astype(F32)
    middle_grad = out_grad + norm_back(second, scaled, inverse, vector(gain_ref))
    low = middle_grad.astype(BF16)
    mg_ref[...] = low
    ga_ref[:, :half] = nt(low, own_ref[...]).astype(BF16)
    ga_ref[:, half:] = nt(low, other_ref[...]).astype(BF16)
    weight_grad = tn(att_ref[...], low)
    sums = jnp.concatenate(
        [
            jnp.sum(value, axis=0, keepdims=True)
            for value in (second * scaled, second, middle_grad, out_grad)
        ],
        axis=0,
    )

    @pl.when(p == 0)
    def _():
        acc_s[...] = weight_grad
        small_ref[...] = sums

    @pl.when(p > 0)
    def _():
        acc_s[...] += weight_grad
        small_ref[...] += sums

    @pl.when(p == pl.num_programs(0) - 1)
    def _():
        rows = half // 2
        near = pl.multiple_of(ids[CORE] * rows, 32)
        far = pl.multiple_of(rows - ids[CORE] * rows, 32)
        for side in range(2):
            keep_ref[side] = acc_s[pl.ds(side * half + near, rows), :].astype(BF16)
            send_ref[side] = acc_s[pl.ds(side * half + far, rows), :].astype(BF16)


def attend_back_kernel(
    head_base, ids, q_ref, k_ref, v_ref, att_ref, ga_ref, lse_ref,
    made_ref, skip_ref, dq_s, dk_s, dv_s, delta_s,
):
    p = pl.program_id(0)
    width = q_ref.shape[1]
    fresh = width // 2
    bounds = doc_bounds(ids)
    place = member_at(p, ids)
    first = doc_start(p * BLOCK, bounds)
    needed = p - first // BLOCK + 1
    low = lax.broadcasted_iota(jnp.int32, (1, PAIR), 1) < HEAD
    picks = [jnp.where(low, SCALE, 0.0).astype(BF16), jnp.where(low, 0.0, SCALE).astype(BF16)]
    ones = [jnp.where(low, 1.0, 0.0).astype(BF16), jnp.where(low, 0.0, 1.0).astype(BF16)]

    @pl.when(p == 0)
    def _():
        dk_s[...] = jnp.zeros_like(dk_s)
        dv_s[...] = jnp.zeros_like(dv_s)

    product = ga_ref[...].astype(F32) * att_ref[...].astype(F32)
    high = product.astype(BF16)
    rest = (product - high.astype(F32)).astype(BF16)
    owner = lax.broadcasted_iota(jnp.int32, (delta_s.shape[0], width), 1) // HEAD
    which = lax.broadcasted_iota(jnp.int32, (delta_s.shape[0], width), 0)
    gather = (owner == which).astype(F32).astype(BF16)
    delta_s[...] = nt(gather, high) + nt(gather, rest)

    def run(count):
        span = count * BLOCK
        base = pl.multiple_of((p - count + 1) * BLOCK, BLOCK)
        row = p * BLOCK + lax.broadcasted_iota(jnp.int32, (1, BLOCK), 1)
        start = doc_start(row, bounds)
        column = base + lax.broadcasted_iota(jnp.int32, (span, 1), 0)
        seen = (column <= row) & (column >= start)
        bias = jnp.where(seen, 0.0, MASKED)

        @pl.loop(0, width // PAIR, unroll=3)
        def _(pair):
            lanes = pl.ds(pl.multiple_of(pair * PAIR, PAIR), PAIR)
            queries = q_ref[:, lanes]
            grads = ga_ref[:, lanes]
            keys = k_ref[pl.ds(base, span), lanes]
            values = v_ref[pl.ds(base, span), lanes]
            query_parts = []
            for side in range(2):
                head = 2 * pair + side
                picked = queries * picks[side]
                chosen = grads * ones[side]
                scores = nt(keys, picked) + bias
                probs = jnp.exp(scores - lse_ref[pl.ds(head_base + head, 1), :])
                dprobs = nt(values, chosen)
                dscores = (probs * (dprobs - delta_s[pl.ds(head, 1), :])).astype(BF16)
                value_part = nn(probs.astype(BF16), chosen)
                key_part = nn(dscores, picked)
                query_parts.append(tn(dscores, keys))
                if side == 0:
                    value_sum, key_sum = value_part, key_part
                else:
                    value_sum, key_sum = value_sum + value_part, key_sum + key_part
            dv_s[pl.ds(base, span), lanes] += value_sum
            dk_s[pl.ds(base, span), lanes] += key_sum
            dq_s[:, lanes] = (
                jnp.where(low, query_parts[0], query_parts[1]) * SCALE
            ).astype(BF16)

    for count in range(1, REACH + 1):
        pl.when(needed == count)(partial(run, count))

    made_ref[place, :, :width] = dq_s[...]

    @pl.when(p == pl.num_programs(0) - 1)
    def _():
        for block in range(SPAN):
            rows = slice(block * BLOCK, (block + 1) * BLOCK)
            to = member_at(block, ids)
            made_ref[to, :, width:2 * width] = dk_s[rows, :].astype(BF16)
            value_grad = dv_s[rows, :]
            made_ref[to, :, 2 * width:] = value_grad[:, :fresh].astype(BF16)
            skip_ref[to] = packed_rows(value_grad.T[fresh:, :].astype(BF16))


def weight_kernel(ids, norm_ref, made_ref, keep_ref, send_ref, sums_ref, made_s):
    rows = norm_ref[...]
    grads = made_ref[...]
    width = rows.shape[1]
    made_s[:width, :] = tn(rows, grads[:, :width])
    made_s[width:, :] = tn(grads[:, width:], rows)
    half = made_s.shape[0] // 2
    near = pl.multiple_of(ids[CORE] * half, 32)
    far = pl.multiple_of(half - ids[CORE] * half, 32)
    for target, start in ((keep_ref, near), (send_ref, far)):
        target[...] = made_s[pl.ds(start, half), :].astype(BF16)
    sums_ref[...] = jnp.sum(grads.astype(F32), axis=0, keepdims=True)


def input_kernel(
    ids, own_ref, other_ref, w_own_ref, w_other_ref, x_ref, mg_ref, skip_own_ref, skip_other_ref,
    gain_ref, *refs
):
    grad_refs, small_ref = refs[:-1], refs[-1]
    p = pl.program_id(0)
    first = None
    for made_ref, weight in ((own_ref, w_own_ref), (other_ref, w_other_ref)):
        width = weight.shape[1]
        part = nt(made_ref[:, :width], weight[:width, :]) + nn(made_ref[:, width:], weight[width:, :])
        first = part if first is None else first + part
    scaled, inverse = normed(x_ref[...].astype(F32))
    tokens, each = x_ref.shape[0], skip_own_ref.shape[0]
    made = (mg_ref[...].astype(F32) + norm_back(first, scaled, inverse, vector(gain_ref))).astype(BF16)
    for distance, grad_ref in enumerate(grad_refs):

        @pl.when(p == distance)
        def _():
            grad_ref[:tokens, :] = made
            grad_ref[tokens:tokens + each, :] = skip_own_ref[...]
            grad_ref[tokens + each:, :] = skip_other_ref[...]
    sums = jnp.concatenate(
        [jnp.sum(value, axis=0, keepdims=True) for value in (first * scaled, first)], axis=0
    )

    @pl.when(p == 0)
    def _():
        small_ref[...] = sums

    @pl.when(p > 0)
    def _():
        small_ref[...] += sums


def fold_kernel(groups, starts, ids, *refs):
    sources = sum(len(group) for group in groups)
    outs = refs[sources:-1]
    total_s = refs[-1]
    row = 0
    place = 0
    for group in groups:
        total = None
        for index in group:
            ref = refs[place]
            place += 1
            if isinstance(index, str):
                value = ref[...].astype(F32)
                value = jnp.where(ids[OUTER] % 2 == int(index), value, jnp.zeros_like(value))
            else:
                value = (ref[...] if index is None else ref[index]).astype(F32)
            total = value if total is None else total + value
        total_s[row:row + total.shape[0], :] = total
        row += total.shape[0]
    if row < total_s.shape[0]:
        total_s[row:, :] = jnp.zeros((total_s.shape[0] - row, total_s.shape[1]), F32)
    for out, start in zip(outs, starts):
        at = start(ids)
        if not isinstance(at, int):
            at = pl.multiple_of(at, 8)
        out[...] = total_s[pl.ds(at, out.shape[0]), :].astype(BF16)


def fold(ids, groups, starts, count, rows=0):
    arrays = [entry[0] for group in groups for entry in group]
    indices = tuple(tuple(entry[1] for entry in group) for group in groups)
    width = arrays[0].shape[-1]
    rows = max(rows, sum(group[0][0].shape[-2] for group in groups))
    return call(
        partial(fold_kernel, indices, starts),
        1,
        (1,),
        [full(array.shape) for array in arrays],
        [full((count, width)) for _ in starts],
        [shape_of((count, width), BF16) for _ in starts],
        scratch=[pltpu.VMEM((rows, width), F32)],
        micros=3.5,
        name="fold",
    )(ids, *arrays)


def spread_sum_kernel(ids, parts_ref, spread_ref):
    total = jnp.sum(parts_ref[...].astype(F32), axis=0).astype(BF16)
    for index in range(parts_ref.shape[0]):
        spread_ref[index] = total


def spread_sum(ids, parts):
    return call(
        spread_sum_kernel,
        1,
        (1,),
        [full(parts.shape)],
        [full(parts.shape)],
        [shape_of(parts.shape, BF16)],
        micros=2.5,
        name="spread_sum",
    )(ids, parts)[0]


def collect_kernel(ids, *refs):
    grad_ref, skip_ref = refs[-2:]
    for distance, ref in enumerate(refs[:-2]):
        place = ids[MINE] ^ distance
        grad_ref[place] = ref[:BLOCK, :].astype(F32)
        for side in range(2):
            rows = ref[BLOCK + side * HEAD:BLOCK + (side + 1) * HEAD, :].astype(F32)
            column = ((ids[TP] ^ side) * SPAN + place) * BLOCK
            columns = pl.ds(pl.multiple_of(column, BLOCK), BLOCK)
            for index in range(rows.shape[1] // BLOCK):
                skip_ref[index * HEAD:(index + 1) * HEAD, columns] = rows[
                    :, index * BLOCK:(index + 1) * BLOCK
                ]


def collect(ids, pieces):
    rows, width = pieces[0].shape
    features = width // BLOCK * HEAD
    return call(
        collect_kernel,
        1,
        (1,),
        [full((rows, width))] * len(pieces),
        [full((SPAN, BLOCK, width)), full((features, 2 * SPAN * BLOCK))],
        [shape_of((SPAN, BLOCK, width), F32), shape_of((features, 2 * SPAN * BLOCK), F32)],
        micros=5,
        name="collect",
    )(ids, *pieces)


def place_feed_kernel(ids, mine_ref, theirs_ref, up_ref, down_ref):
    units = down_ref.shape[0]
    here = pl.program_id(0) == ids[CORE]
    whole = jnp.where(here, mine_ref[...], theirs_ref[...]).astype(F32)
    up_ref[...] = whole[:units].T
    down_ref[...] = whole[units:]


def place_feed(ids, mine, theirs):
    rows, width = mine.shape
    return call(
        place_feed_kernel,
        1,
        (2,),
        [full((rows, width))] * 2,
        [
            pl.BlockSpec((width, rows // 2), lambda h, ids: (0, h)),
            pl.BlockSpec((rows // 2, width), lambda h, ids: (h, 0)),
        ],
        [shape_of((width, rows), F32), shape_of((rows, width), F32)],
        micros=8,
        name="place_feed",
    )(ids, mine, theirs)


def place_qkv_kernel(ids, mine_ref, theirs_ref, q_ref, k_ref, v_ref, out_ref):
    half = q_ref.shape[1]
    split = (q_ref.shape[0] + v_ref.shape[0]) // 2
    half_out = out_ref.shape[0] // 2
    first = ids[CORE] == 0
    mine, theirs = mine_ref[...], theirs_ref[...]
    low = jnp.where(first, mine, theirs).astype(F32)
    high = jnp.where(first, theirs, mine).astype(F32)
    out_ref[:half_out, :] = low[split:split + half_out]
    out_ref[half_out:, :] = high[split:split + half_out]
    rest = q_ref.shape[0] - split
    for ref, columns in ((q_ref, slice(0, half)), (k_ref, slice(half, 2 * half))):
        ref[:split, :] = low[:split, columns]
        ref[split:, :] = high[:rest, columns]
    v_ref[...] = high[rest:split]


def place_qkv(ids, mine, theirs, half, fresh):
    rows, width = mine.shape
    return call(
        place_qkv_kernel,
        1,
        (1,),
        [full((rows, width))] * 2,
        [full((width, half)), full((width, half)), full((fresh, width)), full((half, width))],
        [
            shape_of((width, half), F32), shape_of((width, half), F32),
            shape_of((fresh, width), F32), shape_of((half, width), F32),
        ],
        micros=4,
        name="place_qkv",
    )(ids, mine, theirs)


def tie(value, *others):
    return lax.optimization_barrier((value,) + others)[0]


def per_device(
    sizes,
    layer_in,
    skip_values,
    block_slot,
    doc_lengths,
    gain_attention,
    shift_attention,
    query_weight,
    query_bias,
    key_weight,
    value_weight,
    value_bias,
    out_weight,
    out_bias,
    gain_feed,
    shift_feed,
    up_weight,
    up_bias,
    down_weight,
    down_bias,
    out_grad,
):
    seq_count, tp_count = sizes
    width = layer_in.shape[1]
    half = query_weight.shape[1]
    fresh = value_weight.shape[1]
    units = up_weight.shape[1]
    tokens = layer_in.shape[0]
    batch = skip_values.shape[0] // BLOCK
    heads = width // HEAD
    head_rows = -(-heads // 8) * 8
    packed = 2 * half + fresh
    side = units // 2
    seq_index = lax.axis_index("seq")
    tp_index = lax.axis_index("tp")
    member = seq_index % SPAN
    group = seq_index // SPAN
    core = seq_index % 2
    members = [[g * SPAN + m for m in range(SPAN)] for g in range(seq_count // SPAN)]
    same_core = [list(range(c, seq_count, 2)) for c in range(2)]
    others = seq_count // 2
    local_seq = tp_index * (batch // tp_count) + member

    def swap_seq(value, distance):
        return lax.ppermute(value, "seq", [(i, i ^ distance) for i in range(seq_count)])

    def swap_core(value):
        return swap_seq(value, 1)

    def swap_tp(value):
        return lax.ppermute(value, "tp", [(i, i ^ 1) for i in range(tp_count)])

    def to_seqs(value):
        return lax.all_to_all(value, "seq", 0, 0, tiled=True, axis_index_groups=members)

    def either(bit, first, second):
        return jnp.where(bit == 0, first, second)

    def in_order(bit, mine, theirs):
        return either(
            bit, jnp.concatenate([mine, theirs], 0), jnp.concatenate([theirs, mine], 0)
        )

    def rows_of(value, start, count):
        return lax.dynamic_slice_in_dim(value, start, count, 0)

    def row(value):
        return value.reshape(1, -1)

    local_seq = tp_index * (batch // tp_count) + member
    slots = lax.dynamic_slice(block_slot, (group * SPAN, local_seq), (SPAN, 1))
    holders = jnp.sum(
        jnp.where(
            slots == lax.broadcasted_iota(jnp.int32, (SPAN, SPAN), 1),
            lax.broadcasted_iota(jnp.int32, (SPAN, SPAN), 0), 0,
        ),
        axis=0,
    )
    lengths = lax.dynamic_slice(doc_lengths, (group * batch + local_seq, 0), (1, DOCS))
    ends = jnp.sum(
        jnp.where(
            lax.broadcasted_iota(jnp.int32, (DOCS, DOCS), 0)
            <= lax.broadcasted_iota(jnp.int32, (DOCS, DOCS), 1),
            lengths.reshape(DOCS, 1), 0,
        ),
        axis=0,
    )
    ids = jnp.concatenate(
        [
            jnp.stack([core, member, group, tp_index]).astype(jnp.int32), holders,
            ends[:DOCS - 1],
        ]
    ).astype(jnp.int32)

    qkv_own = jnp.concatenate(
        [jnp.concatenate([query_weight, key_weight], axis=1), value_weight.T], axis=0
    )
    early_sent = jnp.concatenate(
        [
            rows_of(qkv_own, core * (packed // 2), packed // 2),
            rows_of(out_weight, core * (half // 2), half // 2),
        ],
        0,
    )
    early_near = swap_tp(early_sent)
    layer_in, skip_values = lax.optimization_barrier((layer_in, skip_values, early_sent))[:2]
    thirds = fresh // HEAD
    skip_sent = skip_values.T.reshape(thirds, HEAD, tp_count, SPAN, BLOCK)
    skip_sent = skip_sent.transpose(3, 2, 1, 0, 4).reshape(SPAN, tp_count * HEAD, thirds * BLOCK)
    blocks_in = to_seqs(layer_in.reshape(SPAN, BLOCK, width))
    up_bias_half = rows_of(up_bias, core * side, side)
    bias_own = jnp.concatenate([query_bias, value_bias, up_bias_half])
    bias_other = swap_tp(bias_own)
    feed_own = jnp.concatenate(
        [lax.dynamic_slice_in_dim(up_weight, core * side, side, 1).T,
         rows_of(down_weight, core * side, side)], 0,
    )
    feed_own, ids = lax.optimization_barrier((feed_own, ids))
    early_near, bias_other, skip_sent = lax.optimization_barrier(
        (early_near, bias_other, skip_sent, feed_own)
    )[:3]
    skip_in = to_seqs(tie(skip_sent, blocks_in))
    early_far = swap_core(early_near)
    up_part = rows_of(feed_own, group % 2 * (side // 2), side // 2)
    up_near = swap_tp(tie(up_part, early_near))

    qkv_bias = jnp.stack([bias_own[:half + fresh], bias_other[:half + fresh]])
    own_shape = (SPAN, BLOCK, width)
    flat = (tokens, width)

    norm_one, queries, keys, fresh_values, qkv_other, out_other = call(
        project_kernel,
        1,
        (SPAN,),
        [
            placed(width), full((packed, width)), full((packed // 2 + half // 2, width)),
            full((packed // 2 + half // 2, width)), full((2, half + fresh)), full((width,)), full((width,)),
        ],
        [
            placed(width), in_rows(width), in_rows(width),
            pl.BlockSpec((2, BLOCK, fresh), lambda p, *_: (0, p, 0)), full((packed, width)),
            full((half, width)),
        ],
        [
            shape_of(own_shape, BF16), shape_of(flat, BF16), shape_of(flat, BF16),
            shape_of((2, tokens, fresh), BF16), shape_of((packed, width), BF16),
            shape_of((half, width), BF16),
        ],
        micros=9,
        name="project",
    )(ids, blocks_in, qkv_own, early_near, early_far, qkv_bias, gain_attention, shift_attention)

    grad_blocks = to_seqs(tie(out_grad.reshape(SPAN, BLOCK, width), queries, skip_in))
    up_near = tie(up_near, queries)
    up_far = swap_seq(up_near, SPAN)
    skip_in = tie(skip_in, queries)
    skip_other = swap_tp(
        lax.dynamic_slice(
            skip_in, (0, (1 - tp_index) * HEAD, 0), (SPAN, HEAD, width)
        )
    )
    down_other = swap_tp(tie(feed_own[side:], skip_in))
    lse_spec = pl.BlockSpec((head_rows, BLOCK), lambda p, *_: (0, p))
    values, attended, log_total, middle, norm_two = call(
        attend_kernel,
        1,
        (SPAN,),
        [
            placed(width), in_rows(width), full(flat),
            pl.BlockSpec((2, BLOCK, fresh), lambda p, *_: (0, p, 0)),
            pl.BlockSpec(
                (None, HEAD, width),
                lambda p, ids: (member_at(p, ids), ids[TP], 0),
            ),
            placed(width, HEAD),
            full((half, width)), full((half, width)), full((width,)), full((width,)),
            full((width,)),
        ],
        [full(flat), placed(width), lse_spec, placed(width), placed(width)],
        [
            shape_of(flat, BF16), shape_of(own_shape, BF16), shape_of((head_rows, tokens), F32),
            shape_of(own_shape, BF16), shape_of(own_shape, BF16),
        ],
        scratch=[pltpu.VMEM((BLOCK, width), BF16), pltpu.VMEM((BLOCK, 128), F32)],
        micros=27,
        name="attend",
    )(
        ids, blocks_in, queries, keys, fresh_values, skip_in, skip_other, out_weight,
        out_other,        out_bias, gain_feed, shift_feed,
    )
    rows_mine = norm_two.reshape(flat)
    grads_mine = grad_blocks.reshape(flat)

    rows_theirs = swap_core(rows_mine)
    grads_theirs = swap_core(grads_mine)
    feed_other = (up_near, up_far, down_other)
    bias_here = row(up_bias_half)
    bias_there = row(bias_other[half + fresh:])
    out_mine, back_mine, bias_one, made_other = feed(
        ids, rows_mine, grads_mine, feed_other, bias_there
    )
    rows_theirs = tie(rows_theirs, out_mine)
    out_theirs, back_theirs, bias_two, *made_other = feed(
        ids, rows_theirs, grads_theirs, feed_other, bias_there, (), (made_other,), PARTS, True
    )
    cross_one = swap_tp(made_other[0])
    given = swap_seq(made_other[3], SPAN)
    out_theirs, back_theirs, bias_three, made_own = feed(
        ids, rows_theirs, grads_theirs, (feed_own,), tie(bias_here, made_other[0]),
        (out_theirs, back_theirs),
    )
    out_given = swap_core(out_theirs)
    back_given = swap_core(back_theirs)
    cross_two = swap_tp(tie(made_other[1], cross_one, out_theirs))
    given, kept = lax.optimization_barrier((given, made_other[2], out_theirs))[:2]
    pair_sum, = fold(ids, [[(kept, None), (given, None)]], [lambda ids: 0], kept.shape[0])
    out_mine, back_mine, bias_four, *made_own = feed(
        ids, rows_mine, grads_mine, (feed_own,), tie(bias_here, cross_one, pair_sum),
        (out_mine, back_mine), (made_own,), PARTS,
    )
    cross_three = swap_tp(tie(pair_sum, cross_two, out_mine))

    def scatter(value):
        parts = value.reshape(others, value.shape[0] // others, width)
        return lax.all_to_all(parts, "seq", 0, 0, tiled=True, axis_index_groups=same_core)

    def gather(parts):
        spread = spread_sum(ids, parts)
        whole = lax.all_to_all(spread, "seq", 0, 0, tiled=True, axis_index_groups=same_core)
        return whole.reshape(-1, width)

    layer_blocks, middle_grad, att_grad, out_keep, out_send, small_two = call(
        residual_kernel,
        1,
        (SPAN,),
        [in_rows(width)] * 5
        + [
            by_block(width), by_block(width), full((half, width)), full((half, width)),
            full((width,)), full((width,)),
        ],
        [
            by_block(width), by_block(width), by_block(width),
            full((2, half // 2, width)), full((2, half // 2, width)), full((4, width)),
        ],
        [
            shape_of(own_shape, BF16), shape_of(own_shape, BF16), shape_of(own_shape, BF16),
            shape_of((2, half // 2, width), BF16), shape_of((2, half // 2, width), BF16),
            shape_of((4, width), F32),
        ],
        scratch=[pltpu.VMEM((width, width), F32)],
        micros=12.5,
        name="residual",
    )(
        ids, tie(out_mine, cross_two), out_given, back_mine, back_given, grads_mine, middle, attended, out_weight,
        out_other, gain_feed, down_bias,
    )
    sent_given = swap_core(out_send)
    out_total = (out_keep.astype(F32) + sent_given.astype(F32)).astype(BF16)
    cross_three = tie(cross_three, att_grad)
    ready_feed, = fold(
        ids,
        [
            [(made_own[0], None), (cross_one, None)],
            [(made_own[1], None), (cross_two, None)],
            [(made_own[2], None), (cross_three, "0")],
            [(made_own[3], None), (cross_three, "1")],
        ],
        [lambda ids: 0],
        2 * side,
    )
    total_feed = lax.psum(ready_feed, "seq", axis_index_groups=same_core)
    def rest():
        cross_out = swap_tp(out_total[1])

        def attend_back(which, query_rows):
            return call(
                partial(attend_back_kernel, which * (heads // 2)),
                1,
                (SPAN,),
                [
                    pl.BlockSpec((BLOCK, half), lambda p, *_: (p, which)),
                    pl.BlockSpec((tokens, half), lambda p, *_: (0, which)),
                    pl.BlockSpec((tokens, half), lambda p, *_: (0, which)),
                    placed(half, column=which), placed(half, column=which), lse_spec,
                ],
                [full((SPAN, BLOCK, packed)), full((SPAN, HEAD, width))],
                [shape_of((SPAN, BLOCK, packed), BF16), shape_of((SPAN, HEAD, width), BF16)],
                scratch=[
                    pltpu.VMEM((BLOCK, half), BF16), pltpu.VMEM((tokens, half), F32),
                    pltpu.VMEM((tokens, half), F32), pltpu.VMEM((8, BLOCK), F32),
                ],
                micros=17.5,
                name="attend_back",
            )(
                ids, query_rows, keys, values, attended, att_grad,
                log_total,
            )

        qkv_rows = packed // 2
        last_rows = -(-(qkv_rows + half // 2) // 64) * 64

        def weights(made):
            return call(
                weight_kernel,
                1,
                (1,),
                [full(flat), full((tokens, packed))],
                [full((qkv_rows, width)), full((qkv_rows, width)), full((1, packed))],
                [
                    shape_of((qkv_rows, width), BF16), shape_of((qkv_rows, width), BF16),
                    shape_of((1, packed), F32),
                ],
                scratch=[pltpu.VMEM((packed, width), F32)],
                micros=6,
                name="weights",
            )(ids, norm_one.reshape(flat), made.reshape(tokens, packed))

        layer_out = to_seqs(layer_blocks).reshape(flat)
        grads_other, skip_made = attend_back(1, queries)
        keep_other, send_other, sums_other = weights(tie(grads_other, cross_out))
        given_other = swap_core(send_other)
        total_other, = fold(
            ids, [[(keep_other, None), (given_other, None)]], [lambda ids: 0], qkv_rows
        )
        cross_other = swap_tp(total_other)
        grads_own, skip_own = attend_back(0, tie(queries, total_other, layer_out))
        skip_theirs = swap_tp(tie(skip_made, grads_own))
        keep_own, send_own, sums_own = weights(tie(grads_own, cross_other))
        given_own = swap_core(send_own)

        ready_qkv, = fold(
            ids,
            [
                [(keep_own, None), (given_own, None), (cross_other, None)],
                [(out_total, 0), (cross_out, None)],
            ],
            [lambda ids: 0],
            last_rows,
            last_rows,
        )
        parts_qkv = scatter(ready_qkv)
        def by_distance(columns, rows=BLOCK):
            return pl.BlockSpec((None, rows, columns), lambda p, ids: (ids[MINE] ^ p, 0, 0))

        *input_blocks, small_one = call(
            input_kernel,
            1,
            (SPAN,),
            [
                by_distance(packed), by_distance(packed), full((packed, width)),
                full((packed, width)), by_distance(width), by_distance(width),
                by_distance(width, HEAD), by_distance(width, HEAD), full((width,)),
            ],
            [full((BLOCK + 2 * HEAD, width))] * SPAN + [full((2, width))],
            [shape_of((BLOCK + 2 * HEAD, width), BF16)] * SPAN + [shape_of((2, width), F32)],
            micros=9,
            name="input",
        )(
            ids, tie(grads_own, ready_qkv), grads_other, qkv_own, qkv_other, blocks_in, middle_grad,
            skip_own, skip_theirs, gain_attention,
        )
        back = [input_blocks[0]] + [
            swap_seq(input_blocks[distance], distance) for distance in range(1, SPAN)
        ]
        shared = jnp.concatenate([small_one.reshape(-1), small_two.reshape(-1)])
        widened = lambda value: jnp.where(
            lax.broadcasted_iota(jnp.int32, (2, 1), 0) == core, value, 0.0
        ).reshape(-1)
        split_own = jnp.concatenate([sums_own.reshape(-1), widened(bias_three + bias_four)])
        split_other = jnp.concatenate([sums_other.reshape(-1), widened(bias_one + bias_two)])
        vector_own = jnp.concatenate([shared, split_own])
        vector_other = jnp.concatenate([shared, split_other])

        vectors = vector_own + swap_tp(vector_other)
        for distance in [1] + [SPAN << bit for bit in range((seq_count // SPAN).bit_length() - 1)]:
            vectors = vectors + swap_seq(vectors, distance)
        parts_qkv, *back = lax.optimization_barrier((parts_qkv, vectors, *back))
        vectors = back.pop(0)
        return (layer_out, parts_qkv, vectors, *back)

    shapes = jax.eval_shape(rest)
    results = lax.cond(
        jnp.min(lengths) > 0, rest, lambda: tuple(jnp.zeros(s.shape, s.dtype) for s in shapes)
    )
    layer_out, parts_qkv, vectors, *back = results
    late = ids + (vectors[0] * 0.0).astype(jnp.int32)
    whole_qkv = gather(parts_qkv)
    total_feed = tie(total_feed, late)
    far_feed = swap_core(total_feed)
    input_grad, skip_grad = collect(ids, back)
    input_grad, skip_grad = input_grad.reshape(flat), skip_grad.T
    vectors = vectors + swap_seq(vectors, 2)
    grad_up_weight, grad_down_weight = place_feed(late, total_feed, far_feed)
    whole_qkv, vectors = lax.optimization_barrier(
        (whole_qkv, vectors, grad_up_weight, input_grad, skip_grad)
    )[:2]
    grad_query, grad_key, grad_value, grad_out_weight = place_qkv(
        ids, whole_qkv, swap_core(whole_qkv), half, fresh
    )
    shared = vectors[:6 * width].reshape(6, width)
    split = vectors[6 * width:]

    return (
        layer_out,
        input_grad,
        skip_grad,
        shared[0],
        shared[1],
        grad_query,
        split[:half],
        grad_key,
        grad_value.T,
        split[2 * half:packed],
        grad_out_weight,
        shared[4],
        shared[2],
        shared[3],
        grad_up_weight,
        split[packed:],
        grad_down_weight,
        shared[5],
    )


def solution(mesh):
    return jax.shard_map(
        partial(per_device, (mesh.shape["seq"], mesh.shape["tp"])),
        mesh=mesh,
        in_specs=(
            P(("seq", "tp"), None),
            P("seq", "tp"),
            P(),
            P(),
            P(),
            P(),
            P(None, "tp"),
            P("tp"),
            P(None, "tp"),
            P(None, "tp"),
            P("tp"),
            P("tp", None),
            P(),
            P(),
            P(),
            P(None, "tp"),
            P("tp"),
            P("tp", None),
            P(),
            P(("seq", "tp"), None),
        ),
        out_specs=(
            P(("seq", "tp"), None),
            P(("seq", "tp"), None),
            P("seq", "tp"),
            P(),
            P(),
            P(None, "tp"),
            P("tp"),
            P(None, "tp"),
            P(None, "tp"),
            P("tp"),
            P("tp", None),
            P(),
            P(),
            P(),
            P(None, "tp"),
            P("tp"),
            P("tp", None),
            P(),
        ),
        check_vma=False,
    )
```

```python
from functools import partial

import jax
import jax.numpy as jnp
from jax import lax
from jax.experimental import pallas as pl
from jax.experimental.pallas import tpu as pltpu
from jax.sharding import PartitionSpec as P

HEAD = 64
SEQ_LEN = 1024
BLOCK = 256
LONGEST = 512
SPAN = SEQ_LEN // BLOCK
REACH = -(-LONGEST // BLOCK) + 1
PAIR = 2 * HEAD
EPSILON = 1e-05
MASKED = -1e30
GELU_A = 0.7978845608028654
GELU_B = 0.044715
SCALE = HEAD ** (-0.5)
DOCS = 4
PARTS = 4
CORE, MINE, OUTER, TP, MEMBER = 0, 1, 2, 3, 4
BOUND = MEMBER + SPAN
PEAK = 1.15e9
VMEM = 56 * 1024 * 1024

F32 = jnp.float32
BF16 = jnp.bfloat16


def nn(left, right):
    return lax.dot_general(left, right, (((1,), (0,)), ((), ())), preferred_element_type=F32)


def nt(left, right):
    return lax.dot_general(left, right, (((1,), (1,)), ((), ())), preferred_element_type=F32)


def tn(left, right):
    return lax.dot_general(left, right, (((0,), (0,)), ((), ())), preferred_element_type=F32)


def vector(ref):
    return ref[...].reshape(1, -1)


def normed(rows):
    centred = rows - jnp.mean(rows, axis=-1, keepdims=True)
    inverse = lax.rsqrt(jnp.mean(centred * centred, axis=-1, keepdims=True) + EPSILON)
    return centred * inverse, inverse


def norm_back(grad_out, scaled, inverse, gain):
    grad_scaled = grad_out * gain
    first_mean = jnp.mean(grad_scaled, axis=-1, keepdims=True)
    second_mean = jnp.mean(grad_scaled * scaled, axis=-1, keepdims=True)
    return inverse * (grad_scaled - first_mean - scaled * second_mean)


def full(shape):
    return pl.BlockSpec(shape, lambda *_: (0,) * len(shape), pipeline_mode=pl.Buffered(1))


def member_at(p, ids):
    return ids[MEMBER + p]


def doc_bounds(ids):
    return [ids[BOUND + index] for index in range(DOCS - 1)]


def placed(columns, rows=BLOCK, column=0):
    return pl.BlockSpec(
        (None, rows, columns), lambda p, ids: (member_at(p, ids), 0, column)
    )


def in_rows(columns):
    return pl.BlockSpec((BLOCK, columns), lambda p, *_: (p, 0))


def by_block(columns):
    return pl.BlockSpec((None, BLOCK, columns), lambda p, *_: (p, 0, 0))


def shape_of(shape, dtype):
    return jax.ShapeDtypeStruct(shape, dtype)


def call(kernel, scalars, grid, ins, outs, out_shapes, scratch=(), micros=1, name=None,
         aliases=None):
    return pl.pallas_call(
        kernel,
        grid_spec=pltpu.PrefetchScalarGridSpec(
            num_scalar_prefetch=scalars,
            grid=grid,
            in_specs=ins,
            out_specs=outs,
            scratch_shapes=scratch,
        ),
        out_shape=out_shapes,
        compiler_params=pltpu.CompilerParams(
            dimension_semantics=("arbitrary",) * len(grid), vmem_limit_bytes=VMEM
        ),
        cost_estimate=pl.CostEstimate(
            flops=int(micros * PEAK), bytes_accessed=int(micros * PEAK) // 1000, transcendentals=0
        ),
        input_output_aliases=aliases or {},
        name=name,
    )


def project_kernel(
    ids, x_ref, own_ref, near_ref, far_ref, bias_ref, gain_ref, shift_ref,
    norm_ref, q_ref, k_ref, fresh_ref, other_ref, out_ref,
):
    half = q_ref.shape[1] // 2
    fresh = half // 2
    split = other_ref.shape[0] // 2

    @pl.when(pl.program_id(0) == 0)
    def _():
        first = ids[CORE] == 0
        near, far = near_ref[...], far_ref[...]
        low, high = jnp.where(first, near, far), jnp.where(first, far, near)
        other_ref[:split, :] = low[:split]
        other_ref[split:, :] = high[:split]
        out_ref[:half // 2, :] = low[split:]
        out_ref[half // 2:, :] = high[split:]

    scaled, _ = normed(x_ref[...].astype(F32))
    rows = (scaled * vector(gain_ref) + vector(shift_ref)).astype(BF16)
    norm_ref[...] = rows
    for side, weight in enumerate((own_ref, other_ref)):
        made = nn(rows, weight[:2 * half, :])
        value = nt(rows, weight[2 * half:, :])
        columns = slice(side * half, (side + 1) * half)
        q_ref[:, columns] = (made[:, :half] + bias_ref[side:side + 1, :half]).astype(BF16)
        k_ref[:, columns] = made[:, half:].astype(BF16)
        fresh_ref[side] = (value + bias_ref[side:side + 1, half:half + fresh]).astype(BF16)


def unpacked(value):
    return jnp.concatenate(
        [value[:, start:start + BLOCK] for start in range(0, value.shape[1], BLOCK)], axis=0
    ).T


def packed_rows(value):
    return jnp.concatenate(
        [value[start:start + HEAD] for start in range(0, value.shape[0], HEAD)], axis=1
    )


def doc_start(position, bounds):
    start = jnp.zeros_like(position)
    for bound in bounds:
        start = jnp.where(position >= bound, bound, start)
    return start


def attend_kernel(
    ids, x_ref, q_ref, k_ref, fresh_ref, skip_own_ref, skip_other_ref, own_ref, other_ref,
    bias_ref, gain_ref, shift_ref, v_ref, att_ref, lse_ref, middle_ref, norm_ref, att_s, lse_s,
):
    p = pl.program_id(0)
    bounds = doc_bounds(ids)
    skip_own, skip_other = unpacked(skip_own_ref[...]), unpacked(skip_other_ref[...])
    v_ref[pl.ds(pl.multiple_of(p * BLOCK, BLOCK), BLOCK), :] = jnp.concatenate(
        [fresh_ref[0], skip_own, fresh_ref[1], skip_other], axis=1
    )
    width = q_ref.shape[1]
    half = width // 2
    first = doc_start(p * BLOCK, bounds)
    needed = p - first // BLOCK + 1
    lane = lax.broadcasted_iota(jnp.int32, (1, PAIR), 1)
    low = lane < HEAD
    picks = [jnp.where(low, SCALE, 0.0).astype(BF16), jnp.where(low, 0.0, SCALE).astype(BF16)]

    def run(count):
        span = count * BLOCK
        base = pl.multiple_of((p - count + 1) * BLOCK, BLOCK)
        row = p * BLOCK + lax.broadcasted_iota(jnp.int32, (BLOCK, 1), 0)
        start = doc_start(row, bounds)
        column = base + lax.broadcasted_iota(jnp.int32, (1, span), 1)
        seen = (column <= row) & (column >= start)
        bias = jnp.where(seen, 0.0, MASKED)
        head_lane = lax.broadcasted_iota(jnp.int32, (1, 128), 1)

        @pl.loop(0, width // PAIR, unroll=6)
        def _(pair):
            lanes = pl.ds(pl.multiple_of(pair * PAIR, PAIR), PAIR)
            queries = q_ref[:, lanes]
            keys = k_ref[pl.ds(base, span), lanes]
            values = v_ref[pl.ds(base, span), lanes]
            outs = []
            for side in range(2):
                scores = nt(queries * picks[side], keys) + bias
                top = jnp.max(scores, axis=1, keepdims=True)
                probs = jnp.exp(scores - top)
                total = jnp.sum(probs, axis=1, keepdims=True)
                outs.append(nn(probs.astype(BF16), values) / total)
                lse_s[...] = jnp.where(
                    head_lane == 2 * pair + side, top + jnp.log(total), lse_s[...]
                )
            att_s[:, lanes] = jnp.where(low, outs[0], outs[1]).astype(BF16)

    for count in range(1, REACH + 1):
        pl.when(needed == count)(partial(run, count))

    lse_ref[...] = lse_s[...].T[:lse_ref.shape[0], :]
    attended = att_s[...]
    att_ref[...] = attended
    middle = (
        x_ref[...].astype(F32)
        + nn(attended[:, :half], own_ref[...])
        + nn(attended[:, half:], other_ref[...])
        + vector(bias_ref)
    )
    middle_ref[...] = middle.astype(BF16)
    scaled, _ = normed(middle)
    norm_ref[...] = (scaled * vector(gain_ref) + vector(shift_ref)).astype(BF16)


def feed_kernel(fetched, has_sums, has_grads, swapped, ids, *refs):
    norm_ref, grad_ref = refs[:2]
    if fetched:
        mine_ref, theirs_ref, down_ref, bias_ref = refs[2:6]
        refs = refs[6:]
        first = ids[OUTER] % 2 == 0
        mine, theirs = mine_ref[...], theirs_ref[...]
        up = jnp.concatenate(
            [jnp.where(first, mine, theirs), jnp.where(first, theirs, mine)], axis=0
        )
        down = down_ref[...]
    else:
        weight_ref, bias_ref = refs[2:4]
        refs = refs[4:]
        up = weight_ref[:weight_ref.shape[0] // 2, :]
        down = weight_ref[weight_ref.shape[0] // 2:, :]
    units = up.shape[0]
    if has_sums:
        out_in, back_in = refs[:2]
        refs = refs[2:]
    if has_grads:
        made_in = refs[0]
        refs = refs[1:]
    out_ref, back_ref, gb_ref = refs[:3]
    made_refs = refs[3:]
    rows = norm_ref[...]
    grads = grad_ref[...]
    hidden = nt(rows, up) + bias_ref[...]
    square = hidden * hidden
    curve = jnp.tanh(hidden * (GELU_A + GELU_A * GELU_B * square))
    plus = 0.5 + 0.5 * curve
    value = hidden * plus
    active = value.astype(BF16)
    slope = plus + value * (1.0 - curve) * (GELU_A + 3.0 * GELU_A * GELU_B * square)
    hidden_grad = nt(grads, down) * slope
    gb_ref[...] = jnp.sum(hidden_grad, axis=0, keepdims=True)
    hidden_low = hidden_grad.astype(BF16)
    out = nn(active, down)
    back = nn(hidden_low, up)
    if has_sums:
        out = out + out_in[...].astype(F32)
        back = back + back_in[...].astype(F32)
    out_ref[...] = out.astype(BF16)
    back_ref[...] = back.astype(BF16)
    for piece, left, right in (
        (slice(0, units), hidden_low, rows), (slice(units, 2 * units), active, grads)
    ):
        made = tn(left, right)
        if has_grads:
            made = made + made_in[piece, :].astype(F32)
        made = made.astype(BF16)
        count = made_refs[0].shape[0]
        for row in range(piece.start, piece.stop, count):
            part = made_refs[row // count]
            if count > units:
                part[piece, :] = made
            elif swapped and piece.start > 0:
                near = made[row - piece.start:row - piece.start + count]
                far = made[units - count - row + piece.start:units - row + piece.start]
                part[...] = jnp.where(ids[OUTER] % 2 == 0, near, far)
            else:
                part[...] = made[row - piece.start:row - piece.start + count]


def feed(ids, rows, grads, weights, bias, sums=(), made=(), parts=1,
         swapped=False):
    tokens, width = rows.shape
    units = bias.shape[1]
    total = full((tokens, width))
    return call(
        partial(feed_kernel, len(weights) > 1, len(sums) > 0, len(made) > 0, swapped),
        1,
        (1,),
        [total, total] + [full(weight.shape) for weight in weights] + [full((1, units))]
        + [total] * len(sums) + [full((2 * units, width))] * len(made),
        [total, total, full((1, units))] + [full((2 * units // parts, width))] * parts,
        [
            shape_of((tokens, width), BF16), shape_of((tokens, width), BF16),
            shape_of((1, units), F32),
        ] + [shape_of((2 * units // parts, width), BF16)] * parts,
        micros=14,
        name="feed",
    )(ids, rows, grads, *weights, bias, *sums, *made)


def residual_kernel(
    ids, out_a, out_b, back_a, back_b, grad_ref, middle_ref, att_ref, own_ref, other_ref,
    gain_ref, down_bias_ref, layer_ref, mg_ref, ga_ref, keep_ref, send_ref, small_ref, acc_s,
):
    p = pl.program_id(0)
    half = own_ref.shape[0]
    middle = middle_ref[...].astype(F32)
    summed = lambda refs: sum(ref[...].astype(F32) for ref in refs)
    layer_ref[...] = (middle + summed((out_a, out_b)) + vector(down_bias_ref)).astype(BF16)
    scaled, inverse = normed(middle)
    second = summed((back_a, back_b))
    out_grad = grad_ref[...].astype(F32)
    middle_grad = out_grad + norm_back(second, scaled, inverse, vector(gain_ref))
    low = middle_grad.astype(BF16)
    mg_ref[...] = low
    ga_ref[:, :half] = nt(low, own_ref[...]).astype(BF16)
    ga_ref[:, half:] = nt(low, other_ref[...]).astype(BF16)
    weight_grad = tn(att_ref[...], low)
    sums = jnp.concatenate(
        [
            jnp.sum(value, axis=0, keepdims=True)
            for value in (second * scaled, second, middle_grad, out_grad)
        ],
        axis=0,
    )

    @pl.when(p == 0)
    def _():
        acc_s[...] = weight_grad
        small_ref[...] = sums

    @pl.when(p > 0)
    def _():
        acc_s[...] += weight_grad
        small_ref[...] += sums

    @pl.when(p == pl.num_programs(0) - 1)
    def _():
        rows = half // 2
        near = pl.multiple_of(ids[CORE] * rows, 32)
        far = pl.multiple_of(rows - ids[CORE] * rows, 32)
        for side in range(2):
            keep_ref[side] = acc_s[pl.ds(side * half + near, rows), :].astype(BF16)
            send_ref[side] = acc_s[pl.ds(side * half + far, rows), :].astype(BF16)


def attend_back_kernel(
    head_base, ids, q_ref, k_ref, v_ref, att_ref, ga_ref, lse_ref,
    made_ref, skip_ref, dq_s, dk_s, dv_s, delta_s,
):
    p = pl.program_id(0)
    width = q_ref.shape[1]
    fresh = width // 2
    bounds = doc_bounds(ids)
    place = member_at(p, ids)
    first = doc_start(p * BLOCK, bounds)
    needed = p - first // BLOCK + 1
    low = lax.broadcasted_iota(jnp.int32, (1, PAIR), 1) < HEAD
    picks = [jnp.where(low, SCALE, 0.0).astype(BF16), jnp.where(low, 0.0, SCALE).astype(BF16)]
    ones = [jnp.where(low, 1.0, 0.0).astype(BF16), jnp.where(low, 0.0, 1.0).astype(BF16)]

    @pl.when(p == 0)
    def _():
        dk_s[...] = jnp.zeros_like(dk_s)
        dv_s[...] = jnp.zeros_like(dv_s)

    product = ga_ref[...].astype(F32) * att_ref[...].astype(F32)
    high = product.astype(BF16)
    rest = (product - high.astype(F32)).astype(BF16)
    owner = lax.broadcasted_iota(jnp.int32, (delta_s.shape[0], width), 1) // HEAD
    which = lax.broadcasted_iota(jnp.int32, (delta_s.shape[0], width), 0)
    gather = (owner == which).astype(F32).astype(BF16)
    delta_s[...] = nt(gather, high) + nt(gather, rest)

    def run(count):
        span = count * BLOCK
        base = pl.multiple_of((p - count + 1) * BLOCK, BLOCK)
        row = p * BLOCK + lax.broadcasted_iota(jnp.int32, (1, BLOCK), 1)
        start = doc_start(row, bounds)
        column = base + lax.broadcasted_iota(jnp.int32, (span, 1), 0)
        seen = (column <= row) & (column >= start)
        bias = jnp.where(seen, 0.0, MASKED)

        @pl.loop(0, width // PAIR, unroll=3)
        def _(pair):
            lanes = pl.ds(pl.multiple_of(pair * PAIR, PAIR), PAIR)
            queries = q_ref[:, lanes]
            grads = ga_ref[:, lanes]
            keys = k_ref[pl.ds(base, span), lanes]
            values = v_ref[pl.ds(base, span), lanes]
            query_parts = []
            for side in range(2):
                head = 2 * pair + side
                picked = queries * picks[side]
                chosen = grads * ones[side]
                scores = nt(keys, picked) + bias
                probs = jnp.exp(scores - lse_ref[pl.ds(head_base + head, 1), :])
                dprobs = nt(values, chosen)
                dscores = (probs * (dprobs - delta_s[pl.ds(head, 1), :])).astype(BF16)
                value_part = nn(probs.astype(BF16), chosen)
                key_part = nn(dscores, picked)
                query_parts.append(tn(dscores, keys))
                if side == 0:
                    value_sum, key_sum = value_part, key_part
                else:
                    value_sum, key_sum = value_sum + value_part, key_sum + key_part
            dv_s[pl.ds(base, span), lanes] += value_sum
            dk_s[pl.ds(base, span), lanes] += key_sum
            dq_s[:, lanes] = (
                jnp.where(low, query_parts[0], query_parts[1]) * SCALE
            ).astype(BF16)

    for count in range(1, REACH + 1):
        pl.when(needed == count)(partial(run, count))

    made_ref[place, :, :width] = dq_s[...]

    @pl.when(p == pl.num_programs(0) - 1)
    def _():
        for block in range(SPAN):
            rows = slice(block * BLOCK, (block + 1) * BLOCK)
            to = member_at(block, ids)
            made_ref[to, :, width:2 * width] = dk_s[rows, :].astype(BF16)
            value_grad = dv_s[rows, :]
            made_ref[to, :, 2 * width:] = value_grad[:, :fresh].astype(BF16)
            skip_ref[to] = packed_rows(value_grad.T[fresh:, :].astype(BF16))


def weight_kernel(ids, norm_ref, made_ref, keep_ref, send_ref, sums_ref, made_s):
    rows = norm_ref[...]
    grads = made_ref[...]
    width = rows.shape[1]
    made_s[:width, :] = tn(rows, grads[:, :width])
    made_s[width:, :] = tn(grads[:, width:], rows)
    half = made_s.shape[0] // 2
    near = pl.multiple_of(ids[CORE] * half, 32)
    far = pl.multiple_of(half - ids[CORE] * half, 32)
    for target, start in ((keep_ref, near), (send_ref, far)):
        target[...] = made_s[pl.ds(start, half), :].astype(BF16)
    sums_ref[...] = jnp.sum(grads.astype(F32), axis=0, keepdims=True)


def input_kernel(
    ids, own_ref, other_ref, w_own_ref, w_other_ref, x_ref, mg_ref, skip_own_ref, skip_other_ref,
    gain_ref, *refs
):
    grad_refs, small_ref = refs[:-1], refs[-1]
    p = pl.program_id(0)
    first = None
    for made_ref, weight in ((own_ref, w_own_ref), (other_ref, w_other_ref)):
        width = weight.shape[1]
        part = nt(made_ref[:, :width], weight[:width, :]) + nn(made_ref[:, width:], weight[width:, :])
        first = part if first is None else first + part
    scaled, inverse = normed(x_ref[...].astype(F32))
    tokens, each = x_ref.shape[0], skip_own_ref.shape[0]
    made = (mg_ref[...].astype(F32) + norm_back(first, scaled, inverse, vector(gain_ref))).astype(BF16)
    for distance, grad_ref in enumerate(grad_refs):

        @pl.when(p == distance)
        def _():
            grad_ref[:tokens, :] = made
            grad_ref[tokens:tokens + each, :] = skip_own_ref[...]
            grad_ref[tokens + each:, :] = skip_other_ref[...]
    sums = jnp.concatenate(
        [jnp.sum(value, axis=0, keepdims=True) for value in (first * scaled, first)], axis=0
    )

    @pl.when(p == 0)
    def _():
        small_ref[...] = sums

    @pl.when(p > 0)
    def _():
        small_ref[...] += sums


def fold_kernel(groups, starts, ids, *refs):
    sources = sum(len(group) for group in groups)
    outs = refs[sources:-1]
    total_s = refs[-1]
    row = 0
    place = 0
    for group in groups:
        total = None
        for index in group:
            ref = refs[place]
            place += 1
            if isinstance(index, str):
                value = ref[...].astype(F32)
                value = jnp.where(ids[OUTER] % 2 == int(index), value, jnp.zeros_like(value))
            else:
                value = (ref[...] if index is None else ref[index]).astype(F32)
            total = value if total is None else total + value
        total_s[row:row + total.shape[0], :] = total
        row += total.shape[0]
    if row < total_s.shape[0]:
        total_s[row:, :] = jnp.zeros((total_s.shape[0] - row, total_s.shape[1]), F32)
    for out, start in zip(outs, starts):
        at = start(ids)
        if not isinstance(at, int):
            at = pl.multiple_of(at, 8)
        out[...] = total_s[pl.ds(at, out.shape[0]), :].astype(BF16)


def fold(ids, groups, starts, count, rows=0):
    arrays = [entry[0] for group in groups for entry in group]
    indices = tuple(tuple(entry[1] for entry in group) for group in groups)
    width = arrays[0].shape[-1]
    rows = max(rows, sum(group[0][0].shape[-2] for group in groups))
    return call(
        partial(fold_kernel, indices, starts),
        1,
        (1,),
        [full(array.shape) for array in arrays],
        [full((count, width)) for _ in starts],
        [shape_of((count, width), BF16) for _ in starts],
        scratch=[pltpu.VMEM((rows, width), F32)],
        micros=3.5,
        name="fold",
    )(ids, *arrays)


def spread_sum_kernel(ids, parts_ref, spread_ref):
    total = jnp.sum(parts_ref[...].astype(F32), axis=0).astype(BF16)
    for index in range(parts_ref.shape[0]):
        spread_ref[index] = total


def spread_sum(ids, parts):
    return call(
        spread_sum_kernel,
        1,
        (1,),
        [full(parts.shape)],
        [full(parts.shape)],
        [shape_of(parts.shape, BF16)],
        micros=2.5,
        name="spread_sum",
    )(ids, parts)[0]


def collect_kernel(ids, *refs):
    grad_ref, skip_ref = refs[-2:]
    for distance, ref in enumerate(refs[:-2]):
        place = ids[MINE] ^ distance
        grad_ref[place] = ref[:BLOCK, :].astype(F32)
        for side in range(2):
            rows = ref[BLOCK + side * HEAD:BLOCK + (side + 1) * HEAD, :].astype(F32)
            column = ((ids[TP] ^ side) * SPAN + place) * BLOCK
            columns = pl.ds(pl.multiple_of(column, BLOCK), BLOCK)
            for index in range(rows.shape[1] // BLOCK):
                skip_ref[index * HEAD:(index + 1) * HEAD, columns] = rows[
                    :, index * BLOCK:(index + 1) * BLOCK
                ]


def collect(ids, pieces):
    rows, width = pieces[0].shape
    features = width // BLOCK * HEAD
    return call(
        collect_kernel,
        1,
        (1,),
        [full((rows, width))] * len(pieces),
        [full((SPAN, BLOCK, width)), full((features, 2 * SPAN * BLOCK))],
        [shape_of((SPAN, BLOCK, width), F32), shape_of((features, 2 * SPAN * BLOCK), F32)],
        micros=5,
        name="collect",
    )(ids, *pieces)


def place_feed_kernel(ids, mine_ref, theirs_ref, up_ref, down_ref):
    units = down_ref.shape[0]
    here = pl.program_id(0) == ids[CORE]
    whole = jnp.where(here, mine_ref[...], theirs_ref[...]).astype(F32)
    up_ref[...] = whole[:units].T
    down_ref[...] = whole[units:]


def place_feed(ids, mine, theirs):
    rows, width = mine.shape
    return call(
        place_feed_kernel,
        1,
        (2,),
        [full((rows, width))] * 2,
        [
            pl.BlockSpec((width, rows // 2), lambda h, ids: (0, h)),
            pl.BlockSpec((rows // 2, width), lambda h, ids: (h, 0)),
        ],
        [shape_of((width, rows), F32), shape_of((rows, width), F32)],
        micros=8,
        name="place_feed",
    )(ids, mine, theirs)


def place_qkv_kernel(ids, mine_ref, theirs_ref, q_ref, k_ref, v_ref, out_ref):
    half = q_ref.shape[1]
    split = (q_ref.shape[0] + v_ref.shape[0]) // 2
    half_out = out_ref.shape[0] // 2
    first = ids[CORE] == 0
    mine, theirs = mine_ref[...], theirs_ref[...]
    low = jnp.where(first, mine, theirs).astype(F32)
    high = jnp.where(first, theirs, mine).astype(F32)
    out_ref[:half_out, :] = low[split:split + half_out]
    out_ref[half_out:, :] = high[split:split + half_out]
    rest = q_ref.shape[0] - split
    for ref, columns in ((q_ref, slice(0, half)), (k_ref, slice(half, 2 * half))):
        ref[:split, :] = low[:split, columns]
        ref[split:, :] = high[:rest, columns]
    v_ref[...] = high[rest:split]


def place_qkv(ids, mine, theirs, half, fresh):
    rows, width = mine.shape
    return call(
        place_qkv_kernel,
        1,
        (1,),
        [full((rows, width))] * 2,
        [full((width, half)), full((width, half)), full((fresh, width)), full((half, width))],
        [
            shape_of((width, half), F32), shape_of((width, half), F32),
            shape_of((fresh, width), F32), shape_of((half, width), F32),
        ],
        micros=4,
        name="place_qkv",
    )(ids, mine, theirs)


def tie(value, *others):
    return lax.optimization_barrier((value,) + others)[0]


def per_device(
    sizes,
    layer_in,
    skip_values,
    block_slot,
    doc_lengths,
    gain_attention,
    shift_attention,
    query_weight,
    query_bias,
    key_weight,
    value_weight,
    value_bias,
    out_weight,
    out_bias,
    gain_feed,
    shift_feed,
    up_weight,
    up_bias,
    down_weight,
    down_bias,
    out_grad,
):
    seq_count, tp_count = sizes
    width = layer_in.shape[1]
    half = query_weight.shape[1]
    fresh = value_weight.shape[1]
    units = up_weight.shape[1]
    tokens = layer_in.shape[0]
    batch = skip_values.shape[0] // BLOCK
    heads = width // HEAD
    head_rows = -(-heads // 8) * 8
    packed = 2 * half + fresh
    side = units // 2
    seq_index = lax.axis_index("seq")
    tp_index = lax.axis_index("tp")
    member = seq_index % SPAN
    group = seq_index // SPAN
    core = seq_index % 2
    members = [[g * SPAN + m for m in range(SPAN)] for g in range(seq_count // SPAN)]
    same_core = [list(range(c, seq_count, 2)) for c in range(2)]
    others = seq_count // 2
    local_seq = tp_index * (batch // tp_count) + member

    def swap_seq(value, distance):
        return lax.ppermute(value, "seq", [(i, i ^ distance) for i in range(seq_count)])

    def swap_core(value):
        return swap_seq(value, 1)

    def swap_tp(value):
        return lax.ppermute(value, "tp", [(i, i ^ 1) for i in range(tp_count)])

    def to_seqs(value):
        return lax.all_to_all(value, "seq", 0, 0, tiled=True, axis_index_groups=members)

    def either(bit, first, second):
        return jnp.where(bit == 0, first, second)

    def in_order(bit, mine, theirs):
        return either(
            bit, jnp.concatenate([mine, theirs], 0), jnp.concatenate([theirs, mine], 0)
        )

    def rows_of(value, start, count):
        return lax.dynamic_slice_in_dim(value, start, count, 0)

    def row(value):
        return value.reshape(1, -1)

    local_seq = tp_index * (batch // tp_count) + member
    slots = lax.dynamic_slice(block_slot, (group * SPAN, local_seq), (SPAN, 1))
    holders = jnp.sum(
        jnp.where(
            slots == lax.broadcasted_iota(jnp.int32, (SPAN, SPAN), 1),
            lax.broadcasted_iota(jnp.int32, (SPAN, SPAN), 0), 0,
        ),
        axis=0,
    )
    lengths = lax.dynamic_slice(doc_lengths, (group * batch + local_seq, 0), (1, DOCS))
    ends = jnp.sum(
        jnp.where(
            lax.broadcasted_iota(jnp.int32, (DOCS, DOCS), 0)
            <= lax.broadcasted_iota(jnp.int32, (DOCS, DOCS), 1),
            lengths.reshape(DOCS, 1), 0,
        ),
        axis=0,
    )
    ids = jnp.concatenate(
        [
            jnp.stack([core, member, group, tp_index]).astype(jnp.int32), holders,
            ends[:DOCS - 1],
        ]
    ).astype(jnp.int32)

    qkv_own = jnp.concatenate(
        [jnp.concatenate([query_weight, key_weight], axis=1), value_weight.T], axis=0
    )
    early_sent = jnp.concatenate(
        [
            rows_of(qkv_own, core * (packed // 2), packed // 2),
            rows_of(out_weight, core * (half // 2), half // 2),
        ],
        0,
    )
    early_near = swap_tp(early_sent)
    layer_in, skip_values = lax.optimization_barrier((layer_in, skip_values, early_sent))[:2]
    thirds = fresh // HEAD
    skip_sent = skip_values.T.reshape(thirds, HEAD, tp_count, SPAN, BLOCK)
    skip_sent = skip_sent.transpose(3, 2, 1, 0, 4).reshape(SPAN, tp_count * HEAD, thirds * BLOCK)
    blocks_in = to_seqs(layer_in.reshape(SPAN, BLOCK, width))
    up_bias_half = rows_of(up_bias, core * side, side)
    bias_own = jnp.concatenate([query_bias, value_bias, up_bias_half])
    bias_other = swap_tp(bias_own)
    feed_own = jnp.concatenate(
        [lax.dynamic_slice_in_dim(up_weight, core * side, side, 1).T,
         rows_of(down_weight, core * side, side)], 0,
    )
    feed_own, ids = lax.optimization_barrier((feed_own, ids))
    early_near, bias_other, skip_sent = lax.optimization_barrier(
        (early_near, bias_other, skip_sent, feed_own)
    )[:3]
    skip_in = to_seqs(tie(skip_sent, blocks_in))
    early_far = swap_core(early_near)
    up_part = rows_of(feed_own, group % 2 * (side // 2), side // 2)
    up_near = swap_tp(tie(up_part, early_near))

    qkv_bias = jnp.stack([bias_own[:half + fresh], bias_other[:half + fresh]])
    own_shape = (SPAN, BLOCK, width)
    flat = (tokens, width)

    norm_one, queries, keys, fresh_values, qkv_other, out_other = call(
        project_kernel,
        1,
        (SPAN,),
        [
            placed(width), full((packed, width)), full((packed // 2 + half // 2, width)),
            full((packed // 2 + half // 2, width)), full((2, half + fresh)), full((width,)), full((width,)),
        ],
        [
            placed(width), in_rows(width), in_rows(width),
            pl.BlockSpec((2, BLOCK, fresh), lambda p, *_: (0, p, 0)), full((packed, width)),
            full((half, width)),
        ],
        [
            shape_of(own_shape, BF16), shape_of(flat, BF16), shape_of(flat, BF16),
            shape_of((2, tokens, fresh), BF16), shape_of((packed, width), BF16),
            shape_of((half, width), BF16),
        ],
        micros=9,
        name="project",
    )(ids, blocks_in, qkv_own, early_near, early_far, qkv_bias, gain_attention, shift_attention)

    grad_blocks = to_seqs(tie(out_grad.reshape(SPAN, BLOCK, width), queries, skip_in))
    up_near = tie(up_near, queries)
    up_far = swap_seq(up_near, SPAN)
    skip_in = tie(skip_in, queries)
    skip_other = swap_tp(
        lax.dynamic_slice(
            skip_in, (0, (1 - tp_index) * HEAD, 0), (SPAN, HEAD, width)
        )
    )
    down_other = swap_tp(tie(feed_own[side:], skip_in))
    lse_spec = pl.BlockSpec((head_rows, BLOCK), lambda p, *_: (0, p))
    values, attended, log_total, middle, norm_two = call(
        attend_kernel,
        1,
        (SPAN,),
        [
            placed(width), in_rows(width), full(flat),
            pl.BlockSpec((2, BLOCK, fresh), lambda p, *_: (0, p, 0)),
            pl.BlockSpec(
                (None, HEAD, width),
                lambda p, ids: (member_at(p, ids), ids[TP], 0),
            ),
            placed(width, HEAD),
            full((half, width)), full((half, width)), full((width,)), full((width,)),
            full((width,)),
        ],
        [full(flat), placed(width), lse_spec, placed(width), placed(width)],
        [
            shape_of(flat, BF16), shape_of(own_shape, BF16), shape_of((head_rows, tokens), F32),
            shape_of(own_shape, BF16), shape_of(own_shape, BF16),
        ],
        scratch=[pltpu.VMEM((BLOCK, width), BF16), pltpu.VMEM((BLOCK, 128), F32)],
        micros=27,
        name="attend",
    )(
        ids, blocks_in, queries, keys, fresh_values, skip_in, skip_other, out_weight,
        out_other,        out_bias, gain_feed, shift_feed,
    )
    rows_mine = norm_two.reshape(flat)
    grads_mine = grad_blocks.reshape(flat)

    rows_theirs = swap_core(rows_mine)
    grads_theirs = swap_core(grads_mine)
    feed_other = (up_near, up_far, down_other)
    bias_here = row(up_bias_half)
    bias_there = row(bias_other[half + fresh:])
    out_mine, back_mine, bias_one, made_other = feed(
        ids, rows_mine, grads_mine, feed_other, bias_there
    )
    rows_theirs = tie(rows_theirs, out_mine)
    out_theirs, back_theirs, bias_two, *made_other = feed(
        ids, rows_theirs, grads_theirs, feed_other, bias_there, (), (made_other,), PARTS, True
    )
    cross_one = swap_tp(made_other[0])
    given = swap_seq(made_other[3], SPAN)
    out_theirs, back_theirs, bias_three, made_own = feed(
        ids, rows_theirs, grads_theirs, (feed_own,), tie(bias_here, made_other[0]),
        (out_theirs, back_theirs),
    )
    out_given = swap_core(out_theirs)
    back_given = swap_core(back_theirs)
    cross_two = swap_tp(made_other[1])
    given, kept = lax.optimization_barrier((given, made_other[2], out_theirs))[:2]
    pair_sum, = fold(ids, [[(kept, None), (given, None)]], [lambda ids: 0], kept.shape[0])
    out_mine, back_mine, bias_four, *made_own = feed(
        ids, rows_mine, grads_mine, (feed_own,), tie(bias_here, cross_one, pair_sum),
        (out_mine, back_mine), (made_own,), PARTS,
    )
    cross_three = swap_tp(pair_sum)

    def scatter(value):
        parts = value.reshape(others, value.shape[0] // others, width)
        return lax.all_to_all(parts, "seq", 0, 0, tiled=True, axis_index_groups=same_core)

    def gather(parts):
        spread = spread_sum(ids, parts)
        whole = lax.all_to_all(spread, "seq", 0, 0, tiled=True, axis_index_groups=same_core)
        return whole.reshape(-1, width)

    layer_blocks, middle_grad, att_grad, out_keep, out_send, small_two = call(
        residual_kernel,
        1,
        (SPAN,),
        [in_rows(width)] * 5
        + [
            by_block(width), by_block(width), full((half, width)), full((half, width)),
            full((width,)), full((width,)),
        ],
        [
            by_block(width), by_block(width), by_block(width),
            full((2, half // 2, width)), full((2, half // 2, width)), full((4, width)),
        ],
        [
            shape_of(own_shape, BF16), shape_of(own_shape, BF16), shape_of(own_shape, BF16),
            shape_of((2, half // 2, width), BF16), shape_of((2, half // 2, width), BF16),
            shape_of((4, width), F32),
        ],
        scratch=[pltpu.VMEM((width, width), F32)],
        micros=12.5,
        name="residual",
    )(
        ids, tie(out_mine, cross_two), out_given, back_mine, back_given, grads_mine, middle, attended, out_weight,
        out_other, gain_feed, down_bias,
    )
    sent_given = swap_core(out_send)
    out_total = (out_keep.astype(F32) + sent_given.astype(F32)).astype(BF16)
    cross_three = tie(cross_three, att_grad)
    ready_feed, = fold(
        ids,
        [
            [(made_own[0], None), (cross_one, None)],
            [(made_own[1], None), (cross_two, None)],
            [(made_own[2], None), (cross_three, "0")],
            [(made_own[3], None), (cross_three, "1")],
        ],
        [lambda ids: 0],
        2 * side,
    )
    total_feed = lax.psum(ready_feed, "seq", axis_index_groups=same_core)
    def rest():
        cross_out = swap_tp(out_total[1])

        def attend_back(which, query_rows):
            return call(
                partial(attend_back_kernel, which * (heads // 2)),
                1,
                (SPAN,),
                [
                    pl.BlockSpec((BLOCK, half), lambda p, *_: (p, which)),
                    pl.BlockSpec((tokens, half), lambda p, *_: (0, which)),
                    pl.BlockSpec((tokens, half), lambda p, *_: (0, which)),
                    placed(half, column=which), placed(half, column=which), lse_spec,
                ],
                [full((SPAN, BLOCK, packed)), full((SPAN, HEAD, width))],
                [shape_of((SPAN, BLOCK, packed), BF16), shape_of((SPAN, HEAD, width), BF16)],
                scratch=[
                    pltpu.VMEM((BLOCK, half), BF16), pltpu.VMEM((tokens, half), F32),
                    pltpu.VMEM((tokens, half), F32), pltpu.VMEM((8, BLOCK), F32),
                ],
                micros=17.5,
                name="attend_back",
            )(
                ids, query_rows, keys, values, attended, att_grad,
                log_total,
            )

        qkv_rows = packed // 2
        last_rows = -(-(qkv_rows + half // 2) // 64) * 64

        def weights(made):
            return call(
                weight_kernel,
                1,
                (1,),
                [full(flat), full((tokens, packed))],
                [full((qkv_rows, width)), full((qkv_rows, width)), full((1, packed))],
                [
                    shape_of((qkv_rows, width), BF16), shape_of((qkv_rows, width), BF16),
                    shape_of((1, packed), F32),
                ],
                scratch=[pltpu.VMEM((packed, width), F32)],
                micros=6,
                name="weights",
            )(ids, norm_one.reshape(flat), made.reshape(tokens, packed))

        layer_out = to_seqs(layer_blocks).reshape(flat)
        grads_other, skip_made = attend_back(1, queries)
        keep_other, send_other, sums_other = weights(tie(grads_other, cross_out))
        given_other = swap_core(send_other)
        total_other, = fold(
            ids, [[(keep_other, None), (given_other, None)]], [lambda ids: 0], qkv_rows
        )
        cross_other = swap_tp(total_other)
        grads_own, skip_own = attend_back(0, tie(queries, total_other, layer_out))
        skip_theirs = swap_tp(tie(skip_made, grads_own))
        keep_own, send_own, sums_own = weights(tie(grads_own, cross_other))
        given_own = swap_core(send_own)

        ready_qkv, = fold(
            ids,
            [
                [(keep_own, None), (given_own, None), (cross_other, None)],
                [(out_total, 0), (cross_out, None)],
            ],
            [lambda ids: 0],
            last_rows,
            last_rows,
        )
        parts_qkv = scatter(ready_qkv)
        def by_distance(columns, rows=BLOCK):
            return pl.BlockSpec((None, rows, columns), lambda p, ids: (ids[MINE] ^ p, 0, 0))

        *input_blocks, small_one = call(
            input_kernel,
            1,
            (SPAN,),
            [
                by_distance(packed), by_distance(packed), full((packed, width)),
                full((packed, width)), by_distance(width), by_distance(width),
                by_distance(width, HEAD), by_distance(width, HEAD), full((width,)),
            ],
            [full((BLOCK + 2 * HEAD, width))] * SPAN + [full((2, width))],
            [shape_of((BLOCK + 2 * HEAD, width), BF16)] * SPAN + [shape_of((2, width), F32)],
            micros=9,
            name="input",
        )(
            ids, tie(grads_own, ready_qkv), grads_other, qkv_own, qkv_other, blocks_in, middle_grad,
            skip_own, skip_theirs, gain_attention,
        )
        back = [input_blocks[0]] + [
            swap_seq(input_blocks[distance], distance) for distance in range(1, SPAN)
        ]
        shared = jnp.concatenate([small_one.reshape(-1), small_two.reshape(-1)])
        widened = lambda value: jnp.where(
            lax.broadcasted_iota(jnp.int32, (2, 1), 0) == core, value, 0.0
        ).reshape(-1)
        split_own = jnp.concatenate([sums_own.reshape(-1), widened(bias_three + bias_four)])
        split_other = jnp.concatenate([sums_other.reshape(-1), widened(bias_one + bias_two)])
        vector_own = jnp.concatenate([shared, split_own])
        vector_other = jnp.concatenate([shared, split_other])

        vectors = vector_own + swap_tp(vector_other)
        for distance in [1] + [SPAN << bit for bit in range((seq_count // SPAN).bit_length() - 1)]:
            vectors = vectors + swap_seq(vectors, distance)
        parts_qkv, *back = lax.optimization_barrier((parts_qkv, vectors, *back))
        vectors = back.pop(0)
        return (layer_out, parts_qkv, vectors, *back)

    shapes = jax.eval_shape(rest)
    results = lax.cond(
        jnp.min(lengths) > 0, rest, lambda: tuple(jnp.zeros(s.shape, s.dtype) for s in shapes)
    )
    layer_out, parts_qkv, vectors, *back = results
    late = ids + (vectors[0] * 0.0).astype(jnp.int32)
    whole_qkv = gather(parts_qkv)
    total_feed = tie(total_feed, late)
    far_feed = swap_core(total_feed)
    input_grad, skip_grad = collect(ids, back)
    input_grad, skip_grad = input_grad.reshape(flat), skip_grad.T
    vectors = vectors + swap_seq(vectors, 2)
    grad_up_weight, grad_down_weight = place_feed(late, total_feed, far_feed)
    whole_qkv, vectors = lax.optimization_barrier(
        (whole_qkv, vectors, grad_up_weight, input_grad, skip_grad)
    )[:2]
    grad_query, grad_key, grad_value, grad_out_weight = place_qkv(
        ids, whole_qkv, swap_core(whole_qkv), half, fresh
    )
    shared = vectors[:6 * width].reshape(6, width)
    split = vectors[6 * width:]

    return (
        layer_out,
        input_grad,
        skip_grad,
        shared[0],
        shared[1],
        grad_query,
        split[:half],
        grad_key,
        grad_value.T,
        split[2 * half:packed],
        grad_out_weight,
        shared[4],
        shared[2],
        shared[3],
        grad_up_weight,
        split[packed:],
        grad_down_weight,
        shared[5],
    )


def solution(mesh):
    return jax.shard_map(
        partial(per_device, (mesh.shape["seq"], mesh.shape["tp"])),
        mesh=mesh,
        in_specs=(
            P(("seq", "tp"), None),
            P("seq", "tp"),
            P(),
            P(),
            P(),
            P(),
            P(None, "tp"),
            P("tp"),
            P(None, "tp"),
            P(None, "tp"),
            P("tp"),
            P("tp", None),
            P(),
            P(),
            P(),
            P(None, "tp"),
            P("tp"),
            P("tp", None),
            P(),
            P(("seq", "tp"), None),
        ),
        out_specs=(
            P(("seq", "tp"), None),
            P(("seq", "tp"), None),
            P("seq", "tp"),
            P(),
            P(),
            P(None, "tp"),
            P("tp"),
            P(None, "tp"),
            P(None, "tp"),
            P("tp"),
            P("tp", None),
            P(),
            P(),
            P(),
            P(None, "tp"),
            P("tp"),
            P("tp", None),
            P(),
        ),
        check_vma=False,
    )
```
